32 devices in a mesh: section: 2 (over core), dp: 4 (over y, x), seq: 4 (over z).
Axes of the slice: x: 2, y: 2, z: 4, core: 2. Of those that a mesh axis runs over, the one named last changes fastest.
Arguments:
- inputs: bfloat16 [2, 4, 1024, 1024], P(None, 'dp', 'seq'), may hold values from -16 to 16
- doc_lengths: int32 [2, 4, 4], P(None, 'dp'), may hold values from 1 to 512, 1024 in all within a row
- out_grad: bfloat16 [2, 4, 1024, 1024], P(None, 'dp', 'seq'), may hold values from -6 to 6
- norm_gain: bfloat16 [2, 1024], P('section', ('dp', 'seq')), may hold values from 0.5 to 1.5
- in_weight: bfloat16 [2, 1024, 4096], P('section', ('dp', 'seq')), may hold values from -0.1875 to 0.1875
- conv_weight: bfloat16 [2, 4, 2048], P('section', None, ('dp', 'seq')), may hold values from -3 to 3
- conv_bias: bfloat16 [2, 2048], P('section', ('dp', 'seq')), may hold values from -0.5 to 0.5
- select_weight: bfloat16 [2, 2048, 96], P('section', ('dp', 'seq')), may hold values from -0.125 to 0.125
- step_weight: bfloat16 [2, 64, 2048], P('section', None, ('dp', 'seq')), may hold values from -0.75 to 0.75
- step_bias: bfloat16 [2, 2048], P('section', ('dp', 'seq')), may hold values from -6.875 to -2.296875
- log_decay: bfloat16 [2, 16, 2048], P('section', None, ('dp', 'seq')), may hold values from -4 to 2
- skip_gain: bfloat16 [2, 2048], P('section', ('dp', 'seq')), may hold values from 0.5 to 1.5
- out_weight: bfloat16 [2, 2048, 1024], P('section', ('dp', 'seq')), may hold values from -0.25 to 0.25
Outputs:
- layer_out: float32 [2, 2, 4, 1024, 1024], P('section', None, 'dp', 'seq')
- layer_in_grad: float32 [2, 2, 4, 1024, 1024], P('section', None, 'dp', 'seq')
- grad_norm_gain: float32 [2, 1024], P('section', ('dp', 'seq'))
- grad_in_weight: float32 [2, 1024, 4096], P('section', ('dp', 'seq'))
- grad_conv_weight: float32 [2, 4, 2048], P('section', None, ('dp', 'seq'))
- grad_conv_bias: float32 [2, 2048], P('section', ('dp', 'seq'))
- grad_select_weight: float32 [2, 2048, 96], P('section', ('dp', 'seq'))
- grad_step_weight: float32 [2, 64, 2048], P('section', None, ('dp', 'seq'))
- grad_step_bias: float32 [2, 2048], P('section', ('dp', 'seq'))
- grad_log_decay: float32 [2, 16, 2048], P('section', None, ('dp', 'seq'))
- grad_skip_gain: float32 [2, 2048], P('section', ('dp', 'seq'))
- grad_out_weight: float32 [2, 2048, 1024], P('section', ('dp', 'seq'))
- step_moments: float32 [2, 2, 2048], P('section', None, ('dp', 'seq'))
The draws below stay inside these ranges and needn't reach their ends.
Inputs may be any that keep to these rules, and one draw needn't show every extreme that they name: `doc_lengths`: each row's 4 document lengths sum to 1024; the longest is exactly 512.
All inputs are finite; a program needn't handle non-finite values.
Results may differ from the reference program's by a relative error of at most 0.013.
Values may be sent and summed in bfloat16 or wider, within the bound.
A program may use at most 768 MiB of HBM per device.

```python
import math
from functools import partial
import jax
import jax.numpy as jnp
import numpy as np
from jax import lax

D = 1024
DI = 2048
NST = 16
RANK = 64
KW = 4
MB = 2
NDOC = 4
LEN = 1024
ROWS = 4
XW = 96


def draw_inputs(key, part):
    first_key, second_key = jax.random.split(key, 2)
    base = jax.random.normal(first_key, (MB, ROWS, LEN, D), jnp.float32)
    leading = jax.random.normal(second_key, (D,), jnp.float32)
    ramp = 2.0 * jnp.arange(LEN, dtype=jnp.float32) / LEN
    values = base + ramp[:, None] * leading[None, :]
    return jnp.clip(values, -16.0, 16.0).astype(jnp.bfloat16)


def steps_of(rng, shape, cuts, low, largest):
    factor_of = 1.0
    for position, shards_of in cuts:
        steps = jax.random.uniform(jax.random.fold_in(jax.random.fold_in(rng, 6), position), (shards_of,), jnp.float32, low / len(cuts), largest / len(cuts))
        factor_of = factor_of * jnp.repeat(jnp.exp(steps), shape[position] // shards_of).reshape((-1,) + (1,) * (len(shape) - 1 - position))
    return factor_of


def split_up(count, total, limit, lean):
    loads = [(1 << 20) // math.isqrt(standing ** lean) + 1 for standing in range(2, count + 1)]
    spare, holding = total - limit - (count - 1), [1] * (count - 1)
    while spare > 0:
        movable = [i for i in range(count - 1) if holding[i] < limit]
        pool, remaining = sum([loads[i] for i in movable]), spare
        for i in movable:
            addition = min(limit - holding[i], max(1, remaining * loads[i] // pool), spare)
            holding[i] = holding[i] + addition
            spare = spare - addition
    return np.array([limit] + holding)


def uneven(own_key, amount, total, most, lean):
    if amount == 2:
        one = jax.random.randint(own_key, (), max(1, total - most), min(most, total - 1) + 1)
        return jnp.stack([one, total - one])
    sizes = jnp.asarray(split_up(amount, total, most, lean), jnp.int32)
    twos = (amount - 1) // 2
    donor, sink = sizes[1:1 + 2 * twos:2], sizes[2:2 + 2 * twos:2]
    margin = jnp.minimum(donor - 1, most - sink)
    passed = jax.random.randint(jax.random.fold_in(own_key, 1), (twos,), 0, 1 << 20) % (margin + 1)
    sizes = sizes.at[1:1 + 2 * twos:2].set(donor - passed).at[2:2 + 2 * twos:2].set(sink + passed)
    return sizes[jax.random.permutation(jax.random.fold_in(own_key, 2), amount)]


def gaussian(rng, shape, scale, bound, cuts=(), held_as=jnp.bfloat16):
    values = scale * jax.random.normal(rng, shape, jnp.float32)
    if cuts:
        values = values * steps_of(rng, shape, cuts, -0.22, 0.18)
    return jnp.clip(values, -bound, bound).astype(held_as)


def setup_inputs(seed: int = 0) -> dict:
    seeds = jax.random.split(jax.random.key(seed), 14)
    inputs = draw_inputs(jax.random.fold_in(seeds[13], 71), 0)
    doc_lengths = jax.vmap(lambda own: uneven(own, NDOC, LEN, LEN // 2, 2))(jax.random.split(seeds[1], MB * ROWS)).reshape((MB, ROWS, NDOC)).astype(jnp.int32)
    out_grad = gaussian(seeds[2], (MB, ROWS, LEN, D), 1.0, 6.0, ((1, 4), (2, 4)))
    norm_gain = jnp.clip(1.0 + 0.1 * jax.random.normal(seeds[3], (2, D), jnp.float32), 0.5, 1.5).astype(jnp.bfloat16)
    in_weight = gaussian(seeds[4], (2, D, 2 * DI), D ** -0.5, 0.1875, ((0, 2), (1, 16)))
    conv_weight = gaussian(seeds[5], (2, KW, DI), KW ** -0.5, 3.0, ((0, 2), (2, 16)))
    conv_bias = jnp.clip(jax.random.uniform(seeds[6], (2, DI), jnp.float32, -0.5, 0.5) * steps_of(seeds[6], (2, DI), ((0, 2), (1, 16)), -0.4, 0.0), -0.5, 0.5).astype(jnp.bfloat16)
    select_weight = gaussian(seeds[7], (2, DI, XW), DI ** -0.5, 0.125, ((0, 2), (1, 16)))
    step_weight = gaussian(seeds[8], (2, RANK, DI), RANK ** -0.5, 0.75, ((0, 2), (2, 16)))
    step_bias = jnp.clip(-6.875 + 4.578125 * jax.random.uniform(seeds[9], (2, DI), jnp.float32) ** steps_of(seeds[9], (2, DI), ((0, 2), (1, 16)), -0.2, 0.2), -6.875, -2.296875).astype(jnp.bfloat16)
    log_decay = jnp.clip(-4.0 + 6.0 * jax.random.uniform(seeds[10], (2, NST, DI), jnp.float32) ** steps_of(seeds[10], (2, NST, DI), ((0, 2), (2, 16)), -0.2, 0.2), -4.0, 2.0).astype(jnp.bfloat16)
    skip_gain = jnp.clip(0.5 + 1.0 * jax.random.uniform(seeds[11], (2, DI), jnp.float32) ** steps_of(seeds[11], (2, DI), ((0, 2), (1, 16)), -0.2, 0.2), 0.5, 1.5).astype(jnp.bfloat16)
    out_weight = gaussian(seeds[12], (2, DI, D), (DI // 4) ** -0.5, 0.25, ((0, 2), (1, 16)))
    return dict(inputs=inputs, doc_lengths=doc_lengths, out_grad=out_grad, norm_gain=norm_gain, in_weight=in_weight, conv_weight=conv_weight, conv_bias=conv_bias, select_weight=select_weight, step_weight=step_weight, step_bias=step_bias, log_decay=log_decay, skip_gain=skip_gain, out_weight=out_weight)


eps = 1e-05

@jax.custom_vjp
def low(v):
    return lax.optimization_barrier(v.astype(jnp.bfloat16)).astype(jnp.float32)

@jax.custom_vjp
def low_back(v):
    return v

def low_keep(v):
    return (low(v), None)

def low_pass(kept, grad):
    return (grad,)

def back_keep(v):
    return (v, None)

def back_low(kept, grad):
    return (low(grad),)
low.defvjp(low_keep, low_pass)
low_back.defvjp(back_keep, back_low)

def chain_join(earlier, later):
    return (earlier[0] * later[0], later[0] * earlier[1] + later[1])

def doc_layout(lengths, count):
    starts = jnp.cumsum(lengths, axis=-1) - lengths
    places = jnp.arange(count, dtype=jnp.int32)
    before = (starts[:, None, :] <= places[None, :, None]).astype(jnp.int32)
    segment = lax.optimization_barrier(jnp.sum(before, axis=-1)) - 1
    resets = lax.optimization_barrier(jnp.sum((starts[:, None, :] == places[None, :, None]).astype(jnp.float32), axis=-1))
    return (segment, resets)

def row_scan(decay_rate, block_len, pieces):
    step_size, resets, act_rows, input_map, output_map = pieces
    seq_len, inner_width = step_size.shape
    count = seq_len // block_len

    def advance(carried, blocks):
        step_blk, reset_blk, act_blk, in_blk, out_blk = blocks
        keep_rate = jnp.exp(decay_rate[None] * step_blk[:, None, :]) * (1.0 - reset_blk)[:, None, None]
        add_term = (step_blk * act_blk)[:, None, :] * in_blk[:, :, None]
        add_term = jnp.concatenate([add_term[:1] + keep_rate[:1] * carried[None], add_term[1:]], axis=0)
        unused, states = lax.associative_scan(chain_join, (keep_rate, add_term), axis=0)
        scan_out = jnp.einsum('tnd,tn->td', states, out_blk, precision=lax.Precision.HIGHEST)
        return (states[-1], scan_out)
    blocks = tuple((value.reshape((count, block_len) + value.shape[1:]) for value in (step_size, resets, act_rows, input_map, output_map)))
    unused, outputs = lax.scan(jax.checkpoint(advance), jnp.zeros(decay_rate.shape, jnp.float32), blocks)
    return outputs.reshape(seq_len, inner_width)

def mixer_layer(params, xin, segment, resets):
    norm_gain, in_weight, conv_weight, conv_bias, select_weight, step_weight, step_bias, log_decay, skip_gain, out_weight = params
    row_count, seq_len, model_width = xin.shape
    reach_back = conv_weight.shape[0] - 1
    inner_width = conv_weight.shape[1]
    low_rank = step_weight.shape[0]
    nstate = log_decay.shape[0]
    highest = lax.Precision.HIGHEST
    normal_scale = lax.rsqrt(lax.optimization_barrier(jnp.mean(xin * xin, axis=-1, keepdims=True)) + eps)
    normed = low(xin * normal_scale * norm_gain)
    mixed_proj = low(low_back(jnp.dot(normed.reshape(-1, model_width), in_weight, precision=highest)))
    conv_in = mixed_proj[:, :inner_width].reshape(row_count, seq_len, inner_width)
    gate_in = mixed_proj[:, inner_width:]
    padded = jnp.pad(conv_in, ((0, 0), (reach_back, 0), (0, 0)))
    seg_pad = jnp.pad(segment, ((0, 0), (reach_back, 0)), constant_values=-1)
    pre_conv = conv_bias + sum((conv_weight[offset] * padded[:, offset:offset + seq_len] * (seg_pad[:, offset:offset + seq_len] == segment).astype(jnp.float32)[..., None] for offset in range(reach_back + 1)))
    act_rows = low(jax.nn.silu(pre_conv))
    selected = low_back(jnp.dot(act_rows.reshape(-1, inner_width), select_weight, precision=highest))
    step_low = low(selected[:, :low_rank])
    input_map = selected[:, low_rank:low_rank + nstate].reshape(row_count, seq_len, nstate)
    output_map = selected[:, low_rank + nstate:].reshape(row_count, seq_len, nstate)
    step_pre = low_back(jnp.dot(step_low, step_weight, precision=highest)) + step_bias
    step_size = jax.nn.softplus(step_pre)
    decay_rate = -jnp.exp(log_decay)
    block_len = math.gcd(seq_len, 128)
    scanned = lax.map(partial(row_scan, decay_rate, block_len), (step_size.reshape(row_count, seq_len, inner_width), resets, act_rows, input_map, output_map))
    full_out = scanned + skip_gain * act_rows
    gated_out = low(full_out.reshape(-1, inner_width) * jax.nn.silu(gate_in))
    branch = low_back(jnp.dot(gated_out, out_weight, precision=highest))
    result = xin + branch.reshape(xin.shape)
    moments = jnp.stack([lax.optimization_barrier(jnp.sum(step_size, axis=0)), lax.optimization_barrier(jnp.sum(step_size * step_size, axis=0))]) / (row_count * seq_len)
    return (result, moments)

def apply_layer(segment, resets, xin, *params):
    return mixer_layer(params, xin, segment, resets)

def reference(inputs, doc_lengths, out_grad, norm_gain, in_weight, conv_weight, conv_bias, select_weight, step_weight, step_bias, log_decay, skip_gain, out_weight):
    xin = inputs.astype(jnp.float32).reshape(-1, LEN, D)
    segment, resets = doc_layout(doc_lengths.reshape(-1, NDOC), LEN)
    weights = (norm_gain, in_weight, conv_weight, conv_bias, select_weight, step_weight, step_bias, log_decay, skip_gain, out_weight)
    first_params = tuple((weight[0].astype(jnp.float32) for weight in weights))
    second_params = tuple((weight[1].astype(jnp.float32) for weight in weights))
    runner = partial(apply_layer, segment, resets)
    hidden, back_first, first_moments = jax.vjp(runner, xin, *first_params, has_aux=True)
    final, back_second, second_moments = jax.vjp(runner, hidden, *second_params, has_aux=True)
    second_grads = back_second(out_grad.astype(jnp.float32).reshape(final.shape))
    first_grads = back_first(second_grads[0])
    full_shape = (MB, ROWS, LEN, D)
    layer_out = jnp.stack([hidden.reshape(full_shape), final.reshape(full_shape)])
    layer_in_grad = jnp.stack([first_grads[0].reshape(full_shape), second_grads[0].reshape(full_shape)])
    grads = [jnp.stack([first_grads[index + 1], second_grads[index + 1]]) for index in range(10)]
    step_moments = jnp.stack([first_moments, second_moments])
    return (layer_out, layer_in_grad, grads[0], grads[1], grads[2], grads[3], grads[4], grads[5], grads[6], grads[7], grads[8], grads[9], step_moments)
```

```python
import functools
import math

import jax
import jax.numpy as jnp
from jax import lax
from jax.experimental import pallas as pl
from jax.experimental.pallas import tpu as pltpu
from jax.sharding import PartitionSpec as P

EPS = 1e-05
LOG2E = math.log2(math.e)
LN2 = math.log(2.0)
CUT = 1e30
LANES = 128
CHUNKS = 8
VMEM_LIMIT = 60 * 1024 * 1024
F32 = jnp.float32
BF16 = jnp.bfloat16
HIGHEST = lax.Precision.HIGHEST


def silu_slope(values):
    sigma = jax.nn.sigmoid(values)
    return sigma * (1.0 + values * (1.0 - sigma))


def interleave(rows):
    count = rows.shape[0]
    return rows.reshape(CHUNKS, count // CHUNKS, -1).swapaxes(0, 1).reshape(count, -1)


def in_order(rows):
    count = rows.shape[0]
    return rows.reshape(count // CHUNKS, CHUNKS, -1).swapaxes(0, 1).reshape(count, -1)


def column_params(**kw):
    return pltpu.CompilerParams(
        dimension_semantics=("arbitrary",), vmem_limit_bytes=VMEM_LIMIT, **kw
    )


def cols(rows, width=LANES):
    return pl.BlockSpec((rows, width), lambda j: (0, j))


def whole(*shape):
    return pl.BlockSpec(shape, lambda j: (0,) * len(shape))


def conv_taps(conv_ref, halo_ref, steps, reach):
    width = conv_ref.shape[1]
    own = conv_ref[...].astype(F32).reshape(steps, CHUNKS, width)
    tail = own[steps - reach :]
    moved = pltpu.roll(tail.reshape(reach * CHUNKS, width), 1, 0).reshape(reach, CHUNKS, width)
    first = lax.broadcasted_iota(jnp.int32, moved.shape, 1) == 0
    halo = halo_ref[...].astype(F32)[:, None, :]
    head = jnp.where(first, jnp.broadcast_to(halo, moved.shape), moved)
    return jnp.concatenate([head, own], axis=0)


def select_kernel(conv_ref, halo_ref, same_ref, small_ref, sel_ref, act_ref, pre_ref, out_ref, acc):
    j = pl.program_id(0)
    count, width = conv_ref.shape
    reach = halo_ref.shape[0]
    steps = count // CHUNKS
    ext = conv_taps(conv_ref, halo_ref, steps, reach)
    pre = jnp.broadcast_to(small_ref[reach + 1 : reach + 2, :], (count, width)).reshape(
        steps, CHUNKS, width
    )
    for k in range(reach + 1):
        weight = small_ref[k : k + 1, :]
        same = same_ref[k][:, :, None]
        pre = pre + (weight[None] * ext[k : k + steps]) * same
    pre = pre.reshape(count, width)
    pre_ref[...] = pre
    act = (pre * jax.nn.sigmoid(pre)).astype(BF16)
    act_ref[...] = act

    @pl.when(j == 0)
    def _():
        acc[...] = jnp.zeros_like(acc)

    acc[...] += lax.dot_general(
        act, sel_ref[...], (((1,), (1,)), ((), ())), preferred_element_type=F32
    )
    out_ref[...] = acc[...]


def select_call(conv_in, halo, same, small, sel):
    count, inner = conv_in.shape
    width = min(512, inner)
    wide = sel.shape[0]
    return pl.pallas_call(
        select_kernel,
        grid=(inner // width,),
        in_specs=[
            cols(count, width),
            cols(halo.shape[0], width),
            whole(*same.shape),
            cols(small.shape[0], width),
            cols(wide, width),
        ],
        out_specs=[cols(count, width), cols(count, width), whole(count, wide)],
        out_shape=[
            jax.ShapeDtypeStruct((count, inner), BF16),
            jax.ShapeDtypeStruct((count, inner), F32),
            jax.ShapeDtypeStruct((count, wide), F32),
        ],
        scratch_shapes=[pltpu.VMEM((count, wide), F32)],
        compiler_params=column_params(),
        name="conv_select",
    )(conv_in, halo, same, small, sel)


def spread(dst, src_ref, nstate):
    for n in range(nstate):
        dst[n] = jnp.broadcast_to(src_ref[:, n : n + 1], dst.shape[1:])


def chunk_links(ends, sums, rates, backward):
    row = lax.broadcasted_iota(jnp.int32, (CHUNKS, LANES), 0)
    gains = [jnp.exp2(sums * rate) for rate in rates]
    ends = list(ends)
    total = sums
    k = 1
    while k < CHUNKS:
        turn = CHUNKS - k if backward else k
        mask = row < CHUNKS - k if backward else row >= k
        ends = [
            jnp.where(mask, g * pltpu.roll(e, turn, 0) + e, e) for g, e in zip(gains, ends)
        ]
        gains = [jnp.where(mask, g * pltpu.roll(g, turn, 0), g) for g in gains]
        total = jnp.where(mask, pltpu.roll(total, turn, 0) + total, total)
        k *= 2
    turn = CHUNKS - 1 if backward else 1
    mask = row < CHUNKS - 1 if backward else row >= 1
    entering = [jnp.where(mask, pltpu.roll(e, turn, 0), 0.0) for e in ends]
    before = jnp.where(mask, pltpu.roll(total, turn, 0), 0.0)
    last = 0 if backward else CHUNKS - 1
    return entering, [e[last : last + 1] for e in ends], before, total[last : last + 1]


def rate_rows(rate_ref, nstate):
    return [jnp.broadcast_to(rate_ref[n : n + 1, :], (CHUNKS, LANES)) for n in range(nstate)]


def forward_totals_kernel(
    low_ref, stepw_ref, small_ref, act_ref, in_ref, cut_ref, rate_ref,
    step_ref, sig_ref, enter_ref, total_ref, before_ref, sum_ref, moment_ref, inb,
):
    count = act_ref.shape[0]
    nstate = rate_ref.shape[0]

    @pl.when(pl.program_id(0) == 0)
    def _():
        spread(inb, in_ref, nstate)

    pre = jnp.dot(low_ref[...], stepw_ref[...], preferred_element_type=F32) + small_ref[5:6, :]
    near = jnp.exp(-jnp.abs(pre))
    step_all = jnp.maximum(pre, 0.0) + jnp.log1p(near)
    step_ref[...] = step_all
    sig_ref[...] = jnp.where(pre >= 0.0, 1.0, near) / (1.0 + near)
    moment_ref[0:1, :] = jnp.sum(step_all, axis=0, keepdims=True)
    moment_ref[1:2, :] = jnp.sum(step_all * step_all, axis=0, keepdims=True)
    rates = rate_rows(rate_ref, nstate)

    def body(pair, carry):
        states, sums = carry
        act = act_ref[pl.ds(pl.multiple_of(pair * 16, 16), 16), :].astype(F32)
        for half in (0, 1):
            at = pl.ds(pl.multiple_of(pair * 16 + half * 8, 8), 8)
            step = step_ref[at, :]
            away = step + cut_ref[at, :]
            drive = step * act[half * 8 : half * 8 + 8]
            sums = sums + away
            states = tuple(
                jnp.exp2(away * rates[n]) * states[n] + drive * inb[n, at, :]
                for n in range(nstate)
            )
        return states, sums

    zero = jnp.zeros((CHUNKS, LANES), F32)
    ends, sums = lax.fori_loop(0, count // 16, body, ((zero,) * nstate, zero))
    entering, totals, before, total = chunk_links(ends, sums, rates, False)
    for n in range(nstate):
        enter_ref[n] = entering[n]
        total_ref[n : n + 1, :] = totals[n].astype(total_ref.dtype)
    before_ref[...] = before
    sum_ref[...] = total


def forward_totals(low, stepw, small, act, in_map, cut, rate):
    count, inner = act.shape
    nstate = rate.shape[0]
    return pl.pallas_call(
        forward_totals_kernel,
        grid=(inner // LANES,),
        in_specs=[
            whole(*low.shape),
            cols(stepw.shape[0]),
            cols(small.shape[0]),
            cols(count),
            whole(count, nstate),
            whole(count, LANES),
            cols(nstate),
        ],
        out_specs=[
            cols(count),
            cols(count),
            pl.BlockSpec((nstate, CHUNKS, LANES), lambda j: (0, 0, j)),
            cols(nstate),
            cols(CHUNKS),
            cols(1),
            cols(2),
        ],
        out_shape=[
            jax.ShapeDtypeStruct((count, inner), F32),
            jax.ShapeDtypeStruct((count, inner), F32),
            jax.ShapeDtypeStruct((nstate, CHUNKS, inner), F32),
            jax.ShapeDtypeStruct((nstate, inner), BF16),
            jax.ShapeDtypeStruct((CHUNKS, inner), F32),
            jax.ShapeDtypeStruct((1, inner), F32),
            jax.ShapeDtypeStruct((2, inner), F32),
        ],
        scratch_shapes=[pltpu.VMEM((nstate, count, LANES), F32)],
        compiler_params=column_params(),
        name="forward_totals",
    )(low, stepw, small, act, in_map, cut, rate)


def arriving_state(me, totals_ref, sums_ref, rate_ref, backward):
    devices = totals_ref.shape[0]
    state = jnp.zeros(rate_ref.shape, F32)
    order = range(devices - 1, 0, -1) if backward else range(devices - 1)
    for k in order:
        new = jnp.exp2(rate_ref[...] * sums_ref[k]) * state + totals_ref[k].astype(F32)
        state = jnp.where((k > me) if backward else (k < me), new, state)
    return state


def forward_states_kernel(
    me_ref, step_ref, act_ref, gate_ref, in_ref, outm_ref, cut_ref, rate_ref, small_ref,
    enter_ref, before_ref, totals_ref, sums_ref,
    full_ref, gated_ref, keep_ref, inb, outb,
):
    count = act_ref.shape[0]
    nstate = rate_ref.shape[0]

    @pl.when(pl.program_id(0) == 0)
    def _():
        spread(inb, in_ref, nstate)
        spread(outb, outm_ref, nstate)

    rates = rate_rows(rate_ref, nstate)
    arrived = arriving_state(me_ref[0], totals_ref, sums_ref, rate_ref, False)
    before = before_ref[...]
    states = []
    for n in range(nstate):
        state = enter_ref[n] + jnp.exp2(before * rates[n]) * arrived[n : n + 1, :]
        keep_ref[0, n, 0:CHUNKS, :] = state
        states.append(state)
    skip = jnp.broadcast_to(small_ref[6:7, :], (CHUNKS, LANES))

    def body(pair, states):
        rows = pl.ds(pl.multiple_of(pair * 16, 16), 16)
        act = act_ref[rows, :].astype(F32)
        fulls = []
        for half in (0, 1):
            at = pl.ds(pl.multiple_of(pair * 16 + half * 8, 8), 8)
            after = pl.ds(pl.multiple_of(pair * 16 + half * 8 + 8, 8), 8)
            step = step_ref[at, :]
            away = step + cut_ref[at, :]
            act_now = act[half * 8 : half * 8 + 8]
            drive = step * act_now
            out = skip * act_now
            new = []
            for n in range(nstate):
                state = jnp.exp2(away * rates[n]) * states[n] + drive * inb[n, at, :]
                keep_ref[0, n, after, :] = state
                out = out + state * outb[n, at, :]
                new.append(state)
            states = tuple(new)
            fulls.append(out)
        full = jnp.concatenate(fulls, axis=0)
        full_ref[rows, :] = full
        gate = gate_ref[rows, :].astype(F32)
        gated_ref[rows, :] = (full * (gate * jax.nn.sigmoid(gate))).astype(BF16)
        return states

    lax.fori_loop(0, count // 16, body, tuple(states))


def forward_states(me, step, act, mixed, in_map, out_map, cut, rate, small, enter, before, totals, sums):
    count, inner = act.shape
    nstate = rate.shape[0]
    devices = totals.shape[0]
    blocks = inner // LANES
    return pl.pallas_call(
        forward_states_kernel,
        grid=(blocks,),
        in_specs=[
            pl.BlockSpec(memory_space=pltpu.SMEM),
            cols(count),
            cols(count),
            pl.BlockSpec((count, LANES), lambda j: (0, j + blocks)),
            whole(count, nstate),
            whole(count, nstate),
            whole(count, LANES),
            cols(nstate),
            cols(small.shape[0]),
            pl.BlockSpec((nstate, CHUNKS, LANES), lambda j: (0, 0, j)),
            cols(CHUNKS),
            pl.BlockSpec((devices, nstate, LANES), lambda j: (0, 0, j)),
            pl.BlockSpec((devices, 1, LANES), lambda j: (0, 0, j)),
        ],
        out_specs=[
            cols(count),
            cols(count),
            pl.BlockSpec((1, nstate, count + CHUNKS, LANES), lambda j: (j, 0, 0, 0)),
        ],
        out_shape=[
            jax.ShapeDtypeStruct((count, inner), F32),
            jax.ShapeDtypeStruct((count, inner), BF16),
            jax.ShapeDtypeStruct((blocks, nstate, count + CHUNKS, LANES), F32),
        ],
        scratch_shapes=[pltpu.VMEM((nstate, count, LANES), F32)] * 2,
        compiler_params=column_params(),
        name="forward_states",
    )(me, step, act, mixed, in_map, out_map, cut, rate, small, enter, before, totals, sums)


def backward_totals_kernel(
    dgated_ref, gate_ref, full_ref, act_ref, step_ref, outm_ref, cut_ref, rate_ref,
    dfull_ref, dgate_ref, gskip_ref, enter_ref, total_ref, before_ref, sum_ref, outb,
):
    count = act_ref.shape[0]
    nstate = rate_ref.shape[0]
    pairs = count // 16

    @pl.when(pl.program_id(0) == 0)
    def _():
        spread(outb, outm_ref, nstate)

    rates = rate_rows(rate_ref, nstate)

    def body(turn, carry):
        states, sums, gskip = carry
        pair = pairs - 1 - turn
        rows = pl.ds(pl.multiple_of(pair * 16, 16), 16)
        act = act_ref[rows, :].astype(F32)
        gate = gate_ref[rows, :].astype(F32)
        sigma = jax.nn.sigmoid(gate)
        dgated = dgated_ref[rows, :]
        dfull = dgated * (gate * sigma)
        dfull_ref[rows, :] = dfull
        slope = sigma * (1.0 + gate * (1.0 - sigma))
        dgate_ref[rows, :] = (dgated * full_ref[rows, :] * slope).astype(BF16)
        both = dfull * act
        gskip = gskip + both[0:8] + both[8:16]
        for half in (1, 0):
            at = pl.ds(pl.multiple_of(pair * 16 + half * 8, 8), 8)
            away = step_ref[at, :] + cut_ref[at, :]
            grad = dfull[half * 8 : half * 8 + 8]
            sums = sums + away
            states = tuple(
                jnp.exp2(away * rates[n]) * (states[n] + outb[n, at, :] * grad)
                for n in range(nstate)
            )
        return states, sums, gskip

    zero = jnp.zeros((CHUNKS, LANES), F32)
    ends, sums, gskip = lax.fori_loop(0, pairs, body, ((zero,) * nstate, zero, zero))
    gskip_ref[...] = jnp.sum(gskip, axis=0, keepdims=True)
    entering, totals, before, total = chunk_links(ends, sums, rates, True)
    for n in range(nstate):
        enter_ref[n] = entering[n]
        total_ref[n : n + 1, :] = totals[n].astype(total_ref.dtype)
    before_ref[...] = before
    sum_ref[...] = total


def backward_totals(dgated, mixed, full, act, step, out_map, cut, rate):
    count, inner = act.shape
    nstate = rate.shape[0]
    blocks = inner // LANES
    return pl.pallas_call(
        backward_totals_kernel,
        grid=(blocks,),
        in_specs=[
            cols(count),
            pl.BlockSpec((count, LANES), lambda j: (0, j + blocks)),
            cols(count),
            cols(count),
            cols(count),
            whole(count, nstate),
            whole(count, LANES),
            cols(nstate),
        ],
        out_specs=[
            cols(count),
            cols(count),
            cols(1),
            pl.BlockSpec((nstate, CHUNKS, LANES), lambda j: (0, 0, j)),
            cols(nstate),
            cols(CHUNKS),
            cols(1),
        ],
        out_shape=[
            jax.ShapeDtypeStruct((count, inner), F32),
            jax.ShapeDtypeStruct((count, inner), BF16),
            jax.ShapeDtypeStruct((1, inner), F32),
            jax.ShapeDtypeStruct((nstate, CHUNKS, inner), F32),
            jax.ShapeDtypeStruct((nstate, inner), BF16),
            jax.ShapeDtypeStruct((CHUNKS, inner), F32),
            jax.ShapeDtypeStruct((1, inner), F32),
        ],
        scratch_shapes=[pltpu.VMEM((nstate, count, LANES), F32)],
        compiler_params=column_params(),
        name="backward_totals",
    )(dgated, mixed, full, act, step, out_map, cut, rate)


def backward_states_kernel(
    me_ref, step_ref, sig_ref, act_ref, dfull_ref, in_ref, outm_ref, cut_ref, rate_ref, small_ref,
    enter_ref, before_ref, totals_ref, sums_ref, keep_ref, low_ref, stepw_ref,
    dact_ref, gbias_ref, gdecay_ref, gstepw_ref, dsel_ref,
    inb, outb, din_acc, dout_acc, dlow_acc, dstep_buf, dstep_low,
):
    count = act_ref.shape[0]
    nstate = rate_ref.shape[0]
    pairs = count // 16
    j = pl.program_id(0)

    @pl.when(j == 0)
    def _():
        spread(inb, in_ref, nstate)
        spread(outb, outm_ref, nstate)
        din_acc[...] = jnp.zeros_like(din_acc)
        dout_acc[...] = jnp.zeros_like(dout_acc)
        dlow_acc[...] = jnp.zeros_like(dlow_acc)

    rates = rate_rows(rate_ref, nstate)
    arrived = arriving_state(me_ref[0], totals_ref, sums_ref, rate_ref, True)
    before = before_ref[...]
    states = tuple(
        enter_ref[n] + jnp.exp2(before * rates[n]) * arrived[n : n + 1, :] for n in range(nstate)
    )
    skip = jnp.broadcast_to(small_ref[6:7, :], (CHUNKS, LANES))

    def body(turn, carry):
        states, decays = carry
        pair = pairs - 1 - turn
        rows = pl.ds(pl.multiple_of(pair * 16, 16), 16)
        act = act_ref[rows, :].astype(F32)
        for half in (1, 0):
            at = pl.ds(pl.multiple_of(pair * 16 + half * 8, 8), 8)
            after = pl.ds(pl.multiple_of(pair * 16 + half * 8 + 8, 8), 8)
            step = step_ref[at, :]
            away = step + cut_ref[at, :]
            act_now = act[half * 8 : half * 8 + 8]
            drive = step * act_now
            grad = dfull_ref[at, :]
            by_rate = jnp.zeros((CHUNKS, LANES), F32)
            mapped = jnp.zeros((CHUNKS, LANES), F32)
            new, new_decays = [], []
            for n in range(nstate):
                adjoint = states[n] + outb[n, at, :] * grad
                passed = adjoint * jnp.exp2(away * rates[n])
                rho = passed * keep_ref[0, n, at, :]
                by_rate = by_rate + rho * rates[n]
                mapped = mapped + adjoint * inb[n, at, :]
                new_decays.append(decays[n] + rho * step)
                din_acc[n, at, :] += adjoint * drive
                dout_acc[n, at, :] += keep_ref[0, n, after, :] * grad
                new.append(passed)
            states, decays = tuple(new), tuple(new_decays)
            dstep_buf[at, :] = by_rate * LN2 + act_now * mapped
            dact_ref[at, :] = step * mapped + skip * grad
        return states, decays

    zero = jnp.zeros((CHUNKS, LANES), F32)
    states, decays = lax.fori_loop(0, pairs, body, (states, (zero,) * nstate))
    for n in range(nstate):
        gdecay_ref[n : n + 1, :] = (rate_ref[n : n + 1, :] * LN2) * jnp.sum(
            decays[n], axis=0, keepdims=True
        )
    dpre = dstep_buf[...] * sig_ref[...]
    gbias_ref[...] = jnp.sum(dpre, axis=0, keepdims=True)
    dstep_low[...] = dpre.astype(BF16)
    low_dpre = dstep_low[...]
    gstepw_ref[...] = lax.dot_general(
        low_ref[...], low_dpre, (((0,), (0,)), ((), ())), preferred_element_type=F32
    )
    dlow_acc[...] += lax.dot_general(
        low_dpre, stepw_ref[...], (((1,), (1,)), ((), ())), preferred_element_type=F32
    )

    @pl.when(j == pl.num_programs(0) - 1)
    def _():
        column = lax.broadcasted_iota(jnp.int32, (LANES, nstate), 1)
        din = jnp.zeros((count, nstate), F32)
        dout = jnp.zeros((count, nstate), F32)
        for n in range(nstate):
            pick = (column == n).astype(F32)
            din = din + jnp.dot(din_acc[n], pick, precision=HIGHEST, preferred_element_type=F32)
            dout = dout + jnp.dot(dout_acc[n], pick, precision=HIGHEST, preferred_element_type=F32)
        dsel_ref[...] = jnp.concatenate([dlow_acc[...], din, dout], axis=1).astype(BF16)


def backward_states(
    me, step, sig, act, dfull, in_map, out_map, cut, rate, small, enter, before, totals, sums, keep, low, stepw
):
    count, inner = act.shape
    nstate = rate.shape[0]
    devices = totals.shape[0]
    rank = stepw.shape[0]
    wide = rank + 2 * nstate
    blocks = inner // LANES
    return pl.pallas_call(
        backward_states_kernel,
        grid=(blocks,),
        in_specs=[
            pl.BlockSpec(memory_space=pltpu.SMEM),
            cols(count),
            cols(count),
            cols(count),
            cols(count),
            whole(count, nstate),
            whole(count, nstate),
            whole(count, LANES),
            cols(nstate),
            cols(small.shape[0]),
            pl.BlockSpec((nstate, CHUNKS, LANES), lambda j: (0, 0, j)),
            cols(CHUNKS),
            pl.BlockSpec((devices, nstate, LANES), lambda j: (0, 0, j)),
            pl.BlockSpec((devices, 1, LANES), lambda j: (0, 0, j)),
            pl.BlockSpec((1, nstate, count + CHUNKS, LANES), lambda j: (j, 0, 0, 0)),
            whole(count, rank),
            cols(rank),
        ],
        out_specs=[cols(count), cols(1), cols(nstate), cols(rank), whole(count, wide)],
        out_shape=[
            jax.ShapeDtypeStruct((count, inner), F32),
            jax.ShapeDtypeStruct((1, inner), F32),
            jax.ShapeDtypeStruct((nstate, inner), F32),
            jax.ShapeDtypeStruct((rank, inner), F32),
            jax.ShapeDtypeStruct((count, wide), BF16),
        ],
        scratch_shapes=[pltpu.VMEM((nstate, count, LANES), F32)] * 4
        + [
            pltpu.VMEM((count, rank), F32),
            pltpu.VMEM((count, LANES), F32),
            pltpu.VMEM((count, LANES), BF16),
        ],
        compiler_params=column_params(),
        name="backward_states",
    )(me, step, sig, act, dfull, in_map, out_map, cut, rate, small, enter, before, totals, sums, keep, low, stepw)


def conv_grad_kernel(
    conv_ref, halo_ref, same_ref, small_ref, sel_ref, act_ref, pre_ref, dact_ref, dsel_ref,
    dconv_ref, tail_ref, spill_ref, gsel_ref, gsmall_ref,
):
    count, width = conv_ref.shape
    reach = halo_ref.shape[0]
    steps = count // CHUNKS
    ext = conv_taps(conv_ref, halo_ref, steps, reach)
    dsel = dsel_ref[...]
    gsel_ref[...] = lax.dot_general(
        dsel, act_ref[...], (((0,), (0,)), ((), ())), preferred_element_type=F32
    )
    dact = dact_ref[...] + jnp.dot(dsel, sel_ref[...], preferred_element_type=F32)
    dpre = dact * silu_slope(pre_ref[...])
    gsmall_ref[reach + 1 : reach + 2, :] = jnp.sum(dpre, axis=0, keepdims=True)
    dpre = dpre.reshape(steps, CHUNKS, width)
    parts = []
    for k in range(reach + 1):
        masked = dpre * same_ref[k][:, :, None]
        gsmall_ref[k : k + 1, :] = jnp.sum(
            (masked * ext[k : k + steps]).reshape(count, width), axis=0, keepdims=True
        )
        parts.append(masked * small_ref[k : k + 1, :][None])
    own = parts[reach]
    for k in range(reach):
        back = reach - k
        own = own + jnp.concatenate(
            [parts[k][back:], jnp.zeros((back, CHUNKS, width), F32)], axis=0
        )
    heads = []
    for e in range(reach):
        total = parts[0][e]
        for k in range(1, e + 1):
            total = total + parts[k][e - k]
        heads.append(total)
    head = jnp.stack(heads)
    spill_ref[...] = head[:, 0, :]
    row = lax.broadcasted_iota(jnp.int32, head.shape, 1)
    moved = pltpu.roll(head.reshape(reach * CHUNKS, width), reach * CHUNKS - 1, 0)
    moved = jnp.where(row == CHUNKS - 1, 0.0, moved.reshape(head.shape))
    tail = own[steps - reach :] + moved
    tail_ref[...] = tail[:, CHUNKS - 1, :]
    dconv = jnp.concatenate([own[: steps - reach], tail], axis=0)
    dconv_ref[...] = dconv.reshape(count, width).astype(BF16)


def conv_grad(conv_in, halo, same, small, sel, act, pre, dact, dsel):
    count, inner = act.shape
    width = min(512, inner)
    reach = halo.shape[0]
    wide = sel.shape[0]
    return pl.pallas_call(
        conv_grad_kernel,
        grid=(inner // width,),
        in_specs=[
            cols(count, width),
            cols(reach, width),
            whole(*same.shape),
            cols(small.shape[0], width),
            cols(wide, width),
            cols(count, width),
            cols(count, width),
            cols(count, width),
            whole(count, wide),
        ],
        out_specs=[
            cols(count, width),
            cols(reach, width),
            cols(reach, width),
            cols(wide, width),
            cols(8, width),
        ],
        out_shape=[
            jax.ShapeDtypeStruct((count, inner), BF16),
            jax.ShapeDtypeStruct((reach, inner), F32),
            jax.ShapeDtypeStruct((reach, inner), F32),
            jax.ShapeDtypeStruct((wide, inner), F32),
            jax.ShapeDtypeStruct((8, inner), F32),
        ],
        compiler_params=column_params(),
        name="conv_grad",
    )(conv_in, halo, same, small, sel, act, pre, dact, dsel)


def share_kernel(total_ref, sum_ref, totals_ref, sums_ref, send, recv, local):
    count = totals_ref.shape[0]
    me = lax.axis_index("seq")
    barrier = pltpu.get_barrier_semaphore()
    peers = [lax.rem(me + k, count) for k in range(1, count)]
    for peer in peers:
        pl.semaphore_signal(
            barrier, inc=1, device_id={"seq": peer}, device_id_type=pl.DeviceIdType.MESH
        )
    pl.semaphore_wait(barrier, count - 1)
    copies = []
    for k, peer in enumerate(peers):
        for i, (src, dst) in enumerate(((total_ref, totals_ref), (sum_ref, sums_ref))):
            copy = pltpu.make_async_remote_copy(
                src_ref=src,
                dst_ref=dst.at[me],
                send_sem=send.at[i, k],
                recv_sem=recv.at[i, k],
                device_id={"seq": peer},
                device_id_type=pl.DeviceIdType.MESH,
            )
            copy.start()
            copies.append(copy)
    own = [
        pltpu.make_async_copy(total_ref, totals_ref.at[me], local.at[0]),
        pltpu.make_async_copy(sum_ref, sums_ref.at[me], local.at[1]),
    ]
    for copy in own:
        copy.start()
    for copy in own + copies:
        copy.wait()


def share(total, sums, collective):
    count = lax.axis_size("seq")
    vmem = pl.BlockSpec(memory_space=pltpu.VMEM)
    return pl.pallas_call(
        share_kernel,
        in_specs=[vmem, vmem],
        out_specs=[vmem, vmem],
        out_shape=[
            jax.ShapeDtypeStruct((count,) + total.shape, total.dtype),
            jax.ShapeDtypeStruct((count,) + sums.shape, sums.dtype),
        ],
        scratch_shapes=[
            pltpu.SemaphoreType.DMA((2, count - 1)),
            pltpu.SemaphoreType.DMA((2, count - 1)),
            pltpu.SemaphoreType.DMA((2,)),
        ],
        compiler_params=pltpu.CompilerParams(collective_id=collective, has_side_effects=True),
        name="share",
    )(total, sums)


def shifted(value, axis, steps):
    count = lax.axis_size(axis)
    first, last = (max(0, -steps), min(count, count - steps))
    return lax.ppermute(value, axis, [(source, source + steps) for source in range(first, last)])


MESH = pl.DeviceIdType.MESH


def where_am_i():
    c, d, z = lax.axis_index("section"), lax.axis_index("dp"), lax.axis_index("seq")
    y, x = d // 2, d % 2
    flip_x, flip_y = y * 2 + (1 - x), (1 - y) * 2 + x
    return c, y, x, z, flip_x, flip_y


def greet(c, z, flip_x, flip_y, depth):
    barrier = pltpu.get_barrier_semaphore()
    peers = [{"section": 1 - c}, {"dp": flip_x}, {"dp": flip_y}]
    peers += [{"seq": lax.rem(z + o, depth)} for o in range(1, depth)]
    for peer in peers:
        pl.semaphore_signal(barrier, inc=1, device_id=peer, device_id_type=MESH)
    pl.semaphore_wait(barrier, len(peers))


def pipeline(stages, count):
    for turn in range(count + len(stages) - 1):
        for late, stage in reversed(list(enumerate(stages))):
            if 0 <= turn - late < count:
                stage(turn - late)


def gather_kernel(plan, depth, items, *refs):
    srcs, outs = refs[:items], refs[items : 2 * items]
    mine = refs[2 * items : 3 * items]
    send, recv, local = refs[3 * items :]
    c, y, x, z, flip_x, flip_y = where_am_i()
    greet(c, z, flip_x, flip_y, depth)
    near = (1 - c) * flip_y + c * flip_x
    far = (1 - c) * flip_x + c * flip_y
    near_at = (y + (1 - c) * (1 - 2 * y), x + c * (1 - 2 * x))
    far_at = (y + c * (1 - 2 * y), x + (1 - c) * (1 - 2 * x))
    both_at = (1 - y, 1 - x)
    pending = []

    def remote(k, slot, src, dst, peer):
        return pltpu.make_async_remote_copy(
            src_ref=src, dst_ref=dst, send_sem=send.at[k, slot], recv_sem=recv.at[k, slot],
            device_id=peer, device_id_type=MESH,
        )

    def start(copy):
        copy.start()
        pending.append(copy)

    def piece(k, at):
        item, _, cols = plan[k]
        return outs[item].at[at[0], at[1], :, c, :, cols]

    def first(k):
        item, layer, cols = plan[k]
        half = mine[item].shape[1]
        slot = plan[k][2].start // plan[k][2].size
        hand = remote(
            k, 0, srcs[item].at[pl.ds((1 - layer) * half, half), cols], mine[item].at[slot],
            {"section": 1 - c},
        )
        keep = pltpu.make_async_copy(
            srcs[item].at[pl.ds(layer * half, half), cols], mine[item].at[slot], local.at[k, 0]
        )

        @pl.when(c == layer)
        def _():
            hand.start()
            keep.start()

    def along_z(k):
        item, layer, cols = plan[k]
        half = mine[item].shape[1]
        slot = plan[k][2].start // plan[k][2].size
        block = mine[item].at[slot]
        hand = remote(
            k, 0, srcs[item].at[pl.ds((1 - layer) * half, half), cols], block, {"section": 1 - c}
        )
        keep = pltpu.make_async_copy(
            srcs[item].at[pl.ds(layer * half, half), cols], block, local.at[k, 0]
        )

        @pl.when(c == layer)
        def _():
            hand.wait_send()
            keep.wait()

        @pl.when(c != layer)
        def _():
            hand.wait_recv()

        for o in range(1, depth):
            start(
                remote(k, o, block, outs[item].at[y, x, z, c, :, cols], {"seq": lax.rem(z + o, depth)})
            )
        pltpu.make_async_copy(block, outs[item].at[y, x, z, c, :, cols], local.at[k, 1]).start()

    def along_near(k):
        item, _, cols = plan[k]
        block = mine[item].at[plan[k][2].start // plan[k][2].size]
        for o in range(1, depth):
            remote(
                k, o, block, outs[item].at[y, x, z, c, :, cols], {"seq": lax.rem(z + o, depth)}
            ).wait_recv()
        pltpu.make_async_copy(block, outs[item].at[y, x, z, c, :, cols], local.at[k, 1]).wait()
        own = piece(k, (y, x))
        start(remote(k, depth, own, own, {"dp": near}))
        start(remote(k, depth + 3, own, own, {"section": 1 - c}))

    def along_far(k):
        own, other = piece(k, (y, x)), piece(k, near_at)
        remote(k, depth, own, own, {"dp": near}).wait_recv()
        start(remote(k, depth + 1, own, own, {"dp": far}))
        start(remote(k, depth + 2, other, other, {"dp": far}))
        start(remote(k, depth + 4, other, other, {"section": 1 - c}))

    def across(k):
        own, other = piece(k, (y, x)), piece(k, near_at)
        remote(k, depth + 1, own, own, {"dp": far}).wait_recv()
        remote(k, depth + 2, other, other, {"dp": far}).wait_recv()
        for slot, at in ((depth + 5, far_at), (depth + 6, both_at)):
            start(remote(k, slot, piece(k, at), piece(k, at), {"section": 1 - c}))

    def finish(k):
        own = piece(k, (y, x))
        for slot in range(depth + 3, depth + 7):
            remote(k, slot, own, own, {"section": 1 - c}).wait_recv()

    for k in range(len(plan)):
        first(k)
    pipeline([along_z, along_near, along_far, across, finish], len(plan))
    for copy in pending:
        copy.wait_send()


def gather_rows(sources, layers, widths, collective):
    depth = lax.axis_size("seq")
    plan = []
    for item, (source, layer, width) in enumerate(zip(sources, layers, widths)):
        for at in range(0, source.shape[1], width):
            plan.append((item, layer, pl.ds(at, width)))
    anywhere = pl.BlockSpec(memory_space=pl.ANY)
    outs = pl.pallas_call(
        functools.partial(gather_kernel, plan, depth, len(sources)),
        in_specs=[anywhere] * len(sources),
        out_specs=[anywhere] * len(sources),
        out_shape=[
            jax.ShapeDtypeStruct((2, 2, depth, 2, s.shape[0] // 2, s.shape[1]), s.dtype)
            for s in sources
        ],
        scratch_shapes=[
            pltpu.VMEM((s.shape[1] // w, s.shape[0] // 2, w), s.dtype)
            for s, w in zip(sources, widths)
        ]
        + [
            pltpu.SemaphoreType.DMA((len(plan), depth + 7)),
            pltpu.SemaphoreType.DMA((len(plan), depth + 7)),
            pltpu.SemaphoreType.DMA((len(plan), 2)),
        ],
        compiler_params=pltpu.CompilerParams(
            collective_id=collective, has_side_effects=True, vmem_limit_bytes=VMEM_LIMIT
        ),
        name="gather_rows",
    )(*sources)
    return [
        out.reshape(4 * depth * s.shape[0], s.shape[1]) for out, s in zip(outs, sources)
    ]


def reduce_kernel(plan, depth, layer, items, olds, *refs):
    srcs, outs = refs[:items], refs[items + olds : 2 * items + olds]
    at = 2 * items + olds
    own, core, side, edge, line, done = (refs[at + i * items : at + (i + 1) * items] for i in range(6))
    send, recv, local = refs[at + 6 * items :]
    c, y, x, z, flip_x, flip_y = where_am_i()
    greet(c, z, flip_x, flip_y, depth)
    near = (1 - c) * flip_x + c * flip_y
    far = (1 - c) * flip_y + c * flip_x
    kept = (1 - c) * y + c * x
    pending = []

    def remote(k, slot, src, dst, peer):
        return pltpu.make_async_remote_copy(
            src_ref=src, dst_ref=dst, send_sem=send.at[k, slot], recv_sem=recv.at[k, slot],
            device_id=peer, device_id_type=MESH,
        )

    def start(copy):
        copy.start()
        pending.append(copy)

    def chunk(k):
        item, slot, cols = plan[k]
        half = own[item].shape[4]
        return item, slot, cols, half

    def cores(k):
        item, slot, cols, half = chunk(k)
        theirs = srcs[item].at[:, :, :, pl.ds((1 - c) * half, half), cols]
        ours = srcs[item].at[:, :, :, pl.ds(c * half, half), cols]
        return (
            remote(k, 0, theirs, core[item].at[slot], {"section": 1 - c}),
            pltpu.make_async_copy(ours, own[item].at[slot], local.at[k, 0]),
        )

    def to_core(k):
        hand, keep = cores(k)
        start(hand)
        keep.start()

    def sides(k):
        item, slot, _, _ = chunk(k)
        return [
            remote(
                k, 1 + u,
                core[item].at[slot, (1 - c) * u + c * (1 - y), (1 - c) * (1 - x) + c * u],
                side[item].at[slot, u], {"dp": near},
            )
            for u in (0, 1)
        ]

    def to_near(k):
        item, slot, _, _ = chunk(k)
        hand, keep = cores(k)
        hand.wait_recv()
        keep.wait()

        def add(i, _):
            a, b, e = i // (2 * depth), (i // depth) % 2, i % depth
            core[item][slot, a, b, e] = core[item][slot, a, b, e] + own[item][slot, a, b, e]
            return 0

        lax.fori_loop(0, 4 * depth, add, 0)
        for copy in sides(k):
            start(copy)

    def edges(k):
        item, slot, _, _ = chunk(k)
        return remote(k, 3, side[item].at[slot, 1 - kept], edge[item].at[slot], {"dp": far})

    def to_far(k):
        item, slot, _, _ = chunk(k)
        for copy in sides(k):
            copy.wait_recv()

        def add(i, _):
            u, e = i // depth, i % depth
            side[item][slot, u, e] = (
                side[item][slot, u, e]
                + core[item][slot, (1 - c) * u + c * y, (1 - c) * x + c * u, e]
            )
            return 0

        lax.fori_loop(0, 2 * depth, add, 0)
        start(edges(k))

    def lines(k):
        item, slot, _, _ = chunk(k)
        copies = []
        for o in range(1, depth):
            peer = lax.rem(z + o, depth)
            copies.append(
                remote(
                    k, 3 + o, edge[item].at[slot, peer], line[item].at[slot, o - 1], {"seq": peer}
                )
            )
        return copies

    def to_line(k):
        item, slot, _, _ = chunk(k)
        edges(k).wait_recv()

        def add(e, _):
            edge[item][slot, e] = edge[item][slot, e] + side[item][slot, kept, e]
            return 0

        lax.fori_loop(0, depth, add, 0)
        for copy in lines(k):
            start(copy)

    def ends(k):
        item, slot, cols, half = chunk(k)
        target = outs[item].at[pl.ds(c * half, half), cols]
        return (
            remote(k, 3 + depth, done[item].at[slot], target, {"section": 1 - c}),
            pltpu.make_async_copy(done[item].at[slot], target, local.at[k, 1]),
        )

    def to_end(k):
        item, slot, _, _ = chunk(k)
        for copy in lines(k):
            copy.wait_recv()
        total = edge[item][slot, z].astype(F32)
        for o in range(depth - 1):
            total = total + line[item][slot, o].astype(F32)
        done[item][slot] = total
        hand, keep = ends(k)

        @pl.when(c == layer)
        def _():
            keep.start()

        @pl.when(c != layer)
        def _():
            hand.start()

    def finish(k):
        hand, keep = ends(k)

        @pl.when(c == layer)
        def _():
            keep.wait()
            hand.wait_recv()

        @pl.when(c != layer)
        def _():
            hand.wait_send()

    pipeline([to_core, to_near, to_far, to_line, to_end, finish], len(plan))
    for copy in pending:
        copy.wait_send()


def reduce_rows(values, widths, layer, olds, collective):
    depth = lax.axis_size("seq")
    plan, scratch = [], [[] for _ in range(6)]
    for item, (value, width) in enumerate(zip(values, widths)):
        chunks, half = value.shape[2] // width, value.shape[1] // 2
        for slot in range(chunks):
            plan.append((item, slot, pl.ds(slot * width, width)))
        block = (half, width)
        scratch[0].append(pltpu.VMEM((chunks, 2, 2, depth) + block, value.dtype))
        scratch[1].append(pltpu.VMEM((chunks, 2, 2, depth) + block, value.dtype))
        scratch[2].append(pltpu.VMEM((chunks, 2, depth) + block, value.dtype))
        scratch[3].append(pltpu.VMEM((chunks, depth) + block, value.dtype))
        scratch[4].append(pltpu.VMEM((chunks, depth - 1) + block, value.dtype))
        scratch[5].append(pltpu.VMEM((chunks,) + block, F32))
    items = len(values)
    anywhere = pl.BlockSpec(memory_space=pl.ANY)
    return pl.pallas_call(
        functools.partial(reduce_kernel, plan, depth, layer, items, len(olds)),
        in_specs=[anywhere] * (items + len(olds)),
        out_specs=[anywhere] * items,
        out_shape=[jax.ShapeDtypeStruct(v.shape[1:], F32) for v in values],
        scratch_shapes=sum(scratch, [])
        + [
            pltpu.SemaphoreType.DMA((len(plan), depth + 4)),
            pltpu.SemaphoreType.DMA((len(plan), depth + 4)),
            pltpu.SemaphoreType.DMA((len(plan), 2)),
        ],
        input_output_aliases={items + i: i for i in range(len(olds))},
        compiler_params=pltpu.CompilerParams(
            collective_id=collective, has_side_effects=True, vmem_limit_bytes=VMEM_LIMIT
        ),
        name="reduce_rows",
    )(*[v.reshape((2, 2, depth) + v.shape[1:]) for v in values], *olds)


def places(lengths, count, reach):
    steps = count // CHUNKS
    base = lax.axis_index("seq") * count
    starts = jnp.cumsum(lengths) - lengths
    here = (
        base + jnp.arange(steps, dtype=jnp.int32)[:, None]
        + steps * jnp.arange(CHUNKS, dtype=jnp.int32)[None, :]
    )

    def segment(at):
        return jnp.sum((starts[:, None, None] <= at[None]).astype(jnp.int32), axis=0) - 1

    own = segment(here)
    same = jnp.stack(
        [(segment(here - reach + k) == own).astype(F32) for k in range(reach + 1)]
    )
    opens = jnp.any(starts[:, None, None] == here[None], axis=0)
    cut = jnp.where(opens, CUT, 0.0).astype(F32).reshape(count, 1)
    return same, jnp.broadcast_to(cut, (count, LANES))


def layer_forward(xin, weights, same, cut, me):
    in_weight, out_weight, sel, stepw, small, rate, gain = weights
    count = xin.shape[0]
    inner = out_weight.shape[0]
    rank, nstate = stepw.shape[0], rate.shape[0]
    reach = same.shape[0] - 1
    scale = lax.rsqrt(jnp.mean(xin * xin, axis=-1, keepdims=True) + EPS)
    normed = (xin * scale * gain).astype(BF16)
    mixed = jnp.dot(normed, in_weight, preferred_element_type=F32).astype(BF16)
    last = mixed[(count - reach * CHUNKS) :, :inner].reshape(reach, CHUNKS, inner)[:, CHUNKS - 1]
    halo = shifted(last, "seq", 1)
    act, pre, selected = select_call(mixed[:, :inner], halo, same, small, sel)
    low = selected[:, :rank].astype(BF16)
    in_map = selected[:, rank : rank + nstate]
    out_map = selected[:, rank + nstate :]
    step, sig, enter, total, before, sums, moments = forward_totals(
        low, stepw, small, act, in_map, cut, rate
    )
    totals, all_sums = share(total, sums, 1)
    full, gated, keep = forward_states(
        me, step, act, mixed, in_map, out_map, cut, rate, small, enter, before, totals, all_sums
    )
    result = xin + jnp.dot(gated, out_weight, preferred_element_type=F32)
    saved = (xin, scale, normed, mixed, halo, act, pre, low, in_map, out_map, step, sig, full, gated, keep)
    return result, moments, saved


def outer_sum(left, right):
    return lax.dot_general(left, right, (((0,), (0,)), ((), ())), preferred_element_type=F32)


def times_transposed(left, right):
    return lax.dot_general(left, right, (((1,), (1,)), ((), ())), preferred_element_type=F32)


def layer_backward(grad_out, weights, same, cut, me, saved, moments):
    in_weight, out_weight, sel, stepw, small, rate, gain = weights
    (xin, scale, normed, mixed, halo, act, pre, low, in_map, out_map, step, sig, full, gated, keep) = saved
    count, inner = act.shape
    reach = same.shape[0] - 1
    grad_low = grad_out.astype(BF16)
    dgated = times_transposed(grad_low, out_weight)
    gout = outer_sum(gated, grad_low).astype(BF16)
    dfull, dgate, gskip, enter, total, before, sums = backward_totals(
        dgated, mixed, full, act, step, out_map, cut, rate
    )
    totals, all_sums = share(total, sums, 1)
    dact, gbias, gdecay, gstepw, dsel = backward_states(
        me, step, sig, act, dfull, in_map, out_map, cut, rate, small, enter, before, totals, all_sums, keep, low, stepw
    )
    dconv, tail, spill, gsel, gsmall = conv_grad(
        mixed[:, :inner], halo, same, small, sel, act, pre, dact, dsel
    )
    late = (tail + shifted(spill, "seq", -1)).astype(BF16)
    grid = dconv.reshape(count // CHUNKS, CHUNKS, inner)
    dconv = grid.at[count // CHUNKS - reach :, CHUNKS - 1].set(late).reshape(count, inner)
    dmixed = jnp.concatenate([dconv, dgate], axis=1)
    gin = outer_sum(normed, dmixed).astype(BF16)
    dnormed = times_transposed(dmixed, in_weight)
    unit = xin * scale
    ggain = jnp.sum(dnormed * unit, axis=0)
    dunit = dnormed * gain
    grad_in = scale * (dunit - unit * jnp.mean(dunit * unit, axis=-1, keepdims=True)) + grad_out
    shards = lax.axis_size(("dp", "seq"))
    per = inner // shards
    ggain = jnp.pad(ggain.reshape(shards, -1), ((0, 0), (0, per - ggain.shape[0] // shards)))
    rows = jnp.concatenate(
        [gsel, gstepw, gdecay, gsmall[: reach + 2], gbias, gskip, ggain.reshape(1, inner), moments,
         jnp.zeros((6, inner), F32)], axis=0,
    )
    return grad_in, gin, gout, rows


AXES = ("section", "dp", "seq")


def body(
    inputs, doc_lengths, out_grad, norm_gain, in_weight, conv_weight, conv_bias, select_weight,
    step_weight, step_bias, log_decay, skip_gain, out_weight,
):
    section = lax.axis_index("section")
    me = lax.axis_index("seq").reshape(1).astype(jnp.int32)
    micro, _, count, model = inputs.shape
    taps, per = conv_weight.shape[1:]
    shards = lax.axis_size(("dp", "seq"))
    inner = per * shards
    rank, nstate = step_weight.shape[1], log_decay.shape[1]
    wide = rank + 2 * nstate

    kernels = lax.axis_size("dp") == 4 and per % LANES == 0 and in_weight.shape[1] % 32 == 0
    pad = per - norm_gain.shape[1]
    rows = jnp.concatenate(
        [select_weight[0].T, step_weight[0], log_decay[0], conv_weight[0], conv_bias, step_bias, skip_gain,
         jnp.pad(norm_gain, ((0, 0), (0, pad))), jnp.zeros((8, per), BF16)], axis=0,
    )
    if kernels:
        got = gather_rows(
            [rows, rows, in_weight[0], in_weight[0], out_weight[0], out_weight[0]],
            [0, 1, 0, 1, 0, 1], [per, per, 512, 512, 256, 256], 2,
        )
        packed = [g.reshape(shards, -1, per) for g in got[:2]]
        in_all, out_all = got[2:4], got[4:6]
    else:
        packed = lax.all_gather(rows, AXES, axis=0).reshape(2, shards, -1, per)
        in_all = lax.all_gather(in_weight[0], AXES, axis=0, tiled=True).reshape(2, model, -1)
        out_all = lax.all_gather(out_weight[0], AXES, axis=0, tiled=True).reshape(2, inner, model)
    weights = []
    for layer in range(2):
        flat = packed[layer].swapaxes(0, 1).reshape(-1, inner)
        at = wide + rank + nstate
        small = flat[at : at + 16].astype(F32)
        gain = packed[layer][:, at + taps + 3, : norm_gain.shape[1]].reshape(-1).astype(F32)
        rate = -jnp.exp(flat[wide + rank : at].astype(F32)) * LOG2E
        small = jnp.concatenate([small[: taps + 3], jnp.zeros((1, inner), F32)], axis=0)
        weights.append(
            (in_all[layer], out_all[layer], flat[:wide], flat[wide : wide + rank], small, rate, gain)
        )

    mine = lambda value: lax.dynamic_index_in_dim(value, section, 0, keepdims=False)[0]
    same, cut = places(mine(doc_lengths), count, taps - 1)
    state = interleave(mine(inputs).astype(F32))
    outs, kept = [], []
    for layer in range(2):
        state, moments, saved = layer_forward(state, weights[layer], same, cut, me)
        outs.append(state)
        kept.append((saved, moments))
    grad = interleave(mine(out_grad).astype(F32))
    grads, gins, gouts, packs = [None] * 2, [None] * 2, [None] * 2, [None] * 2
    for layer in (1, 0):
        grad, gins[layer], gouts[layer], packs[layer] = layer_backward(
            grad, weights[layer], same, cut, me, *kept[layer]
        )
        grads[layer] = grad

    packs = [pack.reshape(-1, shards, per).swapaxes(0, 1) for pack in packs]
    gins = [g.reshape(shards, -1, g.shape[1]) for g in gins]
    gouts = [g.reshape(shards, -1, model) for g in gouts]
    if kernels:
        found = []
        for layer in (1, 0):
            found = reduce_rows(
                [packs[layer], gins[layer], gouts[layer]], [per, 512, 256], layer, found, 4 - layer
            )
        rows, gin, gout = found
    else:

        def settle(parts):
            return lax.psum_scatter(jnp.stack(parts).reshape((-1,) + parts[0].shape[1:]), AXES, scatter_dimension=0)

        rows, gin, gout = settle(packs), settle(gins).astype(F32), settle(gouts).astype(F32)

    def place(values):
        first, second = (in_order(value) for value in values)
        own = jnp.where(section == 0, first, second)
        other = jnp.where(section == 0, second, first)
        other = lax.ppermute(other, "section", [(0, 1), (1, 0)])
        both = jnp.stack([jnp.where(section == 0, own, other), jnp.where(section == 0, other, own)])
        return both[None, :, None]

    at = wide + rank + nstate
    tokens = micro * inputs.shape[1] * lax.axis_size("dp") * count * lax.axis_size("seq")
    return (
        place(outs),
        place(grads),
        rows[at + taps + 3, : norm_gain.shape[1]][None],
        gin[None],
        rows[at : at + taps][None],
        rows[at + taps][None],
        rows[:wide].T[None],
        rows[wide : wide + rank][None],
        rows[at + taps + 1][None],
        rows[wide + rank : at][None],
        rows[at + taps + 2][None],
        gout[None],
        (rows[at + taps + 4 : at + taps + 6] / tokens)[None],
    )


def solution(mesh):
    vector = P("section", ("dp", "seq"))
    matrix = P("section", ("dp", "seq"), None)
    turned = P("section", None, ("dp", "seq"))
    tokens = P(None, "dp", "seq", None)
    in_specs = (
        tokens, P(None, "dp", None), tokens, vector, matrix, turned, vector, matrix, turned,
        vector, turned, vector, matrix,
    )
    result = P("section", None, "dp", "seq", None)
    out_specs = (
        result, result, vector, matrix, turned, vector, matrix, turned, vector, turned, vector,
        matrix, turned,
    )
    return jax.shard_map(body, mesh=mesh, in_specs=in_specs, out_specs=out_specs, check_vma=False)
```

```python
import functools
import math

import jax
import jax.numpy as jnp
from jax import lax
from jax.experimental import pallas as pl
from jax.experimental.pallas import tpu as pltpu
from jax.sharding import PartitionSpec as P

EPS = 1e-05
LOG2E = math.log2(math.e)
LN2 = math.log(2.0)
CUT = 1e30
LANES = 128
CHUNKS = 8
VMEM_LIMIT = 66_000_000
F32 = jnp.float32
BF16 = jnp.bfloat16


def silu_slope(values):
    sigma = jax.nn.sigmoid(values)
    return sigma * (1.0 + values * (1.0 - sigma))


def interleave(rows):
    count = rows.shape[0]
    return rows.reshape(CHUNKS, count // CHUNKS, -1).swapaxes(0, 1).reshape(count, -1)


def in_order(rows):
    count = rows.shape[0]
    return rows.reshape(count // CHUNKS, CHUNKS, -1).swapaxes(0, 1).reshape(count, -1)


def column_params(**kw):
    return pltpu.CompilerParams(
        dimension_semantics=("arbitrary",), vmem_limit_bytes=VMEM_LIMIT, **kw
    )


def cols(rows, width=LANES):
    return pl.BlockSpec((rows, width), lambda j: (0, j))


def whole(*shape):
    return pl.BlockSpec(shape, lambda j: (0,) * len(shape))


def conv_taps(conv_ref, halo_ref, steps, reach):
    width = conv_ref.shape[1]
    own = conv_ref[...].astype(F32).reshape(steps, CHUNKS, width)
    tail = own[steps - reach :]
    moved = pltpu.roll(tail.reshape(reach * CHUNKS, width), 1, 0).reshape(reach, CHUNKS, width)
    first = lax.broadcasted_iota(jnp.int32, moved.shape, 1) == 0
    halo = halo_ref[...].astype(F32)[:, None, :]
    head = jnp.where(first, jnp.broadcast_to(halo, moved.shape), moved)
    return jnp.concatenate([head, own], axis=0)


def select_kernel(conv_ref, halo_ref, same_ref, small_ref, sel_ref, act_ref, pre_ref, out_ref, acc):
    j = pl.program_id(0)
    count, width = conv_ref.shape
    reach = halo_ref.shape[0]
    steps = count // CHUNKS
    ext = conv_taps(conv_ref, halo_ref, steps, reach)
    pre = jnp.broadcast_to(small_ref[reach + 1 : reach + 2, :], (count, width)).reshape(
        steps, CHUNKS, width
    )
    for k in range(reach + 1):
        weight = small_ref[k : k + 1, :]
        same = same_ref[k][:, :, None]
        pre = pre + (weight[None] * ext[k : k + steps]) * same
    pre = pre.reshape(count, width)
    pre_ref[...] = pre
    act = (pre * jax.nn.sigmoid(pre)).astype(BF16)
    act_ref[...] = act

    @pl.when(j == 0)
    def _():
        acc[...] = jnp.zeros_like(acc)

    acc[...] += lax.dot_general(
        act, sel_ref[...], (((1,), (1,)), ((), ())), preferred_element_type=F32
    )
    out_ref[...] = acc[...]


def select_call(conv_in, halo, same, small, sel):
    count, inner = conv_in.shape
    width = min(512, inner)
    wide = sel.shape[0]
    return pl.pallas_call(
        select_kernel,
        grid=(inner // width,),
        in_specs=[
            cols(count, width),
            cols(halo.shape[0], width),
            whole(*same.shape),
            cols(small.shape[0], width),
            cols(wide, width),
        ],
        out_specs=[cols(count, width), cols(count, width), whole(count, wide)],
        out_shape=[
            jax.ShapeDtypeStruct((count, inner), BF16),
            jax.ShapeDtypeStruct((count, inner), F32),
            jax.ShapeDtypeStruct((count, wide), F32),
        ],
        scratch_shapes=[pltpu.VMEM((count, wide), F32)],
        compiler_params=column_params(),
        name="conv_select",
    )(conv_in, halo, same, small, sel)


def spread(dst, src_ref, nstate, at):
    for n in range(nstate):
        dst[n] = jnp.broadcast_to(src_ref[:, at + n : at + n + 1], dst.shape[1:])


def chunk_links(ends, sums, rates, backward):
    row = lax.broadcasted_iota(jnp.int32, (CHUNKS, LANES), 0)
    gains = [jnp.exp2(sums * rate) for rate in rates]
    ends = list(ends)
    total = sums
    k = 1
    while k < CHUNKS:
        turn = CHUNKS - k if backward else k
        mask = row < CHUNKS - k if backward else row >= k
        ends = [
            jnp.where(mask, g * pltpu.roll(e, turn, 0) + e, e) for g, e in zip(gains, ends)
        ]
        gains = [jnp.where(mask, g * pltpu.roll(g, turn, 0), g) for g in gains]
        total = jnp.where(mask, pltpu.roll(total, turn, 0) + total, total)
        k *= 2
    turn = CHUNKS - 1 if backward else 1
    mask = row < CHUNKS - 1 if backward else row >= 1
    entering = [jnp.where(mask, pltpu.roll(e, turn, 0), 0.0) for e in ends]
    before = jnp.where(mask, pltpu.roll(total, turn, 0), 0.0)
    last = 0 if backward else CHUNKS - 1
    return entering, [e[last : last + 1] for e in ends], before, total[last : last + 1]


def rate_rows(rate_ref, nstate):
    return [jnp.broadcast_to(rate_ref[n : n + 1, :], (CHUNKS, LANES)) for n in range(nstate)]


def arriving_state(me, totals_ref, sums_ref, lanes, rate_ref, backward):
    devices = totals_ref.shape[0]
    state = jnp.zeros(rate_ref.shape, F32)
    order = range(devices - 1, 0, -1) if backward else range(devices - 1)
    for k in order:
        passed = jnp.exp2(rate_ref[...] * sums_ref[k, :, lanes]) * state
        passed = passed + totals_ref[k, :, lanes].astype(F32)
        state = jnp.where((k > me) if backward else (k < me), passed, state)
    return state


def conv_grad_kernel(
    conv_ref, halo_ref, same_ref, small_ref, sel_ref, act_ref, pre_ref, dact_ref, dsel_ref,
    dconv_ref, tail_ref, spill_ref, gsel_ref, gsmall_ref,
):
    count, width = conv_ref.shape
    reach = halo_ref.shape[0]
    steps = count // CHUNKS
    ext = conv_taps(conv_ref, halo_ref, steps, reach)
    dsel = dsel_ref[...]
    gsel_ref[...] = lax.dot_general(
        dsel, act_ref[...], (((0,), (0,)), ((), ())), preferred_element_type=F32
    )
    dact = dact_ref[...] + jnp.dot(dsel, sel_ref[...], preferred_element_type=F32)
    dpre = dact * silu_slope(pre_ref[...])
    gsmall_ref[reach + 1 : reach + 2, :] = jnp.sum(dpre, axis=0, keepdims=True)
    dpre = dpre.reshape(steps, CHUNKS, width)
    parts = []
    for k in range(reach + 1):
        masked = dpre * same_ref[k][:, :, None]
        gsmall_ref[k : k + 1, :] = jnp.sum(
            (masked * ext[k : k + steps]).reshape(count, width), axis=0, keepdims=True
        )
        parts.append(masked * small_ref[k : k + 1, :][None])
    own = parts[reach]
    for k in range(reach):
        back = reach - k
        own = own + jnp.concatenate(
            [parts[k][back:], jnp.zeros((back, CHUNKS, width), F32)], axis=0
        )
    heads = []
    for e in range(reach):
        total = parts[0][e]
        for k in range(1, e + 1):
            total = total + parts[k][e - k]
        heads.append(total)
    head = jnp.stack(heads)
    spill_ref[...] = head[:, 0, :]
    row = lax.broadcasted_iota(jnp.int32, head.shape, 1)
    moved = pltpu.roll(head.reshape(reach * CHUNKS, width), reach * CHUNKS - 1, 0)
    moved = jnp.where(row == CHUNKS - 1, 0.0, moved.reshape(head.shape))
    tail = own[steps - reach :] + moved
    tail_ref[...] = tail[:, CHUNKS - 1, :]
    dconv = jnp.concatenate([own[: steps - reach], tail], axis=0)
    dconv_ref[...] = dconv.reshape(count, width).astype(BF16)


def conv_grad(conv_in, halo, same, small, sel, act, pre, dact, dsel):
    count, inner = act.shape
    width = min(512, inner)
    reach = halo.shape[0]
    wide = sel.shape[0]
    return pl.pallas_call(
        conv_grad_kernel,
        grid=(inner // width,),
        in_specs=[
            cols(count, width),
            cols(reach, width),
            whole(*same.shape),
            cols(small.shape[0], width),
            cols(wide, width),
            cols(count, width),
            cols(count, width),
            cols(count, width),
            whole(count, wide),
        ],
        out_specs=[
            cols(count, width),
            cols(reach, width),
            cols(reach, width),
            cols(wide, width),
            cols(8, width),
        ],
        out_shape=[
            jax.ShapeDtypeStruct((count, inner), BF16),
            jax.ShapeDtypeStruct((reach, inner), F32),
            jax.ShapeDtypeStruct((reach, inner), F32),
            jax.ShapeDtypeStruct((wide, inner), F32),
            jax.ShapeDtypeStruct((8, inner), F32),
        ],
        compiler_params=column_params(),
        name="conv_grad",
    )(conv_in, halo, same, small, sel, act, pre, dact, dsel)


def shifted(value, axis, steps):
    count = lax.axis_size(axis)
    first, last = (max(0, -steps), min(count, count - steps))
    return lax.ppermute(value, axis, [(source, source + steps) for source in range(first, last)])


MESH = pl.DeviceIdType.MESH


def where_am_i():
    c, d, z = lax.axis_index("section"), lax.axis_index("dp"), lax.axis_index("seq")
    y, x = d // 2, d % 2
    flip_x, flip_y = y * 2 + (1 - x), (1 - y) * 2 + x
    return c, y, x, z, flip_x, flip_y


def peers_of(depth):
    c, y, x, z, flip_x, flip_y = where_am_i()
    peers = [{"section": 1 - c}, {"dp": flip_x}, {"dp": flip_y}]
    return peers + [{"seq": lax.rem(z + o, depth)} for o in range(1, depth)]


def hail(depth):
    barrier = pltpu.get_barrier_semaphore()
    for peer in peers_of(depth):
        pl.semaphore_signal(barrier, inc=1, device_id=peer, device_id_type=MESH)


def await_hails(depth):
    pl.semaphore_wait(pltpu.get_barrier_semaphore(), 2 + depth)


def greet(depth):
    hail(depth)
    await_hails(depth)


def pipeline(stages, count, lags):
    for turn in range(count + lags[-1]):
        for lag, stage in zip(lags, stages):
            if 0 <= turn - lag < count:
                stage(turn - lag)


class Gather:
    def __init__(self, depth, layer, width, base, src, out, mine, send, recv, local):
        self.depth, self.layer, self.width, self.base = depth, layer, width, base
        self.src, self.out, self.mine = src, out, mine
        self.send, self.recv, self.local = send, recv, local
        self.count = mine.shape[0]
        c, y, x, z, flip_x, flip_y = where_am_i()
        self.c, self.y, self.x, self.z = c, y, x, z
        self.near = {"dp": (1 - c) * flip_y + c * flip_x}
        self.far = {"dp": (1 - c) * flip_x + c * flip_y}
        self.near_at = (y + (1 - c) * (1 - 2 * y), x + c * (1 - 2 * x))
        self.far_at = (y + c * (1 - 2 * y), x + (1 - c) * (1 - 2 * x))
        self.partner = {"section": 1 - c}

    def cols(self, k, base=0):
        if isinstance(k, int):
            return pl.ds(base + k * self.width, self.width)
        return pl.ds(pl.multiple_of(base + k * self.width, LANES), self.width)

    def remote(self, k, slot, src, dst, peer):
        return pltpu.make_async_remote_copy(
            src_ref=src, dst_ref=dst, send_sem=self.send.at[k, slot], recv_sem=self.recv.at[k, slot],
            device_id=peer, device_id_type=MESH,
        )

    def piece(self, k, at):
        return self.out.at[at[0], at[1], :, self.c, :, self.cols(k)]

    def hand(self, k):
        half = self.mine.shape[1]
        src = self.src.at[pl.ds((1 - self.layer) * half, half), self.cols(k, self.base)]
        return self.remote(k, 0, src, self.mine.at[k], self.partner)

    def keep(self, k):
        half = self.mine.shape[1]
        src = self.src.at[pl.ds(self.layer * half, half), self.cols(k, self.base)]
        return pltpu.make_async_copy(src, self.mine.at[k], self.local.at[k, 0])

    def line(self, k):
        target = self.out.at[self.y, self.x, self.z, self.c, :, self.cols(k)]
        return [
            self.remote(k, o, self.mine.at[k], target, {"seq": lax.rem(self.z + o, self.depth)})
            for o in range(1, self.depth)
        ]

    def place(self, k):
        target = self.out.at[self.y, self.x, self.z, self.c, :, self.cols(k)]
        return pltpu.make_async_copy(self.mine.at[k], target, self.local.at[k, 1])

    def move(self, k, slot, at, peer):
        return self.remote(k, self.depth + slot, self.piece(k, at), self.piece(k, at), peer)

    def near_own(self, k):
        return self.move(k, 0, (self.y, self.x), self.near)

    def far_own(self, k):
        return self.move(k, 1, (self.y, self.x), self.far)

    def far_other(self, k):
        return self.move(k, 2, self.near_at, self.far)

    def crossings(self, k):
        places = ((self.y, self.x), self.near_at, self.far_at, (1 - self.y, 1 - self.x))
        return [lambda i=i, at=at: self.move(k, 3 + i, at, self.partner) for i, at in enumerate(places)]

    def first(self, k):
        @pl.when(self.c == self.layer)
        def _():
            self.hand(k).start()
            self.keep(k).start()

    def along_z(self, k):
        @pl.when(self.c == self.layer)
        def _():
            self.hand(k).wait_send()
            self.keep(k).wait()

        @pl.when(self.c != self.layer)
        def _():
            self.hand(k).wait_recv()

        for copy in self.line(k):
            copy.start()
        self.place(k).start()

    def along_near(self, k):
        for copy in self.line(k):
            copy.wait_recv()
        self.place(k).wait()
        self.near_own(k).start()
        self.crossings(k)[0]().start()

    def along_far(self, k):
        self.near_own(k).wait_recv()
        self.far_own(k).start()
        self.far_other(k).start()
        self.crossings(k)[1]().start()

    def across(self, k):
        self.far_own(k).wait_recv()
        self.far_other(k).wait_recv()
        self.crossings(k)[2]().start()
        self.crossings(k)[3]().start()

    def finish(self, k):
        for copy in self.crossings(k):
            copy().wait()
        for copy in self.line(k) + [self.near_own(k), self.far_own(k), self.far_other(k)]:
            copy.wait_send()

    def stages(self):
        return [self.along_z, self.along_near, self.along_far, self.across, self.finish]


def gather_scratch(specs, depth):
    scratch = []
    for rows, columns, width, dtype in specs:
        chunks = columns // width
        scratch += [
            pltpu.VMEM((chunks, rows // 2, width), dtype),
            pltpu.SemaphoreType.DMA((chunks, depth + 7)),
            pltpu.SemaphoreType.DMA((chunks, depth + 7)),
            pltpu.SemaphoreType.DMA((chunks, 2)),
        ]
    return scratch


def gather_shape(rows, columns, depth, dtype):
    return jax.ShapeDtypeStruct((2, 2, depth, 2, rows // 2, columns), dtype)


def gather_kernel(tasks, depth, *refs):
    count = len(tasks)
    srcs, outs, rest = refs[:count], refs[count : 2 * count], refs[2 * count :]
    greet(depth)
    work = []
    for i, (layer, width, base) in enumerate(tasks):
        gather = Gather(depth, layer, width, base, srcs[i], outs[i], *rest[4 * i : 4 * i + 4])
        work += [(gather, k) for k in range(gather.count)]
    for gather, k in work:
        gather.first(k)
    pipeline(
        [lambda i, s=s: work[i][0].stages()[s](work[i][1]) for s in range(5)],
        len(work), (0, 2, 4, 6, 8),
    )


def gather_rows(sources, tasks, columns, collective):
    depth = lax.axis_size("seq")
    anywhere = pl.BlockSpec(memory_space=pl.ANY)
    outs = pl.pallas_call(
        functools.partial(gather_kernel, tasks, depth),
        in_specs=[anywhere] * len(sources),
        out_specs=[anywhere] * len(sources),
        out_shape=[
            gather_shape(s.shape[0], n, depth, s.dtype) for s, n in zip(sources, columns)
        ],
        scratch_shapes=gather_scratch(
            [(s.shape[0], n, t[1], s.dtype) for s, t, n in zip(sources, tasks, columns)], depth
        ),
        compiler_params=pltpu.CompilerParams(
            collective_id=collective, has_side_effects=True, vmem_limit_bytes=VMEM_LIMIT
        ),
        name="gather_rows",
    )(*sources)
    return [flat_rows(out) for out in outs]


def flat_rows(out):
    return out.reshape(-1, out.shape[-1])


class Reduce:
    def __init__(self, depth, layer, width, src, out, own, core, side, edge, line, done, send, recv, local):
        self.depth, self.layer, self.width, self.src, self.out = depth, layer, width, src, out
        self.own, self.core, self.side, self.edge, self.line = own, core, side, edge, line
        self.done, self.send, self.recv, self.local = done, send, recv, local
        self.count = own.shape[0]
        self.half = own.shape[4]
        c, y, x, z, flip_x, flip_y = where_am_i()
        self.c, self.y, self.x, self.z = c, y, x, z
        self.near = {"dp": (1 - c) * flip_x + c * flip_y}
        self.far = {"dp": (1 - c) * flip_y + c * flip_x}
        self.kept = (1 - c) * y + c * x
        self.partner = {"section": 1 - c}

    def cols(self, k):
        if isinstance(k, int):
            return pl.ds(k * self.width, self.width)
        return pl.ds(pl.multiple_of(k * self.width, LANES), self.width)

    def remote(self, k, slot, src, dst, peer):
        return pltpu.make_async_remote_copy(
            src_ref=src, dst_ref=dst, send_sem=self.send.at[k, slot], recv_sem=self.recv.at[k, slot],
            device_id=peer, device_id_type=MESH,
        )

    def hand(self, k):
        theirs = self.src.at[:, :, :, pl.ds((1 - self.c) * self.half, self.half), self.cols(k)]
        return self.remote(k, 0, theirs, self.core.at[k], self.partner)

    def keep(self, k):
        ours = self.src.at[:, :, :, pl.ds(self.c * self.half, self.half), self.cols(k)]
        return pltpu.make_async_copy(ours, self.own.at[k], self.local.at[k, 0])

    def sides(self, k):
        c = self.c
        return [
            self.remote(
                k, 1 + u,
                self.core.at[k, (1 - c) * u + c * (1 - self.y), (1 - c) * (1 - self.x) + c * u],
                self.side.at[k, u], self.near,
            )
            for u in (0, 1)
        ]

    def edges(self, k):
        return self.remote(k, 3, self.side.at[k, 1 - self.kept], self.edge.at[k], self.far)

    def lines(self, k):
        copies = []
        for o in range(1, self.depth):
            peer = lax.rem(self.z + o, self.depth)
            copies.append(
                self.remote(k, 3 + o, self.edge.at[k, peer], self.line.at[k, o - 1], {"seq": peer})
            )
        return copies

    def target(self):
        return pl.ds(self.c * self.half, self.half)

    def give(self, k):
        target = self.out.at[self.target(), self.cols(k)]
        return self.remote(k, 3 + self.depth, self.done.at[k], target, self.partner)

    def take(self, k):
        target = self.out.at[self.target(), self.cols(k)]
        return pltpu.make_async_copy(self.done.at[k], target, self.local.at[k, 1])

    def to_core(self, k):
        self.hand(k).start()
        self.keep(k).start()

    def to_near(self, k):
        self.hand(k).wait_recv()
        self.keep(k).wait()
        core, own, depth = self.core, self.own, self.depth

        def add(i, _):
            a, b, e = i // (2 * depth), (i // depth) % 2, i % depth
            core[k, a, b, e] = core[k, a, b, e] + own[k, a, b, e]
            return 0

        lax.fori_loop(0, 4 * depth, add, 0)
        for copy in self.sides(k):
            copy.start()

    def to_far(self, k):
        for copy in self.sides(k):
            copy.wait_recv()
        core, side, depth, c = self.core, self.side, self.depth, self.c

        def add(i, _):
            u, e = i // depth, i % depth
            kept = core[k, (1 - c) * u + c * self.y, (1 - c) * self.x + c * u, e]
            side[k, u, e] = side[k, u, e] + kept
            return 0

        lax.fori_loop(0, 2 * depth, add, 0)
        self.edges(k).start()

    def to_line(self, k):
        self.edges(k).wait_recv()
        edge, side = self.edge, self.side

        def add(e, _):
            edge[k, e] = edge[k, e] + side[k, self.kept, e]
            return 0

        lax.fori_loop(0, self.depth, add, 0)
        for copy in self.lines(k):
            copy.start()

    def to_end(self, k):
        for copy in self.lines(k):
            copy.wait_recv()
        total = self.edge[k, self.z].astype(F32)
        for o in range(self.depth - 1):
            total = total + self.line[k, o].astype(F32)
        self.done[k] = total

        @pl.when(self.c == self.layer)
        def _():
            self.take(k).start()

        @pl.when(self.c != self.layer)
        def _():
            self.give(k).start()

    def finish(self, k):
        @pl.when(self.c == self.layer)
        def _():
            self.take(k).wait()
            self.give(k).wait_recv()

        @pl.when(self.c != self.layer)
        def _():
            self.give(k).wait_send()

        for copy in [self.hand(k), self.edges(k)] + self.sides(k) + self.lines(k):
            copy.wait_send()

    def stages(self):
        return [self.to_core, self.to_near, self.to_far, self.to_line, self.to_end, self.finish]


def reduce_scratch(specs, depth):
    scratch = []
    for rows, columns, width, dtype in specs:
        chunks, block = columns // width, (rows // 2, width)
        scratch += [
            pltpu.VMEM((chunks, 2, 2, depth) + block, dtype),
            pltpu.VMEM((chunks, 2, 2, depth) + block, dtype),
            pltpu.VMEM((chunks, 2, depth) + block, dtype),
            pltpu.VMEM((chunks, depth) + block, dtype),
            pltpu.VMEM((chunks, depth - 1) + block, dtype),
            pltpu.VMEM((chunks,) + block, F32),
            pltpu.SemaphoreType.DMA((chunks, depth + 4)),
            pltpu.SemaphoreType.DMA((chunks, depth + 4)),
            pltpu.SemaphoreType.DMA((chunks, 2)),
        ]
    return scratch


def by_chip(value, depth):
    return value.reshape((2, 2, depth) + value.shape[1:])


def reduce_kernel(tasks, depth, *refs):
    count = len(tasks)
    srcs, outs, rest = refs[:count], refs[count : 2 * count], refs[2 * count :]
    greet(depth)
    work = []
    for i, (layer, width) in enumerate(tasks):
        item = Reduce(depth, layer, width, srcs[i], outs[i], *rest[9 * i : 9 * i + 9])
        work += [(item, k) for k in range(item.count)]
    pipeline(
        [lambda i, s=s: work[i][0].stages()[s](work[i][1]) for s in range(6)],
        len(work), (0, 1, 3, 5, 7, 9),
    )


def reduce_rows(values, tasks, collective):
    depth = lax.axis_size("seq")
    anywhere = pl.BlockSpec(memory_space=pl.ANY)
    return pl.pallas_call(
        functools.partial(reduce_kernel, tasks, depth),
        in_specs=[anywhere] * len(values),
        out_specs=[anywhere] * len(values),
        out_shape=[jax.ShapeDtypeStruct(v.shape[1:], F32) for v in values],
        scratch_shapes=reduce_scratch(
            [v.shape[1:] + (t[1], v.dtype) for v, t in zip(values, tasks)], depth
        ),
        compiler_params=pltpu.CompilerParams(
            collective_id=collective, has_side_effects=True, vmem_limit_bytes=VMEM_LIMIT
        ),
        name="reduce_rows",
    )(*[by_chip(v, depth) for v in values])


def scan_map(phases, shift=0):
    def index(p, j, last):
        if phases == 2:
            return shift + j
        if phases == 0:
            return shift + j * (1 - p) + last * p
        return shift + j * p

    return index


def spec(rows, last, phases, width=LANES):
    index = scan_map(phases)
    return pl.BlockSpec((rows, width), lambda p, j: (0, index(p, j, last)))


def fixed(*shape):
    return pl.BlockSpec(shape, lambda p, j: (0,) * len(shape))


def timetable(turn, blocks, weight, slots, works):
    total = sum(count for count, _ in works)
    if not total:
        return
    span = (blocks - 1) * (1 + weight) + 1 - slots[-1]
    assert total * weight <= span + weight

    def chunk(at, start):
        past = jnp.where(at < blocks, at, blocks + (at - blocks) * weight) - start
        return jnp.where((past < 0) | (at < 0), -1, past * total // span)

    for stage, start in enumerate(slots):
        k = chunk(turn, start)
        due = (k != chunk(turn - 1, start)) & (k < total)
        base = 0
        for count, stages in works:
            local = k - base

            @pl.when(due & (local >= 0) & (local < count))
            def _(stages=stages, local=local, stage=stage):
                stages[stage](local)

            base += count

    @pl.when(turn == 2 * blocks - 1)
    def _():
        for count, stages in works:
            lax.fori_loop(0, count, lambda k, _, s=stages[-1]: (s(k), 0)[1], 0)


def exchange(total_ref, sum_ref, totals_ref, sums_ref, send, recv):
    count = totals_ref.shape[0]
    me = lax.axis_index("seq")
    copies = []
    for o in range(1, count):
        peer = {"seq": lax.rem(me + o, count)}
        for i, (src, dst) in enumerate(((total_ref, totals_ref), (sum_ref, sums_ref))):
            copies.append(
                pltpu.make_async_remote_copy(
                    src_ref=src, dst_ref=dst.at[me], send_sem=send.at[i, o - 1],
                    recv_sem=recv.at[i, o - 1], device_id=peer, device_id_type=MESH,
                )
            )
    for copy in copies:
        copy.start()
    for copy in copies:
        copy.wait()


def forward_scan_kernel(
    tasks, depth, lead, stepw_ref, small_ref, act_ref, sel_ref, cut_ref, rate_ref, *refs
):
    hosted = len(tasks)
    srcs, refs = refs[:hosted], refs[hosted:]
    (step_ref, sig_ref, moment_ref, full_ref, keep_ref), refs = refs[:5], refs[5:]
    gouts, refs = refs[:hosted], refs[hosted:]
    (low, inb, outb, decay, drives, enter, befores, total_ref, sum_ref, totals_ref, sums_ref, send, recv), rest = refs[:13], refs[13:]
    count = act_ref.shape[0]
    nstate = rate_ref.shape[0]
    rank = low.shape[1]
    p, j = pl.program_id(0), pl.program_id(1)
    blocks = pl.num_programs(1)
    turn = p * blocks + j
    me = lax.axis_index("seq")
    lanes = pl.ds(pl.multiple_of(j * LANES, LANES), LANES)
    gathers = [
        Gather(depth, layer, width, base, srcs[i], gouts[i], *rest[4 * i : 4 * i + 4])
        for i, (layer, width, base, _) in enumerate(tasks)
    ]

    @pl.when(turn == 0)
    def _():
        hail(depth)
        low[...] = sel_ref[:, :rank].astype(BF16)
        spread(inb, sel_ref, nstate, rank)
        spread(outb, sel_ref, nstate, rank + nstate)

    @pl.when(turn == 1)
    def _():
        await_hails(depth)
        for gather in gathers:
            lax.fori_loop(0, gather.count, lambda k, _, g=gather: (g.first(k), 0)[1], 0)

    timetable(turn, lead, 1, (2, 5, 9, 14), [(g.count, g.stages()) for g in gathers])

    @pl.when(p == 0)
    def _():
        pre = jnp.dot(low[...], stepw_ref[...], preferred_element_type=F32) + small_ref[5:6, :]
        near = jnp.exp(-jnp.abs(pre))
        step_all = jnp.maximum(pre, 0.0) + jnp.log1p(near)
        step_ref[...] = step_all
        sig_ref[...] = jnp.where(pre >= 0.0, 1.0, near) / (1.0 + near)
        moment_ref[0:1, :] = jnp.sum(step_all, axis=0, keepdims=True)
        moment_ref[1:2, :] = jnp.sum(step_all * step_all, axis=0, keepdims=True)
        rates = rate_rows(rate_ref, nstate)

        def body(pair, carry):
            states, sums = carry
            act = act_ref[pl.ds(pl.multiple_of(pair * 16, 16), 16), :].astype(F32)
            for half in (0, 1):
                at = pl.ds(pl.multiple_of(pair * 16 + half * 8, 8), 8)
                step = step_ref[at, :]
                away = step + cut_ref[at, :]
                drive = step * act[half * 8 : half * 8 + 8]
                drives[j, at, :] = drive
                sums = sums + away
                new = []
                for n in range(nstate):
                    gain = jnp.exp2(away * rates[n])
                    decay[j, n, at, :] = gain
                    new.append(gain * states[n] + drive * inb[n, at, :])
                states = tuple(new)
            return states, sums

        zero = jnp.zeros((CHUNKS, LANES), F32)
        ends, sums = lax.fori_loop(0, count // 16, body, ((zero,) * nstate, zero), unroll=2)
        entering, totals, before, total = chunk_links(ends, sums, rates, False)
        for n in range(nstate):
            enter[j, n] = entering[n]
        total_ref[:, lanes] = jnp.concatenate(totals, axis=0).astype(total_ref.dtype)
        befores[j] = before
        sum_ref[:, lanes] = total

    @pl.when(turn == blocks)
    def _():
        exchange(total_ref, sum_ref, totals_ref, sums_ref, send, recv)

    @pl.when(p == 1)
    def _():
        rates = rate_rows(rate_ref, nstate)
        arrived = arriving_state(me, totals_ref, sums_ref, lanes, rate_ref, False)
        before = befores[j]
        states = tuple(
            enter[j, n] + jnp.exp2(before * rates[n]) * arrived[n : n + 1, :] for n in range(nstate)
        )
        skip = jnp.broadcast_to(small_ref[6:7, :], (CHUNKS, LANES))

        def body(pair, states):
            rows = pl.ds(pl.multiple_of(pair * 16, 16), 16)
            act = act_ref[rows, :].astype(F32)
            held = []
            for half in (0, 1):
                at = pl.ds(pl.multiple_of(pair * 16 + half * 8, 8), 8)
                held.append(states)
                drive = drives[j, at, :]
                out = skip * act[half * 8 : half * 8 + 8]
                new = []
                for n in range(nstate):
                    state = decay[j, n, at, :] * states[n] + drive * inb[n, at, :]
                    out = out + state * outb[n, at, :]
                    new.append(state)
                states = tuple(new)
                full_ref[at, :] = out
            for n in range(nstate):
                both = jnp.concatenate([held[0][n], held[1][n]], axis=0)
                keep_ref[0, n, rows, :] = both.astype(keep_ref.dtype)
            return states

        ends = lax.fori_loop(0, count // 16, body, states, unroll=2)
        for n in range(nstate):
            both = jnp.concatenate([ends[n], ends[n]], axis=0)
            keep_ref[0, n, count : count + 16, :] = both.astype(keep_ref.dtype)


def forward_scan(stepw, small, act, selected, cut, rate, sources, tasks, collective):
    count, inner = act.shape
    nstate, rank = rate.shape[0], stepw.shape[0]
    depth = lax.axis_size("seq")
    blocks = inner // LANES
    last = blocks - 1
    anywhere = pl.BlockSpec(memory_space=pl.ANY)
    outs = pl.pallas_call(
        functools.partial(forward_scan_kernel, tasks, depth, blocks),
        grid=(2, blocks),
        in_specs=[
            spec(rank, last, 0),
            spec(small.shape[0], last, 2),
            spec(count, last, 2),
            fixed(*selected.shape),
            fixed(count, LANES),
            spec(nstate, last, 2),
        ]
        + [anywhere] * len(tasks),
        out_specs=[
            spec(count, last, 0),
            spec(count, last, 0),
            spec(2, last, 0),
            spec(count, last, 1),
            pl.BlockSpec((1, nstate, count + 16, LANES), lambda p, j: (j * p, 0, 0, 0)),
        ]
        + [anywhere] * len(tasks),
        out_shape=[
            jax.ShapeDtypeStruct((count, inner), F32),
            jax.ShapeDtypeStruct((count, inner), F32),
            jax.ShapeDtypeStruct((2, inner), F32),
            jax.ShapeDtypeStruct((count, inner), F32),
            jax.ShapeDtypeStruct((blocks, nstate, count + 16, LANES), BF16),
        ]
        + [gather_shape(s.shape[0], t[3], depth, s.dtype) for s, t in zip(sources, tasks)],
        scratch_shapes=[
            pltpu.VMEM((count, rank), BF16),
            pltpu.VMEM((nstate, count, LANES), F32),
            pltpu.VMEM((nstate, count, LANES), F32),
            pltpu.VMEM((blocks, nstate, count, LANES), F32),
            pltpu.VMEM((blocks, count, LANES), F32),
            pltpu.VMEM((blocks, nstate, CHUNKS, LANES), F32),
            pltpu.VMEM((blocks, CHUNKS, LANES), F32),
            pltpu.VMEM((nstate, inner), BF16),
            pltpu.VMEM((1, inner), F32),
            pltpu.VMEM((depth, nstate, inner), BF16),
            pltpu.VMEM((depth, 1, inner), F32),
            pltpu.SemaphoreType.DMA((2, depth - 1)),
            pltpu.SemaphoreType.DMA((2, depth - 1)),
        ]
        + gather_scratch([(s.shape[0], t[3], t[1], s.dtype) for s, t in zip(sources, tasks)], depth),
        compiler_params=pltpu.CompilerParams(
            dimension_semantics=("arbitrary", "arbitrary"), collective_id=collective,
            has_side_effects=True, vmem_limit_bytes=VMEM_LIMIT,
        ),
        name="forward_scan",
    )(stepw, small, act, selected, cut, rate, *sources)
    return outs[:5], [flat_rows(out) for out in outs[5:]]


def backward_scan_kernel(
    tasks, depth, lead, dfull_ref, step_ref, cut_ref, rate_ref, sel_ref, act_ref, sig_ref, keep_ref,
    small_ref, stepw_ref, *refs
):
    hosted = len(tasks)
    srcs, refs = refs[:hosted], refs[hosted:]
    (dact_ref, gbias_ref, gskip_ref, gdecay_ref, gstepw_ref, dsel_ref), refs = refs[:6], refs[6:]
    gouts, refs = refs[:hosted], refs[hosted:]
    (
        low, inb, outb, decay, enter, befores, total_ref, sum_ref, totals_ref, sums_ref,
        din_acc, dout_acc, decay_acc, dlow_acc, dstep_buf, send, recv,
    ), rest = refs[:17], refs[17:]
    count = act_ref.shape[0]
    nstate = rate_ref.shape[0]
    rank = low.shape[1]
    pairs = count // 16
    p, j = pl.program_id(0), pl.program_id(1)
    blocks = pl.num_programs(1)
    turn = p * blocks + j
    me = lax.axis_index("seq")
    lanes = pl.ds(pl.multiple_of(j * LANES, LANES), LANES)
    items = [
        Reduce(depth, layer, width, srcs[i], gouts[i], *rest[9 * i : 9 * i + 9])
        for i, (layer, width) in enumerate(tasks)
    ]

    @pl.when(turn == 0)
    def _():
        hail(depth)
        low[...] = sel_ref[:, :rank].astype(BF16)
        spread(inb, sel_ref, nstate, rank)
        spread(outb, sel_ref, nstate, rank + nstate)
        din_acc[...] = jnp.zeros_like(din_acc)
        dout_acc[...] = jnp.zeros_like(dout_acc)
        dlow_acc[...] = jnp.zeros_like(dlow_acc)

    @pl.when(turn == 1)
    def _():
        await_hails(depth)

    timetable(
        turn, lead, 2, (1, 4, 8, 11, 14), [(item.count, item.stages()) for item in items]
    )

    @pl.when(p == 0)
    def _():
        rates = rate_rows(rate_ref, nstate)

        def body(step_back, carry):
            states, sums = carry
            pair = pairs - 1 - step_back
            for half in (1, 0):
                at = pl.ds(pl.multiple_of(pair * 16 + half * 8, 8), 8)
                away = step_ref[at, :] + cut_ref[at, :]
                grad = dfull_ref[at, :]
                sums = sums + away
                new = []
                for n in range(nstate):
                    gain = jnp.exp2(away * rates[n])
                    decay[j, n, at, :] = gain
                    new.append(gain * (states[n] + outb[n, at, :] * grad))
                states = tuple(new)
            return states, sums

        zero = jnp.zeros((CHUNKS, LANES), F32)
        ends, sums = lax.fori_loop(0, pairs, body, ((zero,) * nstate, zero), unroll=2)
        entering, totals, before, total = chunk_links(ends, sums, rates, True)
        for n in range(nstate):
            enter[j, n] = entering[n]
        total_ref[:, lanes] = jnp.concatenate(totals, axis=0).astype(total_ref.dtype)
        befores[j] = before
        sum_ref[:, lanes] = total

    @pl.when(turn == blocks)
    def _():
        exchange(total_ref, sum_ref, totals_ref, sums_ref, send, recv)

    @pl.when(p == 1)
    def _():
        rates = rate_rows(rate_ref, nstate)
        arrived = arriving_state(me, totals_ref, sums_ref, lanes, rate_ref, True)
        before = befores[j]
        states = tuple(
            enter[j, n] + jnp.exp2(before * rates[n]) * arrived[n : n + 1, :] for n in range(nstate)
        )
        skip = jnp.broadcast_to(small_ref[6:7, :], (CHUNKS, LANES))
        for n in range(nstate):
            decay_acc[n] = jnp.zeros((CHUNKS, LANES), F32)
            last = keep_ref[0, n, count : count + 16, :].astype(F32)[0:CHUNKS]
            dout_acc[n, pl.ds(count, CHUNKS), :] += last * dfull_ref[pl.ds(count - CHUNKS, CHUNKS), :]

        def body(step_back, carry):
            states, gskip = carry
            pair = pairs - 1 - step_back
            rows = pl.ds(pl.multiple_of(pair * 16, 16), 16)
            act = act_ref[rows, :].astype(F32)
            held = [keep_ref[0, n, rows, :].astype(F32) for n in range(nstate)]
            sums = [None] * nstate
            for half in (1, 0):
                at = pl.ds(pl.multiple_of(pair * 16 + half * 8, 8), 8)
                step = step_ref[at, :]
                act_now = act[half * 8 : half * 8 + 8]
                drive = step * act_now
                grad = dfull_ref[at, :]
                gskip = gskip + grad * act_now
                if half:
                    earlier = dfull_ref[pl.ds(pl.multiple_of(pair * 16, 8), 8), :]
                else:
                    earlier = dfull_ref[pl.ds(pl.multiple_of(jnp.maximum(pair * 16 - 8, 0), 8), 8), :]
                by_rate = jnp.zeros((CHUNKS, LANES), F32)
                mapped = jnp.zeros((CHUNKS, LANES), F32)
                new = []
                for n in range(nstate):
                    prior = held[n][half * 8 : half * 8 + 8]
                    adjoint = states[n] + outb[n, at, :] * grad
                    passed = adjoint * decay[j, n, at, :]
                    rho = passed * prior
                    by_rate = by_rate + rho * rates[n]
                    mapped = mapped + adjoint * inb[n, at, :]
                    sums[n] = rho * step if half else sums[n] + rho * step
                    din_acc[n, at, :] += adjoint * drive
                    dout_acc[n, at, :] += prior * earlier
                    new.append(passed)
                states = tuple(new)
                dstep_buf[at, :] = by_rate * LN2 + act_now * mapped
                dact_ref[at, :] = step * mapped + skip * grad
            for n in range(nstate):
                decay_acc[n] += sums[n]
            return states, gskip

        _, gskip = lax.fori_loop(0, pairs, body, (states, jnp.zeros((CHUNKS, LANES), F32)))
        gskip_ref[...] = jnp.sum(gskip, axis=0, keepdims=True)
        for n in range(nstate):
            gdecay_ref[n : n + 1, :] = (rate_ref[n : n + 1, :] * LN2) * jnp.sum(
                decay_acc[n], axis=0, keepdims=True
            )
        dpre = dstep_buf[...] * sig_ref[...]
        gbias_ref[...] = jnp.sum(dpre, axis=0, keepdims=True)
        low_dpre = dpre.astype(BF16)
        gstepw_ref[...] = lax.dot_general(
            low[...], low_dpre, (((0,), (0,)), ((), ())), preferred_element_type=F32
        )
        dlow_acc[...] += lax.dot_general(
            low_dpre, stepw_ref[...], (((1,), (1,)), ((), ())), preferred_element_type=F32
        )

    @pl.when(turn == 2 * lead - 1)
    def _():
        column = lax.broadcasted_iota(jnp.int32, (LANES, nstate), 1)
        din = jnp.zeros((count, nstate), F32)
        dout = jnp.zeros((count, nstate), F32)
        for n in range(nstate):
            pick = (column == n).astype(BF16)
            din = din + jnp.dot(din_acc[n].astype(BF16), pick, preferred_element_type=F32)
            part = dout_acc[n, CHUNKS : count + CHUNKS, :].astype(BF16)
            dout = dout + jnp.dot(part, pick, preferred_element_type=F32)
        dsel_ref[...] = jnp.concatenate([dlow_acc[...], din, dout], axis=1).astype(BF16)


def backward_scan(
    dfull, step, cut, rate, selected, act, sig, keep, small, stepw, sources, tasks, collective
):
    count, inner = act.shape
    nstate, rank = rate.shape[0], stepw.shape[0]
    depth = lax.axis_size("seq")
    blocks = inner // LANES
    last = blocks - 1
    anywhere = pl.BlockSpec(memory_space=pl.ANY)
    outs = pl.pallas_call(
        functools.partial(backward_scan_kernel, tasks, depth, blocks),
        grid=(2, blocks),
        in_specs=[
            spec(count, last, 2),
            spec(count, last, 2),
            fixed(count, LANES),
            spec(nstate, last, 2),
            fixed(*selected.shape),
            spec(count, last, 1),
            spec(count, last, 1),
            pl.BlockSpec((1, nstate, count + 16, LANES), lambda p, j: (j * p, 0, 0, 0)),
            spec(small.shape[0], last, 1),
            spec(rank, last, 1),
        ]
        + [anywhere] * len(tasks),
        out_specs=[
            spec(count, last, 1),
            spec(1, last, 1),
            spec(1, last, 1),
            spec(nstate, last, 1),
            spec(rank, last, 1),
            fixed(*selected.shape),
        ]
        + [anywhere] * len(tasks),
        out_shape=[
            jax.ShapeDtypeStruct((count, inner), F32),
            jax.ShapeDtypeStruct((1, inner), F32),
            jax.ShapeDtypeStruct((1, inner), F32),
            jax.ShapeDtypeStruct((nstate, inner), F32),
            jax.ShapeDtypeStruct((rank, inner), F32),
            jax.ShapeDtypeStruct(selected.shape, BF16),
        ]
        + [jax.ShapeDtypeStruct(s.shape[1:], F32) for s in sources],
        scratch_shapes=[
            pltpu.VMEM((count, rank), BF16),
            pltpu.VMEM((nstate, count, LANES), F32),
            pltpu.VMEM((nstate, count, LANES), F32),
            pltpu.VMEM((blocks, nstate, count, LANES), F32),
            pltpu.VMEM((blocks, nstate, CHUNKS, LANES), F32),
            pltpu.VMEM((blocks, CHUNKS, LANES), F32),
            pltpu.VMEM((nstate, inner), BF16),
            pltpu.VMEM((1, inner), F32),
            pltpu.VMEM((depth, nstate, inner), BF16),
            pltpu.VMEM((depth, 1, inner), F32),
            pltpu.VMEM((nstate, count, LANES), F32),
            pltpu.VMEM((nstate, count + CHUNKS, LANES), F32),
            pltpu.VMEM((nstate, CHUNKS, LANES), F32),
            pltpu.VMEM((count, rank), F32),
            pltpu.VMEM((count, LANES), F32),
            pltpu.SemaphoreType.DMA((2, depth - 1)),
            pltpu.SemaphoreType.DMA((2, depth - 1)),
        ]
        + reduce_scratch([s.shape[1:] + (t[1], s.dtype) for s, t in zip(sources, tasks)], depth),
        compiler_params=pltpu.CompilerParams(
            dimension_semantics=("arbitrary", "arbitrary"), collective_id=collective,
            has_side_effects=True, vmem_limit_bytes=VMEM_LIMIT,
        ),
        name="backward_scan",
    )(dfull, step, cut, rate, selected, act, sig, keep, small, stepw, *[by_chip(s, depth) for s in sources])
    return outs[:6], outs[6:]


def places(lengths, count, reach):
    steps = count // CHUNKS
    base = lax.axis_index("seq") * count
    starts = jnp.cumsum(lengths) - lengths
    here = (
        base + jnp.arange(steps, dtype=jnp.int32)[:, None]
        + steps * jnp.arange(CHUNKS, dtype=jnp.int32)[None, :]
    )

    def segment(at):
        return jnp.sum((starts[:, None, None] <= at[None]).astype(jnp.int32), axis=0) - 1

    own = segment(here)
    same = jnp.stack(
        [(segment(here - reach + k) == own).astype(F32) for k in range(reach + 1)]
    )
    opens = jnp.any(starts[:, None, None] == here[None], axis=0)
    cut = jnp.where(opens, CUT, 0.0).astype(F32).reshape(count, 1)
    return same, jnp.broadcast_to(cut, (count, LANES))


def layer_forward(xin, in_conv, other, same, cut, host, collective):
    sel, stepw, small, rate, gain = other
    count = xin.shape[0]
    inner = in_conv.shape[1]
    reach = same.shape[0] - 1
    scale = lax.rsqrt(jnp.mean(xin * xin, axis=-1, keepdims=True) + EPS)
    normed = (xin * scale * gain).astype(BF16)
    conv_in = jnp.dot(normed, in_conv, preferred_element_type=F32).astype(BF16)
    last = conv_in[(count - reach * CHUNKS) :].reshape(reach, CHUNKS, inner)[:, CHUNKS - 1]
    halo = shifted(last, "seq", 1)
    act, pre, selected = select_call(conv_in, halo, same, small, sel)
    (step, sig, moments, full, keep), got = forward_scan(
        stepw, small, act, selected, cut, rate, host[0], host[1], collective
    )
    return (scale, normed, conv_in, halo, act, pre, selected, step, sig, full, keep), moments, got


def layer_output(xin, normed, full, in_gate, out_weight):
    gate = jnp.dot(normed, in_gate, preferred_element_type=F32).astype(BF16)
    wide = gate.astype(F32)
    gated = (full * (wide * jax.nn.sigmoid(wide))).astype(BF16)
    return xin + jnp.dot(gated, out_weight, preferred_element_type=F32), gate, gated


def outer_sum(left, right):
    return lax.dot_general(left, right, (((0,), (0,)), ((), ())), preferred_element_type=F32)


def times_transposed(left, right):
    return lax.dot_general(left, right, (((1,), (1,)), ((), ())), preferred_element_type=F32)


def layer_backward(grad_out, weights, same, cut, saved, moments, host, collective):
    in_conv, in_gate, out_weight, sel, stepw, small, rate, gain = weights
    (xin, scale, normed, conv_in, halo, act, pre, selected, step, sig, full, keep, gate, gated) = saved
    count, inner = act.shape
    reach = same.shape[0] - 1
    grad_low = grad_out.astype(BF16)
    dgated = times_transposed(grad_low, out_weight)
    gout = outer_sum(gated, grad_low).astype(BF16)
    wide = gate.astype(F32)
    dfull = dgated * (wide * jax.nn.sigmoid(wide))
    dgate = (dgated * full * silu_slope(wide)).astype(BF16)
    gin_gate = outer_sum(normed, dgate).astype(BF16)
    sources, tasks = host(gout, gin_gate)
    (dact, gbias, gskip, gdecay, gstepw, dsel), found = backward_scan(
        dfull, step, cut, rate, selected, act, sig, keep, small, stepw, sources, tasks, collective
    )
    dconv, tail, spill, gsel, gsmall = conv_grad(
        conv_in, halo, same, small, sel, act, pre, dact, dsel
    )
    late = (tail + shifted(spill, "seq", -1)).astype(BF16)
    grid = dconv.reshape(count // CHUNKS, CHUNKS, inner)
    dconv = grid.at[count // CHUNKS - reach :, CHUNKS - 1].set(late).reshape(count, inner)
    gin_conv = outer_sum(normed, dconv).astype(BF16)
    dnormed = times_transposed(dconv, in_conv) + times_transposed(dgate, in_gate)
    unit = xin * scale
    ggain = jnp.sum(dnormed * unit, axis=0)
    dunit = dnormed * gain
    grad_in = scale * (dunit - unit * jnp.mean(dunit * unit, axis=-1, keepdims=True)) + grad_out
    shards = lax.axis_size(("dp", "seq"))
    per = inner // shards
    ggain = jnp.pad(ggain.reshape(shards, -1), ((0, 0), (0, per - ggain.shape[0] // shards)))
    rows = jnp.concatenate(
        [gsel, gstepw, gdecay, gsmall[: reach + 2], gbias, gskip, ggain.reshape(1, inner), moments,
         jnp.zeros((6, inner), F32)], axis=0,
    )
    return grad_in, gin_conv, gin_gate, gout, rows, found


AXES = ("section", "dp", "seq")


def body(
    inputs, doc_lengths, out_grad, norm_gain, in_weight, conv_weight, conv_bias, select_weight,
    step_weight, step_bias, log_decay, skip_gain, out_weight,
):
    section = lax.axis_index("section")
    micro, _, count, model = inputs.shape
    taps, per = conv_weight.shape[1:]
    shards = lax.axis_size(("dp", "seq"))
    inner = per * shards
    rank, nstate = step_weight.shape[1], log_decay.shape[1]
    wide = rank + 2 * nstate

    kernels = lax.axis_size("dp") == 4 and per % LANES == 0 and in_weight.shape[1] % 32 == 0
    pad = per - norm_gain.shape[1]
    rows = jnp.concatenate(
        [select_weight[0].T, step_weight[0], log_decay[0], conv_weight[0], conv_bias, step_bias, skip_gain,
         jnp.pad(norm_gain, ((0, 0), (0, pad))), jnp.zeros((8, per), BF16)], axis=0,
    )
    in_half, out_half = in_weight[0], out_weight[0]
    if kernels:
        packs = gather_rows(
            [rows, rows, in_half, in_half],
            [(0, per, 0), (1, per, 0), (0, 256, 0), (0, 256, inner)], [per, per, inner, inner], 2,
        )
        packed = [g.reshape(shards, -1, per) for g in packs[:2]]
        in_conv, in_gate = [packs[2], None], [packs[3], None]
        outs_weight = lax.all_gather(out_half, AXES, axis=0, tiled=True).reshape(2, inner, model)
        hosts = [([in_half], [(1, 256, base, inner)]) for base in (0, inner)]
    else:
        packed = lax.all_gather(rows, AXES, axis=0).reshape(2, shards, -1, per)
        in_all = lax.all_gather(in_half, AXES, axis=0, tiled=True).reshape(2, model, -1)
        in_conv, in_gate = in_all[:, :, :inner], in_all[:, :, inner:]
        outs_weight = lax.all_gather(out_half, AXES, axis=0, tiled=True).reshape(2, inner, model)
        hosts = [([], []), ([], [])]
    others = []
    for layer in range(2):
        flat = packed[layer].swapaxes(0, 1).reshape(-1, inner)
        at = wide + rank + nstate
        small = flat[at : at + 16].astype(F32)
        gain = packed[layer][:, at + taps + 3, : norm_gain.shape[1]].reshape(-1).astype(F32)
        rate = -jnp.exp(flat[wide + rank : at].astype(F32)) * LOG2E
        small = jnp.concatenate([small[: taps + 3], jnp.zeros((1, inner), F32)], axis=0)
        others.append((flat[:wide], flat[wide : wide + rank], small, rate, gain))

    mine = lambda value: lax.dynamic_index_in_dim(value, section, 0, keepdims=False)[0]
    same, cut = places(mine(doc_lengths), count, taps - 1)
    state = interleave(mine(inputs).astype(F32))
    outs, kept, weights = [], [], []
    for layer in range(2):
        saved, moments, got = layer_forward(
            state, in_conv[layer], others[layer], same, cut, hosts[layer], 5 + layer
        )
        if kernels:
            (in_gate if layer else in_conv)[1] = got[0]
        result, gate, gated = layer_output(
            state, saved[1], saved[9], in_gate[layer], outs_weight[layer]
        )
        weights.append((in_conv[layer], in_gate[layer], outs_weight[layer]) + others[layer])
        kept.append(((state,) + saved + (gate, gated), moments))
        state = result
        outs.append(state)
    grad = interleave(mine(out_grad).astype(F32))
    def split(value):
        return value.reshape(shards, -1, value.shape[1])

    grads = [None] * 2
    parts, sums = [None] * 2, [{}, {}]
    for layer in (1, 0):
        if not kernels:
            host = lambda gout, gin_gate: ([], [])
        elif layer == 1:
            host = lambda gout, gin_gate: ([split(gout), split(gin_gate)], [(1, 128), (1, 256)])
        else:
            host = lambda gout, gin_gate: ([split(gout), parts[1][1]], [(0, 128), (1, 256)])
        grad, gin_conv, gin_gate, gout, pack, found = layer_backward(
            grad, weights[layer], same, cut, *kept[layer], host, 7 + layer
        )
        grads[layer] = grad
        pack = pack.reshape(-1, shards, per).swapaxes(0, 1)
        parts[layer] = [pack, split(gin_conv), split(gin_gate), split(gout)]
        if kernels and layer == 1:
            sums[1][3], sums[1][2] = found
        elif kernels:
            sums[0][3], sums[1][1] = found

    if kernels:
        sums[0][2], sums[0][1], sums[0][0], sums[1][0] = reduce_rows(
            [parts[0][2], parts[0][1], parts[0][0], parts[1][0]],
            [(0, 256), (0, 256), (0, per), (1, per)], 3,
        )
        rows, gin_conv, gin_gate, gout = (
            jnp.where(section == 0, sums[0][i], sums[1][i]) for i in range(4)
        )
    else:
        found = []
        for pair in zip(*parts):
            both = jnp.stack(pair).reshape((-1,) + pair[0].shape[1:])
            found.append(lax.psum_scatter(both, AXES, scatter_dimension=0).astype(F32))
        rows, gin_conv, gin_gate, gout = found
    gin = jnp.concatenate([gin_conv, gin_gate], axis=1)

    def place(values):
        first, second = (in_order(value) for value in values)
        own = jnp.where(section == 0, first, second)
        other = jnp.where(section == 0, second, first)
        other = lax.ppermute(other, "section", [(0, 1), (1, 0)])
        both = jnp.stack([jnp.where(section == 0, own, other), jnp.where(section == 0, other, own)])
        return both[None, :, None]

    at = wide + rank + nstate
    tokens = micro * inputs.shape[1] * lax.axis_size("dp") * count * lax.axis_size("seq")
    return (
        place(outs),
        place(grads),
        rows[at + taps + 3, : norm_gain.shape[1]][None],
        gin[None],
        rows[at : at + taps][None],
        rows[at + taps][None],
        rows[:wide].T[None],
        rows[wide : wide + rank][None],
        rows[at + taps + 1][None],
        rows[wide + rank : at][None],
        rows[at + taps + 2][None],
        gout[None],
        (rows[at + taps + 4 : at + taps + 6] / tokens)[None],
    )


def solution(mesh):
    vector = P("section", ("dp", "seq"))
    matrix = P("section", ("dp", "seq"), None)
    turned = P("section", None, ("dp", "seq"))
    tokens = P(None, "dp", "seq", None)
    in_specs = (
        tokens, P(None, "dp", None), tokens, vector, matrix, turned, vector, matrix, turned,
        vector, turned, vector, matrix,
    )
    result = P("section", None, "dp", "seq", None)
    out_specs = (
        result, result, vector, matrix, turned, vector, matrix, turned, vector, turned, vector,
        matrix, turned,
    )
    return jax.shard_map(body, mesh=mesh, in_specs=in_specs, out_specs=out_specs, check_vma=False)
```

```python
import functools
import itertools
import math

import jax
import jax.numpy as jnp
from jax import lax
from jax.experimental import pallas as pl
from jax.experimental.pallas import tpu as pltpu
from jax.sharding import PartitionSpec as P

EPS = 1e-05
LOG2E = math.log2(math.e)
LN2 = math.log(2.0)
CUT = 1e30
LANES = 128
CHUNKS = 8
VMEM_LIMIT = 66_000_000
F32 = jnp.float32
BF16 = jnp.bfloat16


def silu_slope(values):
    sigma = jax.nn.sigmoid(values)
    return sigma * (1.0 + values * (1.0 - sigma))


def interleave(rows):
    count = rows.shape[0]
    return rows.reshape(CHUNKS, count // CHUNKS, -1).swapaxes(0, 1).reshape(count, -1)


def in_order(rows):
    count = rows.shape[0]
    return rows.reshape(count // CHUNKS, CHUNKS, -1).swapaxes(0, 1).reshape(count, -1)


def column_params(**kw):
    return pltpu.CompilerParams(
        dimension_semantics=("arbitrary",), vmem_limit_bytes=VMEM_LIMIT, **kw
    )


def cols(rows, width=LANES):
    return pl.BlockSpec((rows, width), lambda j: (0, j))


def whole(*shape):
    return pl.BlockSpec(shape, lambda j: (0,) * len(shape))


def conv_taps(conv_ref, halo_ref, steps, reach):
    width = conv_ref.shape[1]
    own = conv_ref[...].astype(F32).reshape(steps, CHUNKS, width)
    tail = own[steps - reach :]
    moved = pltpu.roll(tail.reshape(reach * CHUNKS, width), 1, 0).reshape(reach, CHUNKS, width)
    first = lax.broadcasted_iota(jnp.int32, moved.shape, 1) == 0
    halo = halo_ref[...].astype(F32)[:, None, :]
    head = jnp.where(first, jnp.broadcast_to(halo, moved.shape), moved)
    return jnp.concatenate([head, own], axis=0)


def lanes_of(pack_ref, start, stop):
    return jnp.concatenate([pack_ref[i, start:stop, :] for i in range(pack_ref.shape[0])], axis=1)


def select_kernel(conv_ref, halo_ref, same_ref, pack_ref, act_ref, pre_ref, out_ref, acc):
    j = pl.program_id(0)
    count, width = conv_ref.shape
    reach = halo_ref.shape[0]
    steps = count // CHUNKS
    small_ref = lanes_of(pack_ref, pack_ref.shape[1] - 16, pack_ref.shape[1]).astype(F32)
    ext = conv_taps(conv_ref, halo_ref, steps, reach)
    pre = jnp.broadcast_to(small_ref[reach + 1 : reach + 2, :], (count, width)).reshape(
        steps, CHUNKS, width
    )
    for k in range(reach + 1):
        weight = small_ref[k : k + 1, :]
        same = same_ref[k][:, :, None]
        pre = pre + (weight[None] * ext[k : k + steps]) * same
    pre = pre.reshape(count, width)
    pre_ref[...] = pre
    act = (pre * jax.nn.sigmoid(pre)).astype(BF16)
    act_ref[...] = act

    @pl.when(j == 0)
    def _():
        acc[...] = jnp.zeros_like(acc)

    acc[...] += lax.dot_general(
        act, lanes_of(pack_ref, 0, acc.shape[1]), (((1,), (1,)), ((), ())),
        preferred_element_type=F32,
    )
    out_ref[...] = acc[...]


def pack_blocks(pack, width):
    return pl.BlockSpec((width // LANES,) + pack.shape[1:], lambda j: (j, 0, 0))


def select_call(conv_in, halo, same, pack, wide):
    count, inner = conv_in.shape
    width = min(512, inner)
    return pl.pallas_call(
        select_kernel,
        grid=(inner // width,),
        in_specs=[
            cols(count, width),
            cols(halo.shape[0], width),
            whole(*same.shape),
            pack_blocks(pack, width),
        ],
        out_specs=[cols(count, width), cols(count, width), whole(count, wide)],
        out_shape=[
            jax.ShapeDtypeStruct((count, inner), BF16),
            jax.ShapeDtypeStruct((count, inner), F32),
            jax.ShapeDtypeStruct((count, wide), F32),
        ],
        scratch_shapes=[pltpu.VMEM((count, wide), F32)],
        compiler_params=column_params(),
        name="conv_select",
    )(conv_in, halo, same, pack)


def spread(dst, src_ref, nstate, at):
    for n in range(nstate):
        dst[n] = jnp.broadcast_to(src_ref[:, at + n : at + n + 1], dst.shape[1:])


def chunk_links(ends, sums, rates, backward):
    row = lax.broadcasted_iota(jnp.int32, (CHUNKS, LANES), 0)
    gains = [jnp.exp2(sums * rate) for rate in rates]
    ends = list(ends)
    total = sums
    k = 1
    while k < CHUNKS:
        turn = CHUNKS - k if backward else k
        mask = row < CHUNKS - k if backward else row >= k
        ends = [
            jnp.where(mask, g * pltpu.roll(e, turn, 0) + e, e) for g, e in zip(gains, ends)
        ]
        gains = [jnp.where(mask, g * pltpu.roll(g, turn, 0), g) for g in gains]
        total = jnp.where(mask, pltpu.roll(total, turn, 0) + total, total)
        k *= 2
    turn = CHUNKS - 1 if backward else 1
    mask = row < CHUNKS - 1 if backward else row >= 1
    entering = [jnp.where(mask, pltpu.roll(e, turn, 0), 0.0) for e in ends]
    before = jnp.where(mask, pltpu.roll(total, turn, 0), 0.0)
    last = 0 if backward else CHUNKS - 1
    return entering, [e[last : last + 1] for e in ends], before, total[last : last + 1]


def rates_of(pack_ref, nstate):
    end = pack_ref.shape[1] - 16
    return -jnp.exp(pack_ref[0, end - nstate : end, :].astype(F32)) * LOG2E


def vector_of(pack_ref, row):
    at = pack_ref.shape[1] - 16
    return pack_ref[0, at : at + 16, :].astype(F32)[row : row + 1]


def rate_rows(rate, nstate):
    return [jnp.broadcast_to(rate[n : n + 1, :], (CHUNKS, LANES)) for n in range(nstate)]


def arriving_state(me, totals_ref, sums_ref, lanes, rate, backward):
    devices = totals_ref.shape[0]
    state = jnp.zeros(rate.shape, F32)
    order = range(devices - 1, 0, -1) if backward else range(devices - 1)
    for k in order:
        passed = jnp.exp2(rate * sums_ref[k, :, lanes]) * state
        passed = passed + totals_ref[k, :, lanes].astype(F32)
        state = jnp.where((k > me) if backward else (k < me), passed, state)
    return state


def conv_grad_kernel(
    conv_ref, halo_ref, same_ref, pack_ref, act_ref, pre_ref, dact_ref, dsel_ref,
    gbias_ref, gskip_ref, dconv_ref, tail_ref, spill_ref, gsel_ref, gsmall_ref,
):
    count, width = conv_ref.shape
    reach = halo_ref.shape[0]
    steps = count // CHUNKS
    ext = conv_taps(conv_ref, halo_ref, steps, reach)
    small_ref = lanes_of(pack_ref, pack_ref.shape[1] - 16, pack_ref.shape[1]).astype(F32)
    sel = lanes_of(pack_ref, 0, dsel_ref.shape[1])
    dsel = dsel_ref[...]
    gsel = lax.dot_general(
        dsel, act_ref[...], (((0,), (0,)), ((), ())), preferred_element_type=F32
    )
    dact = dact_ref[...] + jnp.dot(dsel, sel, preferred_element_type=F32)
    dpre = dact * silu_slope(pre_ref[...])
    vectors = [jnp.sum(dpre, axis=0, keepdims=True), gbias_ref[...], gskip_ref[...]]
    dpre = dpre.reshape(steps, CHUNKS, width)
    parts, taps = [], []
    for k in range(reach + 1):
        masked = dpre * same_ref[k][:, :, None]
        taps.append(
            jnp.sum((masked * ext[k : k + steps]).reshape(count, width), axis=0, keepdims=True)
        )
        parts.append(masked * small_ref[k : k + 1, :][None])
    vectors = jnp.concatenate(taps + vectors + [jnp.zeros((4 - reach, width), F32)], axis=0)
    for i in range(width // LANES):
        gsel_ref[i] = gsel[:, i * LANES : (i + 1) * LANES].astype(gsel_ref.dtype)
        gsmall_ref[i] = vectors[:, i * LANES : (i + 1) * LANES]
    own = parts[reach]
    for k in range(reach):
        back = reach - k
        own = own + jnp.concatenate(
            [parts[k][back:], jnp.zeros((back, CHUNKS, width), F32)], axis=0
        )
    heads = []
    for e in range(reach):
        total = parts[0][e]
        for k in range(1, e + 1):
            total = total + parts[k][e - k]
        heads.append(total)
    head = jnp.stack(heads)
    spill_ref[...] = head[:, 0, :]
    row = lax.broadcasted_iota(jnp.int32, head.shape, 1)
    moved = pltpu.roll(head.reshape(reach * CHUNKS, width), reach * CHUNKS - 1, 0)
    moved = jnp.where(row == CHUNKS - 1, 0.0, moved.reshape(head.shape))
    tail = own[steps - reach :] + moved
    tail_ref[...] = tail[:, CHUNKS - 1, :]
    dconv = jnp.concatenate([own[: steps - reach], tail], axis=0)
    dconv_ref[...] = dconv.reshape(count, width).astype(BF16)


def conv_grad(conv_in, halo, same, pack, act, pre, dact, dsel, gbias, gskip):
    count, inner = act.shape
    width = min(512, inner)
    reach = halo.shape[0]
    wide = dsel.shape[1]
    return pl.pallas_call(
        conv_grad_kernel,
        grid=(inner // width,),
        in_specs=[
            cols(count, width),
            cols(reach, width),
            whole(*same.shape),
            pack_blocks(pack, width),
            cols(count, width),
            cols(count, width),
            cols(count, width),
            whole(count, wide),
            cols(1, width),
            cols(1, width),
        ],
        out_specs=[
            cols(count, width),
            cols(reach, width),
            cols(reach, width),
            pl.BlockSpec((width // LANES, wide, LANES), lambda j: (j, 0, 0)),
            pl.BlockSpec((width // LANES, 8, LANES), lambda j: (j, 0, 0)),
        ],
        out_shape=[
            jax.ShapeDtypeStruct((count, inner), BF16),
            jax.ShapeDtypeStruct((reach, inner), F32),
            jax.ShapeDtypeStruct((reach, inner), F32),
            jax.ShapeDtypeStruct((inner // LANES, wide, LANES), BF16),
            jax.ShapeDtypeStruct((inner // LANES, 8, LANES), F32),
        ],
        compiler_params=column_params(),
        name="conv_grad",
    )(conv_in, halo, same, pack, act, pre, dact, dsel, gbias, gskip)


def shifted(value, axis, steps):
    count = lax.axis_size(axis)
    first, last = (max(0, -steps), min(count, count - steps))
    return lax.ppermute(value, axis, [(source, source + steps) for source in range(first, last)])


MESH = pl.DeviceIdType.MESH


def where_am_i():
    c, d, z = lax.axis_index("section"), lax.axis_index("dp"), lax.axis_index("seq")
    y, x = d // 2, d % 2
    flip_x, flip_y = y * 2 + (1 - x), (1 - y) * 2 + x
    return c, y, x, z, flip_x, flip_y


def peers_of(depth):
    c, y, x, z, flip_x, flip_y = where_am_i()
    peers = [{"section": 1 - c}, {"dp": flip_x}, {"dp": flip_y}]
    return peers + [{"seq": lax.rem(z + o, depth)} for o in range(1, depth)]


def hail(depth):
    barrier = pltpu.get_barrier_semaphore()
    for peer in peers_of(depth):
        pl.semaphore_signal(barrier, inc=1, device_id=peer, device_id_type=MESH)


def await_hails(depth):
    pl.semaphore_wait(pltpu.get_barrier_semaphore(), 2 + depth)


def greet(depth):
    hail(depth)
    await_hails(depth)


def pipeline(stages, count, lags):
    for turn in range(count + lags[-1]):
        for lag, stage in zip(lags, stages):
            if 0 <= turn - lag < count:
                stage(turn - lag)


class Gather:
    def __init__(self, depth, layer, width, base, src, out, mine, send, recv, local):
        self.depth, self.layer, self.width, self.base = depth, layer, width, base
        self.src, self.out, self.mine = src, out, mine
        self.send, self.recv, self.local = send, recv, local
        self.count = mine.shape[0]
        c, y, x, z, flip_x, flip_y = where_am_i()
        self.c, self.y, self.x, self.z = c, y, x, z
        self.near = {"dp": (1 - c) * flip_y + c * flip_x}
        self.far = {"dp": (1 - c) * flip_x + c * flip_y}
        self.partner = {"section": 1 - c}

    def cols(self, k, base=0):
        if isinstance(k, int):
            return pl.ds(base + k * self.width, self.width)
        return pl.ds(pl.multiple_of(base + k * self.width, LANES), self.width)

    def remote(self, k, slot, src, dst, peer):
        return pltpu.make_async_remote_copy(
            src_ref=src, dst_ref=dst, send_sem=self.send.at[k, slot], recv_sem=self.recv.at[k, slot],
            device_id=peer, device_id_type=MESH,
        )

    def piece(self, k, at):
        return self.out.at[at[0], at[1], :, self.c, :, self.cols(k)]

    def pieces(self, k, half):
        rows = self.mine.shape[1]
        if not isinstance(self.src, tuple):
            return [(0, self.src.at[pl.ds(half * rows, rows), self.cols(k, self.base)])]
        found, at = [], 0
        for ref in self.src[half]:
            found.append((at, ref))
            at += ref.shape[0]
        return found

    def hand_wait(self, k):
        return self.remote(k, 0, self.mine.at[k], self.mine.at[k], self.partner)

    def keep_wait(self, k):
        return pltpu.make_async_copy(self.mine.at[k], self.mine.at[k], self.local.at[k, 0])

    def line(self, k):
        target = self.out.at[self.y, self.x, self.z, self.c, :, self.cols(k)]
        return [
            self.remote(k, o, self.mine.at[k], target, {"seq": lax.rem(self.z + o, self.depth)})
            for o in range(1, self.depth)
        ]

    def place(self, k):
        target = self.out.at[self.y, self.x, self.z, self.c, :, self.cols(k)]
        return pltpu.make_async_copy(self.mine.at[k], target, self.local.at[k, 1])

    def move(self, k, slot, at, peer):
        return self.remote(k, self.depth + slot, self.piece(k, at), self.piece(k, at), peer)

    def near_copy(self, k):
        return self.move(k, 0, (self.y, self.x), self.near)

    def far_copy(self, k, core):
        at = (slice(None), self.x) if core == 0 else (self.y, slice(None))
        return self.move(k, 1, at, self.far)

    def cross(self, k):
        return self.move(k, 2, (slice(None), slice(None)), self.partner)

    def first(self, k):
        @pl.when(self.c == self.layer)
        def _():
            for at, ref in self.pieces(k, 1 - self.layer):
                there = self.mine.at[k, pl.ds(at, ref.shape[0])]
                self.remote(k, 0, ref, there, self.partner).start()
            for at, ref in self.pieces(k, self.layer):
                here = self.mine.at[k, pl.ds(at, ref.shape[0])]
                pltpu.make_async_copy(ref, here, self.local.at[k, 0]).start()

    def along_z(self, k):
        @pl.when(self.c == self.layer)
        def _():
            self.hand_wait(k).wait_send()
            self.keep_wait(k).wait()

        @pl.when(self.c != self.layer)
        def _():
            self.hand_wait(k).wait_recv()

        for copy in self.line(k):
            copy.start()
        self.place(k).start()

    def along_near(self, k):
        for copy in self.line(k):
            copy.wait_recv()
        self.place(k).wait()
        self.near_copy(k).start()

    def along_far(self, k):
        self.near_copy(k).wait_recv()
        for core in (0, 1):

            @pl.when(self.c == core)
            def _(core=core):
                self.far_copy(k, core).start()

    def across(self, k):
        self.far_copy(k, 0).wait_recv()
        self.cross(k).start()

    def finish(self, k):
        self.cross(k).wait()
        for copy in self.line(k) + [self.near_copy(k), self.far_copy(k, 0)]:
            copy.wait_send()

    def stages(self):
        return [self.along_z, self.along_near, self.along_far, self.across, self.finish]


def gather_scratch(specs, depth):
    scratch = []
    for rows, columns, width, dtype in specs:
        chunks = columns // width
        scratch += [
            pltpu.VMEM((chunks, rows // 2, width), dtype),
            pltpu.SemaphoreType.DMA((chunks, depth + 3)),
            pltpu.SemaphoreType.DMA((chunks, depth + 3)),
            pltpu.SemaphoreType.DMA((chunks, 2)),
        ]
    return scratch


def gather_shape(rows, columns, depth, dtype):
    return jax.ShapeDtypeStruct((2, 2, depth, 2, rows // 2, columns), dtype)


def gather_kernel(tasks, depth, refs_of, relayed, *refs):
    count = len(tasks)
    inputs = 1 + max(i for of in refs_of for i in (sum(of, ()) if isinstance(of, tuple) else (of,)))
    srcs, refs = refs[:inputs], refs[inputs:]
    relay, refs = refs[:relayed], refs[relayed:]
    outs, relays, rest = refs[:count], refs[count : count + relayed], refs[count + relayed :]
    greet(depth)
    work = []
    for i, ((layer, width, base), of) in enumerate(zip(tasks, refs_of)):
        src = tuple([srcs[n] for n in half] for half in of) if isinstance(of, tuple) else srcs[of]
        gather = Gather(depth, layer, width, base, src, outs[i], *rest[4 * i : 4 * i + 4])
        work += [(gather, k) for k in range(gather.count)]
    for gather, k in work:
        gather.first(k)
    if relayed:
        held, sem = rest[4 * count :]
        pltpu.make_async_copy(relay[0], held, sem).start()
    pipeline(
        [lambda i, s=s: work[i][0].stages()[s](work[i][1]) for s in range(5)],
        len(work), (0, 2, 4, 6, 8),
    )
    if relayed:
        pltpu.make_async_copy(relay[0], held, sem).wait()
        last = pltpu.make_async_copy(held, relays[0], sem)
        last.start()
        last.wait()


def gather_rows(sources, refs_of, tasks, shapes, relay, collective):
    depth = lax.axis_size("seq")
    anywhere = pl.BlockSpec(memory_space=pl.ANY)
    dtype = sources[0].dtype
    relay = [] if relay is None else [relay]
    outs = pl.pallas_call(
        functools.partial(gather_kernel, tasks, depth, refs_of, len(relay)),
        in_specs=[anywhere] * (len(sources) + len(relay)),
        out_specs=[anywhere] * (len(tasks) + len(relay)),
        out_shape=[gather_shape(r, w, depth, dtype) for r, w in shapes]
        + [jax.ShapeDtypeStruct(r.shape, r.dtype) for r in relay],
        scratch_shapes=gather_scratch(
            [(r, w, t[1], dtype) for (r, w), t in zip(shapes, tasks)], depth
        )
        + sum([[pltpu.VMEM(r.shape, r.dtype), pltpu.SemaphoreType.DMA] for r in relay], []),
        compiler_params=pltpu.CompilerParams(
            collective_id=collective, has_side_effects=True, vmem_limit_bytes=VMEM_LIMIT
        ),
        name="gather_rows",
    )(*sources, *relay)
    return [flat_rows(out) for out in outs[: len(tasks)]] + list(outs[len(tasks) :])


def flat_rows(out):
    return out.reshape(-1, out.shape[-1])


class Reduce:
    def __init__(self, depth, layer, width, src, out, own, core, side, edge, line, done, send, recv, local):
        self.depth, self.layer, self.width, self.src, self.out = depth, layer, width, src, out
        self.own, self.core, self.side, self.edge, self.line = own, core, side, edge, line
        self.done, self.send, self.recv, self.local = done, send, recv, local
        self.count = own.shape[0]
        self.half = own.shape[4]
        c, y, x, z, flip_x, flip_y = where_am_i()
        self.c, self.y, self.x, self.z = c, y, x, z
        self.near = {"dp": (1 - c) * flip_x + c * flip_y}
        self.far = {"dp": (1 - c) * flip_y + c * flip_x}
        self.kept = (1 - c) * y + c * x
        self.partner = {"section": 1 - c}

    def cols(self, k):
        if isinstance(k, int):
            return pl.ds(k * self.width, self.width)
        return pl.ds(pl.multiple_of(k * self.width, LANES), self.width)

    def remote(self, k, slot, src, dst, peer):
        return pltpu.make_async_remote_copy(
            src_ref=src, dst_ref=dst, send_sem=self.send.at[k, slot], recv_sem=self.recv.at[k, slot],
            device_id=peer, device_id_type=MESH,
        )

    def pieces(self, k, half):
        if not isinstance(self.src, tuple):
            rows = pl.ds(half * self.half, self.half)
            return [(0, self.half, self.src.at[:, :, :, rows, self.cols(k)])]
        found, at = [], 0
        for ref in self.src[half]:
            found.append((at, ref.shape[3], ref))
            at += ref.shape[3]
        return found

    def hand_wait(self, k):
        return self.remote(k, 0, self.core.at[k], self.core.at[k], self.partner)

    def keep_wait(self, k):
        return pltpu.make_async_copy(self.own.at[k], self.own.at[k], self.local.at[k, 0])

    def side_copy(self, k, core):
        at = (slice(None), 1 - self.x) if core == 0 else (1 - self.y, slice(None))
        return self.remote(k, 1, self.core.at[k, at[0], at[1]], self.side.at[k], self.near)

    def edges(self, k):
        return self.remote(k, 2, self.side.at[k, 1 - self.kept], self.edge.at[k], self.far)

    def lines(self, k):
        copies = []
        for o in range(1, self.depth):
            peer = lax.rem(self.z + o, self.depth)
            copies.append(
                self.remote(k, 2 + o, self.edge.at[k, peer], self.line.at[k, o - 1], {"seq": peer})
            )
        return copies

    def target(self):
        return pl.ds(self.c * self.half, self.half)

    def give(self, k):
        target = self.out.at[self.target(), self.cols(k)]
        return self.remote(k, 2 + self.depth, self.done.at[k], target, self.partner)

    def take(self, k):
        target = self.out.at[self.target(), self.cols(k)]
        return pltpu.make_async_copy(self.done.at[k], target, self.local.at[k, 1])

    def to_core(self, k):
        def begin(theirs, ours):
            for at, rows, ref in self.pieces(k, theirs):
                there = self.core.at[k, :, :, :, pl.ds(at, rows)]
                self.remote(k, 0, ref, there, self.partner).start()
            for at, rows, ref in self.pieces(k, ours):
                here = self.own.at[k, :, :, :, pl.ds(at, rows)]
                pltpu.make_async_copy(ref, here, self.local.at[k, 0]).start()

        if not isinstance(self.src, tuple):
            begin(1 - self.c, self.c)
            return
        for core in (0, 1):

            @pl.when(self.c == core)
            def _(core=core):
                begin(1 - core, core)

    def to_near(self, k):
        self.hand_wait(k).wait_recv()
        self.keep_wait(k).wait()
        for at in itertools.product(range(2), range(2), range(self.depth)):
            at = (k,) + at
            self.core[at] = self.core[at] + self.own[at]
        for core in (0, 1):

            @pl.when(self.c == core)
            def _(core=core):
                self.side_copy(k, core).start()

    def to_far(self, k):
        self.side_copy(k, 0).wait_recv()
        c = self.c
        for u in range(2):
            a, b = (1 - c) * u + c * self.y, (1 - c) * self.x + c * u
            for e in range(self.depth):
                self.side[k, u, e] = self.side[k, u, e] + self.core[k, a, b, e]
        self.edges(k).start()

    def to_line(self, k):
        self.edges(k).wait_recv()
        for e in range(self.depth):
            self.edge[k, e] = self.edge[k, e] + self.side[k, self.kept, e]
        for copy in self.lines(k):
            copy.start()

    def to_end(self, k):
        for copy in self.lines(k):
            copy.wait_recv()
        total = self.edge[k, self.z].astype(F32)
        for o in range(self.depth - 1):
            total = total + self.line[k, o].astype(F32)
        self.done[k] = total

        @pl.when(self.c == self.layer)
        def _():
            self.take(k).start()

        @pl.when(self.c != self.layer)
        def _():
            self.give(k).start()

    def finish(self, k):
        @pl.when(self.c == self.layer)
        def _():
            self.take(k).wait()
            self.give(k).wait_recv()

        @pl.when(self.c != self.layer)
        def _():
            self.give(k).wait_send()

        for copy in [self.hand_wait(k), self.side_copy(k, 0), self.edges(k)] + self.lines(k):
            copy.wait_send()

    def stages(self):
        return [self.to_core, self.to_near, self.to_far, self.to_line, self.to_end, self.finish]


def reduce_scratch(specs, depth):
    scratch = []
    for rows, columns, width, dtype in specs:
        chunks, block = columns // width, (rows // 2, width)
        scratch += [
            pltpu.VMEM((chunks, 2, 2, depth) + block, dtype),
            pltpu.VMEM((chunks, 2, 2, depth) + block, dtype),
            pltpu.VMEM((chunks, 2, depth) + block, dtype),
            pltpu.VMEM((chunks, depth) + block, dtype),
            pltpu.VMEM((chunks, depth - 1) + block, dtype),
            pltpu.VMEM((chunks,) + block, F32),
            pltpu.SemaphoreType.DMA((chunks, depth + 3)),
            pltpu.SemaphoreType.DMA((chunks, depth + 3)),
            pltpu.SemaphoreType.DMA((chunks, 2)),
        ]
    return scratch


def by_chip(value, depth):
    return value.reshape((2, 2, depth) + value.shape[1:])


def pieces_of(source):
    return list(source[0]) + list(source[1]) if isinstance(source, tuple) else [source]


def shard_of(source):
    first = pieces_of(source)[0]
    rows = sum(piece.shape[1] for piece in pieces_of(source))
    return (rows, first.shape[2])


def split_refs(refs, sources):
    found = []
    for numbers in sources:
        if numbers:
            one, two = numbers
            found.append((refs[:one], refs[one : one + two]))
            refs = refs[one + two :]
        else:
            found.append(refs[0])
            refs = refs[1:]
    return found, refs


def counts_of(sources):
    return [tuple(len(half) for half in s) if isinstance(s, tuple) else 0 for s in sources]


def reduce_kernel(tasks, numbers, depth, pairs, *refs):
    count = len(tasks)
    values, refs = refs[: 2 * pairs], refs[2 * pairs :]
    srcs, refs = split_refs(refs, numbers)
    placed, refs = refs[:pairs], refs[pairs:]
    outs, (staged, place_send, place_recv, place_local), rest = refs[:count], refs[count : count + 4], refs[count + 4 :]
    c = lax.axis_index("section")
    greet(depth)

    def stage(i, layer):
        return pltpu.make_async_copy(values[2 * i + layer], staged.at[i], place_local.at[i])

    def settle(i, layer):
        return pltpu.make_async_copy(staged.at[i], placed[i].at[layer], place_local.at[i])

    def swap(i, layer):
        return pltpu.make_async_remote_copy(
            src_ref=values[2 * i + 1 - layer], dst_ref=placed[i].at[layer],
            send_sem=place_send.at[i], recv_sem=place_recv.at[i],
            device_id={"section": 1 - c}, device_id_type=MESH,
        )

    def each_pair(act):
        for layer in (0, 1):

            @pl.when(c == layer)
            def _(layer=layer):
                for i in range(pairs):
                    act(i, layer)

    def begin(i, layer):
        swap(i, layer).start()
        stage(i, layer).start()

    def middle(i, layer):
        stage(i, layer).wait()
        settle(i, layer).start()

    def end(i, layer):
        settle(i, layer).wait()
        swap(i, layer).wait()

    each_pair(begin)
    work = []
    for i, (layer, width) in enumerate(tasks):
        item = Reduce(depth, layer, width, srcs[i], outs[i], *rest[9 * i : 9 * i + 9])
        work += [(item, k) for k in range(item.count)]
    pipeline(
        [lambda i, s=s: work[i][0].stages()[s](work[i][1]) for s in range(5)],
        len(work), (0, 1, 3, 5, 7),
    )
    each_pair(middle)
    for item, k in work:
        item.finish(k)
    each_pair(end)


def reduce_rows(values, tasks, results, collective):
    depth = lax.axis_size("seq")
    pairs = len(results) // 2
    anywhere = pl.BlockSpec(memory_space=pl.ANY)
    arrays = [by_chip(piece, depth) for value in values for piece in pieces_of(value)]
    outs = pl.pallas_call(
        functools.partial(reduce_kernel, tasks, counts_of(values), depth, pairs),
        in_specs=[anywhere] * (len(results) + len(arrays)),
        out_specs=[anywhere] * (pairs + len(values)),
        out_shape=[jax.ShapeDtypeStruct((2,) + r.shape, r.dtype) for r in results[::2]]
        + [jax.ShapeDtypeStruct(shard_of(v), F32) for v in values],
        scratch_shapes=[pltpu.VMEM((pairs,) + results[0].shape, F32)]
        + [pltpu.SemaphoreType.DMA((pairs,))] * 3
        + reduce_scratch([shard_of(v) + (t[1], BF16) for v, t in zip(values, tasks)], depth),
        compiler_params=pltpu.CompilerParams(
            collective_id=collective, has_side_effects=True, vmem_limit_bytes=VMEM_LIMIT
        ),
        name="reduce_rows",
    )(*results, *arrays)
    return outs[:pairs], outs[pairs:]


def scan_map(phases, shift=0):
    def index(p, j, last):
        if phases == 2:
            return shift + j
        if phases == 0:
            return shift + j * (1 - p) + last * p
        return shift + j * p

    return index


def spec(rows, last, phases, width=LANES):
    index = scan_map(phases)
    return pl.BlockSpec((rows, width), lambda p, j: (0, index(p, j, last)))


def fixed(*shape):
    return pl.BlockSpec(shape, lambda p, j: (0,) * len(shape))


def timetable(now, before, rate, slots, works):
    for stage, start in enumerate(slots):
        chunk, earlier = ((now - start) * rate) >> 4, ((before - start) * rate) >> 4
        base = 0
        for count, stages in works:
            local = chunk - base

            @pl.when((chunk != earlier) & (local >= 0) & (local < count))
            def _(stages=stages, local=local, stage=stage):
                stages[stage](local)

            base += count


def wind_up(now, rate, slots, works):
    steps = [(stages, k) for count, stages in works for k in range(count)]
    while any(((now - start) * rate) >> 4 < len(steps) - 1 for start in slots):
        now += 1
        for stage, start in enumerate(slots):
            k = ((now - start) * rate) >> 4
            if k != ((now - 1 - start) * rate) >> 4 and 0 <= k < len(steps):
                steps[k][0][stage](steps[k][1])
    for count, stages in works:
        lax.fori_loop(0, count, lambda k, _, s=stages[-1]: (s(k), 0)[1], 0)


def exchange(total_ref, sum_ref, totals_ref, sums_ref, send, recv):
    count = totals_ref.shape[0]
    me = lax.axis_index("seq")
    copies = []
    for o in range(1, count):
        peer = {"seq": lax.rem(me + o, count)}
        for i, (src, dst) in enumerate(((total_ref, totals_ref), (sum_ref, sums_ref))):
            copies.append(
                pltpu.make_async_remote_copy(
                    src_ref=src, dst_ref=dst.at[me], send_sem=send.at[i, o - 1],
                    recv_sem=recv.at[i, o - 1], device_id=peer, device_id_type=MESH,
                )
            )
    for copy in copies:
        copy.start()
    for copy in copies:
        copy.wait()


def forward_scan_kernel(
    tasks, numbers, depth, lead, nstate, pack_ref, act_ref, sel_ref, cut_ref, *refs
):
    hosted = len(tasks)
    srcs, refs = split_refs(refs, numbers)
    (step_ref, sig_ref, moment_ref, full_ref, keep_ref), refs = refs[:5], refs[5:]
    gouts, refs = refs[:hosted], refs[hosted:]
    (low, inb, outb, decay, drives, enter, befores, total_ref, sum_ref, totals_ref, sums_ref, send, recv), rest = refs[:13], refs[13:]
    count = act_ref.shape[0]
    rank = low.shape[1]
    wide = sel_ref.shape[1]
    p, j = pl.program_id(0), pl.program_id(1)
    blocks = pl.num_programs(1)
    turn = p * blocks + j
    me = lax.axis_index("seq")
    lanes = pl.ds(pl.multiple_of(j * LANES, LANES), LANES)
    gathers = [
        Gather(depth, layer, width, base, srcs[i], gouts[i], *rest[4 * i : 4 * i + 4])
        for i, (layer, width, base, _) in enumerate(tasks)
    ]

    @pl.when(turn == 0)
    def _():
        hail(depth)
        low[...] = sel_ref[:, :rank].astype(BF16)
        spread(inb, sel_ref, nstate, rank)
        spread(outb, sel_ref, nstate, rank + nstate)

    @pl.when(turn == 1)
    def _():
        await_hails(depth)
        for gather in gathers:
            lax.fori_loop(0, gather.count, lambda k, _, g=gather: (g.first(k), 0)[1], 0)

    works = [(gather.count, gather.stages()) for gather in gathers]
    pace, slots = 12, (2, 5, 9, 13)
    timetable(turn, turn - 1, pace, slots, works)

    @pl.when(turn == 2 * lead - 1)
    def _():
        wind_up(2 * lead - 1, pace, slots, works)

    @pl.when(p == 0)
    def _():
        stepw = pack_ref[0, wide : wide + rank, :]
        pre = jnp.dot(low[...], stepw, preferred_element_type=F32) + vector_of(pack_ref, 5)
        near = jnp.exp(-jnp.abs(pre))
        step_all = jnp.maximum(pre, 0.0) + jnp.log1p(near)
        step_ref[...] = step_all
        sig_ref[...] = jnp.where(pre >= 0.0, 1.0, near) / (1.0 + near)
        moment_ref[0:1, :] = jnp.sum(step_all, axis=0, keepdims=True)
        moment_ref[1:2, :] = jnp.sum(step_all * step_all, axis=0, keepdims=True)
        rate = rates_of(pack_ref, nstate)
        rates = rate_rows(rate, nstate)

        def body(pair, carry):
            states, sums = carry
            act = act_ref[pl.ds(pl.multiple_of(pair * 16, 16), 16), :].astype(F32)
            for half in (0, 1):
                at = pl.ds(pl.multiple_of(pair * 16 + half * 8, 8), 8)
                step = step_ref[at, :]
                away = step + cut_ref[at, :]
                drive = step * act[half * 8 : half * 8 + 8]
                drives[j, at, :] = drive
                sums = sums + away
                new = []
                for n in range(nstate):
                    gain = jnp.exp2(away * rates[n])
                    decay[j, n, at, :] = gain
                    new.append(gain * states[n] + drive * inb[n, at, :])
                states = tuple(new)
            return states, sums

        zero = jnp.zeros((CHUNKS, LANES), F32)
        ends, sums = lax.fori_loop(0, count // 16, body, ((zero,) * nstate, zero), unroll=2)
        entering, totals, before, total = chunk_links(ends, sums, rates, False)
        for n in range(nstate):
            enter[j, n] = entering[n]
        total_ref[:, lanes] = jnp.concatenate(totals, axis=0).astype(total_ref.dtype)
        befores[j] = before
        sum_ref[:, lanes] = total

    @pl.when(turn == blocks)
    def _():
        exchange(total_ref, sum_ref, totals_ref, sums_ref, send, recv)

    @pl.when(p == 1)
    def _():
        rate = rates_of(pack_ref, nstate)
        rates = rate_rows(rate, nstate)
        arrived = arriving_state(me, totals_ref, sums_ref, lanes, rate, False)
        before = befores[j]
        states = tuple(
            enter[j, n] + jnp.exp2(before * rates[n]) * arrived[n : n + 1, :] for n in range(nstate)
        )
        skip = jnp.broadcast_to(vector_of(pack_ref, 6), (CHUNKS, LANES))

        def body(pair, states):
            rows = pl.ds(pl.multiple_of(pair * 16, 16), 16)
            act = act_ref[rows, :].astype(F32)
            held = []
            for half in (0, 1):
                at = pl.ds(pl.multiple_of(pair * 16 + half * 8, 8), 8)
                held.append(states)
                drive = drives[j, at, :]
                out = skip * act[half * 8 : half * 8 + 8]
                new = []
                for n in range(nstate):
                    state = decay[j, n, at, :] * states[n] + drive * inb[n, at, :]
                    out = out + state * outb[n, at, :]
                    new.append(state)
                states = tuple(new)
                full_ref[at, :] = out
            for n in range(nstate):
                both = jnp.concatenate([held[0][n], held[1][n]], axis=0)
                keep_ref[0, n, rows, :] = both.astype(keep_ref.dtype)
            return states

        ends = lax.fori_loop(0, count // 16, body, states, unroll=2)
        for n in range(nstate):
            both = jnp.concatenate([ends[n], ends[n]], axis=0)
            keep_ref[0, n, count : count + 16, :] = both.astype(keep_ref.dtype)


def forward_scan(pack, nstate, act, selected, cut, sources, tasks, collective):
    count, inner = act.shape
    rank = selected.shape[1] - 2 * nstate
    depth = lax.axis_size("seq")
    blocks = inner // LANES
    last = blocks - 1
    arrays = [piece for source in sources for piece in pieces_of(source)]
    lengths = [sum(piece.shape[0] for piece in pieces_of(source)) for source in sources]
    anywhere = pl.BlockSpec(memory_space=pl.ANY)
    outs = pl.pallas_call(
        functools.partial(forward_scan_kernel, tasks, counts_of(sources), depth, blocks, nstate),
        grid=(2, blocks),
        in_specs=[
            pl.BlockSpec((1,) + pack.shape[1:], lambda p, j: (j, 0, 0)),
            spec(count, last, 2),
            fixed(*selected.shape),
            fixed(count, LANES),
        ]
        + [anywhere] * len(arrays),
        out_specs=[
            spec(count, last, 0),
            spec(count, last, 0),
            spec(2, last, 0),
            spec(count, last, 1),
            pl.BlockSpec((1, nstate, count + 16, LANES), lambda p, j: (j * p, 0, 0, 0)),
        ]
        + [anywhere] * len(tasks),
        out_shape=[
            jax.ShapeDtypeStruct((count, inner), F32),
            jax.ShapeDtypeStruct((count, inner), F32),
            jax.ShapeDtypeStruct((2, inner), F32),
            jax.ShapeDtypeStruct((count, inner), F32),
            jax.ShapeDtypeStruct((blocks, nstate, count + 16, LANES), BF16),
        ]
        + [gather_shape(r, t[3], depth, BF16) for r, t in zip(lengths, tasks)],
        scratch_shapes=[
            pltpu.VMEM((count, rank), BF16),
            pltpu.VMEM((nstate, count, LANES), F32),
            pltpu.VMEM((nstate, count, LANES), F32),
            pltpu.VMEM((blocks, nstate, count, LANES), F32),
            pltpu.VMEM((blocks, count, LANES), F32),
            pltpu.VMEM((blocks, nstate, CHUNKS, LANES), F32),
            pltpu.VMEM((blocks, CHUNKS, LANES), F32),
            pltpu.VMEM((nstate, inner), BF16),
            pltpu.VMEM((1, inner), F32),
            pltpu.VMEM((depth, nstate, inner), BF16),
            pltpu.VMEM((depth, 1, inner), F32),
            pltpu.SemaphoreType.DMA((2, depth - 1)),
            pltpu.SemaphoreType.DMA((2, depth - 1)),
        ]
        + gather_scratch([(r, t[3], t[1], BF16) for r, t in zip(lengths, tasks)], depth),
        compiler_params=pltpu.CompilerParams(
            dimension_semantics=("arbitrary", "arbitrary"), collective_id=collective,
            has_side_effects=True, vmem_limit_bytes=VMEM_LIMIT,
        ),
        name="forward_scan",
    )(pack, act, selected, cut, *arrays)
    return outs[:5], [flat_rows(out) for out in outs[5:]]


def backward_scan_kernel(
    tasks, numbers, depth, lead, nstate, dfull_ref, step_ref, cut_ref, pack_ref, sel_ref, act_ref, sig_ref,
    keep_ref, *refs
):
    hosted = len(tasks)
    srcs, refs = split_refs(refs, numbers)
    (dact_ref, gbias_ref, gskip_ref, gdecay_ref, gstepw_ref, dsel_ref), refs = refs[:6], refs[6:]
    gouts, refs = refs[:hosted], refs[hosted:]
    (
        low, inb, outb, decay, enter, befores, total_ref, sum_ref, totals_ref, sums_ref,
        din_acc, dout_acc, decay_acc, dlow_acc, dstep_buf, send, recv,
    ), rest = refs[:17], refs[17:]
    count = act_ref.shape[0]
    rank = low.shape[1]
    wide = sel_ref.shape[1]
    pairs = count // 16
    p, j = pl.program_id(0), pl.program_id(1)
    blocks = pl.num_programs(1)
    turn = p * blocks + j
    me = lax.axis_index("seq")
    lanes = pl.ds(pl.multiple_of(j * LANES, LANES), LANES)
    items = [
        Reduce(depth, layer, width, srcs[i], gouts[i], *rest[9 * i : 9 * i + 9])
        for i, (layer, width) in enumerate(tasks)
    ]

    @pl.when(turn == 0)
    def _():
        hail(depth)
        low[...] = sel_ref[:, :rank].astype(BF16)
        spread(inb, sel_ref, nstate, rank)
        spread(outb, sel_ref, nstate, rank + nstate)
        din_acc[...] = jnp.zeros_like(din_acc)
        dout_acc[...] = jnp.zeros_like(dout_acc)
        dlow_acc[...] = jnp.zeros_like(dlow_acc)

    @pl.when(turn == 1)
    def _():
        await_hails(depth)

    works = [(item.count, item.stages()) for item in items]
    pace, slots = 5 if len(works) > 2 else 4, (2, 4, 9, 14, 18)
    timetable(turn + p * j, turn - 1 + p * jnp.maximum(j - 1, 0), pace, slots, works)

    @pl.when(turn == 2 * lead - 1)
    def _():
        wind_up(3 * lead - 2, pace, slots, works)

    @pl.when(p == 0)
    def _():
        rate = rates_of(pack_ref, nstate)
        rates = rate_rows(rate, nstate)

        def body(step_back, carry):
            states, sums = carry
            pair = pairs - 1 - step_back
            for half in (1, 0):
                at = pl.ds(pl.multiple_of(pair * 16 + half * 8, 8), 8)
                away = step_ref[at, :] + cut_ref[at, :]
                grad = dfull_ref[at, :]
                sums = sums + away
                new = []
                for n in range(nstate):
                    gain = jnp.exp2(away * rates[n])
                    decay[j, n, at, :] = gain
                    new.append(gain * (states[n] + outb[n, at, :] * grad))
                states = tuple(new)
            return states, sums

        zero = jnp.zeros((CHUNKS, LANES), F32)
        ends, sums = lax.fori_loop(0, pairs, body, ((zero,) * nstate, zero), unroll=2)
        entering, totals, before, total = chunk_links(ends, sums, rates, True)
        for n in range(nstate):
            enter[j, n] = entering[n]
        total_ref[:, lanes] = jnp.concatenate(totals, axis=0).astype(total_ref.dtype)
        befores[j] = before
        sum_ref[:, lanes] = total

    @pl.when(turn == blocks)
    def _():
        exchange(total_ref, sum_ref, totals_ref, sums_ref, send, recv)

    @pl.when(p == 1)
    def _():
        rate = rates_of(pack_ref, nstate)
        rates = rate_rows(rate, nstate)
        arrived = arriving_state(me, totals_ref, sums_ref, lanes, rate, True)
        before = befores[j]
        states = tuple(
            enter[j, n] + jnp.exp2(before * rates[n]) * arrived[n : n + 1, :] for n in range(nstate)
        )
        skip = jnp.broadcast_to(vector_of(pack_ref, 6), (CHUNKS, LANES))
        for n in range(nstate):
            decay_acc[n] = jnp.zeros((CHUNKS, LANES), F32)
            last = keep_ref[0, n, count : count + 16, :].astype(F32)[0:CHUNKS]
            dout_acc[n, pl.ds(count, CHUNKS), :] += last * dfull_ref[pl.ds(count - CHUNKS, CHUNKS), :]

        def body(step_back, carry):
            states, gskip = carry
            pair = pairs - 1 - step_back
            rows = pl.ds(pl.multiple_of(pair * 16, 16), 16)
            act = act_ref[rows, :].astype(F32)
            held = [keep_ref[0, n, rows, :].astype(F32) for n in range(nstate)]
            sums = [None] * nstate
            for half in (1, 0):
                at = pl.ds(pl.multiple_of(pair * 16 + half * 8, 8), 8)
                step = step_ref[at, :]
                act_now = act[half * 8 : half * 8 + 8]
                drive = step * act_now
                grad = dfull_ref[at, :]
                gskip = gskip + grad * act_now
                if half:
                    earlier = dfull_ref[pl.ds(pl.multiple_of(pair * 16, 8), 8), :]
                else:
                    earlier = dfull_ref[pl.ds(pl.multiple_of(jnp.maximum(pair * 16 - 8, 0), 8), 8), :]
                by_rate = jnp.zeros((CHUNKS, LANES), F32)
                mapped = jnp.zeros((CHUNKS, LANES), F32)
                new = []
                for n in range(nstate):
                    prior = held[n][half * 8 : half * 8 + 8]
                    adjoint = states[n] + outb[n, at, :] * grad
                    passed = adjoint * decay[j, n, at, :]
                    rho = passed * prior
                    by_rate = by_rate + rho * rates[n]
                    mapped = mapped + adjoint * inb[n, at, :]
                    sums[n] = rho * step if half else sums[n] + rho * step
                    din_acc[n, at, :] += adjoint * drive
                    dout_acc[n, at, :] += prior * earlier
                    new.append(passed)
                states = tuple(new)
                dstep_buf[at, :] = by_rate * LN2 + act_now * mapped
                dact_ref[at, :] = step * mapped + skip * grad
            for n in range(nstate):
                decay_acc[n] += sums[n]
            return states, gskip

        _, gskip = lax.fori_loop(0, pairs, body, (states, jnp.zeros((CHUNKS, LANES), F32)), unroll=2)
        gskip_ref[...] = jnp.sum(gskip, axis=0, keepdims=True)
        decays = [jnp.sum(decay_acc[n], axis=0, keepdims=True) for n in range(nstate)]
        gdecay = (rate * LN2) * jnp.concatenate(decays, axis=0)
        gdecay_ref[0] = gdecay.astype(gdecay_ref.dtype)
        dpre = dstep_buf[...] * sig_ref[...]
        gbias_ref[...] = jnp.sum(dpre, axis=0, keepdims=True)
        low_dpre = dpre.astype(BF16)
        gstepw_ref[0] = lax.dot_general(
            low[...], low_dpre, (((0,), (0,)), ((), ())), preferred_element_type=F32
        ).astype(gstepw_ref.dtype)
        dlow_acc[...] += lax.dot_general(
            low_dpre, pack_ref[0, wide : wide + rank, :], (((1,), (1,)), ((), ())),
            preferred_element_type=F32,
        )

    @pl.when(turn == 2 * lead - 1)
    def _():
        column = lax.broadcasted_iota(jnp.int32, (LANES, nstate), 1)
        din = jnp.zeros((count, nstate), F32)
        dout = jnp.zeros((count, nstate), F32)
        for n in range(nstate):
            pick = (column == n).astype(BF16)
            din = din + jnp.dot(din_acc[n].astype(BF16), pick, preferred_element_type=F32)
            part = dout_acc[n, CHUNKS : count + CHUNKS, :].astype(BF16)
            dout = dout + jnp.dot(part, pick, preferred_element_type=F32)
        dsel_ref[...] = jnp.concatenate([dlow_acc[...], din, dout], axis=1).astype(BF16)


def backward_scan(
    dfull, step, cut, pack, nstate, selected, act, sig, keep, sources, tasks, collective
):
    count, inner = act.shape
    rank = selected.shape[1] - 2 * nstate
    depth = lax.axis_size("seq")
    blocks = inner // LANES
    last = blocks - 1
    arrays = [by_chip(piece, depth) for source in sources for piece in pieces_of(source)]
    anywhere = pl.BlockSpec(memory_space=pl.ANY)
    outs = pl.pallas_call(
        functools.partial(backward_scan_kernel, tasks, counts_of(sources), depth, blocks, nstate),
        grid=(2, blocks),
        in_specs=[
            spec(count, last, 2),
            spec(count, last, 2),
            fixed(count, LANES),
            pl.BlockSpec((1,) + pack.shape[1:], lambda p, j: (j, 0, 0)),
            fixed(*selected.shape),
            spec(count, last, 1),
            spec(count, last, 1),
            pl.BlockSpec((1, nstate, count + 16, LANES), lambda p, j: (j * p, 0, 0, 0)),
        ]
        + [anywhere] * len(arrays),
        out_specs=[
            spec(count, last, 1),
            spec(1, last, 1),
            spec(1, last, 1),
            pl.BlockSpec((1, nstate, LANES), lambda p, j: (j * p, 0, 0)),
            pl.BlockSpec((1, rank, LANES), lambda p, j: (j * p, 0, 0)),
            fixed(*selected.shape),
        ]
        + [anywhere] * len(tasks),
        out_shape=[
            jax.ShapeDtypeStruct((count, inner), F32),
            jax.ShapeDtypeStruct((1, inner), F32),
            jax.ShapeDtypeStruct((1, inner), F32),
            jax.ShapeDtypeStruct((blocks, nstate, LANES), BF16),
            jax.ShapeDtypeStruct((blocks, rank, LANES), BF16),
            jax.ShapeDtypeStruct(selected.shape, BF16),
        ]
        + [jax.ShapeDtypeStruct(shard_of(s), F32) for s in sources],
        scratch_shapes=[
            pltpu.VMEM((count, rank), BF16),
            pltpu.VMEM((nstate, count, LANES), F32),
            pltpu.VMEM((nstate, count, LANES), F32),
            pltpu.VMEM((blocks, nstate, count, LANES), F32),
            pltpu.VMEM((blocks, nstate, CHUNKS, LANES), F32),
            pltpu.VMEM((blocks, CHUNKS, LANES), F32),
            pltpu.VMEM((nstate, inner), BF16),
            pltpu.VMEM((1, inner), F32),
            pltpu.VMEM((depth, nstate, inner), BF16),
            pltpu.VMEM((depth, 1, inner), F32),
            pltpu.VMEM((nstate, count, LANES), F32),
            pltpu.VMEM((nstate, count + CHUNKS, LANES), F32),
            pltpu.VMEM((nstate, CHUNKS, LANES), F32),
            pltpu.VMEM((count, rank), F32),
            pltpu.VMEM((count, LANES), F32),
            pltpu.SemaphoreType.DMA((2, depth - 1)),
            pltpu.SemaphoreType.DMA((2, depth - 1)),
        ]
        + reduce_scratch([shard_of(s) + (t[1], BF16) for s, t in zip(sources, tasks)], depth),
        compiler_params=pltpu.CompilerParams(
            dimension_semantics=("arbitrary", "arbitrary"), collective_id=collective,
            has_side_effects=True, vmem_limit_bytes=VMEM_LIMIT,
        ),
        name="backward_scan",
    )(dfull, step, cut, pack, selected, act, sig, keep, *arrays)
    return outs[:6], outs[6:]


def places(lengths, count, reach):
    steps = count // CHUNKS
    base = lax.axis_index("seq") * count
    starts = jnp.cumsum(lengths) - lengths
    here = (
        base + jnp.arange(steps, dtype=jnp.int32)[:, None]
        + steps * jnp.arange(CHUNKS, dtype=jnp.int32)[None, :]
    )

    def segment(at):
        return jnp.sum((starts[:, None, None] <= at[None]).astype(jnp.int32), axis=0) - 1

    own = segment(here)
    same = jnp.stack(
        [(segment(here - reach + k) == own).astype(F32) for k in range(reach + 1)]
    )
    opens = jnp.any(starts[:, None, None] == here[None], axis=0)
    cut = jnp.where(opens, CUT, 0.0).astype(F32).reshape(count, 1)
    return same, jnp.broadcast_to(cut, (count, LANES))


def layer_forward(xin, in_conv, other, same, cut, host, collective):
    pack, gain, wide, nstate = other
    count = xin.shape[0]
    inner = in_conv.shape[1]
    reach = same.shape[0] - 1
    scale = lax.rsqrt(jnp.mean(xin * xin, axis=-1, keepdims=True) + EPS)
    normed = (xin * scale * gain).astype(BF16)
    conv_in = jnp.dot(normed, in_conv, preferred_element_type=F32).astype(BF16)
    last = conv_in[(count - reach * CHUNKS) :].reshape(reach, CHUNKS, inner)[:, CHUNKS - 1]
    halo = shifted(last, "seq", 1)
    act, pre, selected = select_call(conv_in, halo, same, pack, wide)
    (step, sig, moments, full, keep), got = forward_scan(
        pack, nstate, act, selected, cut, host[0], host[1], collective
    )
    return (scale, normed, conv_in, halo, act, pre, selected, step, sig, full, keep), moments, got


def layer_output(xin, normed, full, in_gate, out_weight):
    gate = jnp.dot(normed, in_gate, preferred_element_type=F32).astype(BF16)
    wide = gate.astype(F32)
    gated = (full * (wide * jax.nn.sigmoid(wide))).astype(BF16)
    return xin + jnp.dot(gated, out_weight, preferred_element_type=F32), gate, gated


def outer_sum(left, right):
    return lax.dot_general(left, right, (((0,), (0,)), ((), ())), preferred_element_type=F32)


def times_transposed(left, right):
    return lax.dot_general(left, right, (((1,), (1,)), ((), ())), preferred_element_type=F32)


def layer_backward(grad_out, weights, same, cut, saved, moments, host, collective):
    in_conv, in_gate, out_weight, pack, gain, _, nstate = weights
    (xin, scale, normed, conv_in, halo, act, pre, selected, step, sig, full, keep, gate, gated) = saved
    count, inner = act.shape
    reach = same.shape[0] - 1
    grad_low = grad_out.astype(BF16)
    dgated = times_transposed(grad_low, out_weight)
    gout = outer_sum(gated, grad_low).astype(BF16)
    wide = gate.astype(F32)
    dfull = dgated * (wide * jax.nn.sigmoid(wide))
    dgate = (dgated * full * silu_slope(wide)).astype(BF16)
    gin_gate = outer_sum(normed, dgate).astype(BF16)
    sources, tasks = host(gout, gin_gate)
    (dact, gbias, gskip, gdecay, gstepw, dsel), found = backward_scan(
        dfull, step, cut, pack, nstate, selected, act, sig, keep, sources, tasks, collective
    )
    dconv, tail, spill, gsel, gsmall = conv_grad(
        conv_in, halo, same, pack, act, pre, dact, dsel, gbias, gskip
    )
    late = (tail + shifted(spill, "seq", -1)).astype(BF16)
    grid = dconv.reshape(count // CHUNKS, CHUNKS, inner)
    dconv = grid.at[count // CHUNKS - reach :, CHUNKS - 1].set(late).reshape(count, inner)
    gin_conv = outer_sum(normed, dconv).astype(BF16)
    dnormed = times_transposed(dconv, in_conv) + times_transposed(dgate, in_gate)
    unit = xin * scale
    ggain = jnp.sum(dnormed * unit, axis=0)
    dunit = dnormed * gain
    grad_in = scale * (dunit - unit * jnp.mean(dunit * unit, axis=-1, keepdims=True)) + grad_out
    shards = lax.axis_size(("dp", "seq"))
    per = inner // shards
    if per < LANES:
        blocked = lambda rows: rows.swapaxes(0, 1).reshape(rows.shape[1], shards, per).swapaxes(0, 1)
        gsel, gstepw, gdecay, gsmall = (blocked(rows) for rows in (gsel, gstepw, gdecay, gsmall))
    ggain = jnp.pad(ggain.reshape(shards, 1, -1), ((0, 0), (0, 0), (0, per - ggain.shape[0] // shards)))
    moments = moments.reshape(2, shards, per).swapaxes(0, 1)
    rest = jnp.concatenate([ggain, moments, jnp.zeros((shards, 5, per), F32)], axis=1)
    rest = jnp.concatenate([gsmall, rest], axis=1).astype(BF16)
    rows = ([gsel], [gstepw, gdecay, rest])
    return grad_in, gin_conv, gin_gate, gout, rows, found


AXES = ("section", "dp", "seq")


def body(
    inputs, doc_lengths, out_grad, norm_gain, in_weight, conv_weight, conv_bias, select_weight,
    step_weight, step_bias, log_decay, skip_gain, out_weight,
):
    section = lax.axis_index("section")
    micro, _, count, model = inputs.shape
    taps, per = conv_weight.shape[1:]
    shards = lax.axis_size(("dp", "seq"))
    inner = per * shards
    rank, nstate = step_weight.shape[1], log_decay.shape[1]
    wide = rank + 2 * nstate

    kernels = lax.axis_size("dp") == 4 and per % LANES == 0 and in_weight.shape[1] % 32 == 0
    pad = per - norm_gain.shape[1]
    vectors = [conv_weight[0], conv_bias, step_bias, skip_gain, jnp.pad(norm_gain, ((0, 0), (0, pad)))]
    vectors = [v.astype(F32) for v in vectors] + [jnp.zeros((16 - taps - 4, per), F32)]
    vectors = jnp.concatenate(vectors, axis=0).astype(BF16)
    pieces = [select_weight[0].T, step_weight[0], log_decay[0], vectors]
    in_half, out_half = in_weight[0], out_weight[0]
    if kernels:
        length = sum(piece.shape[0] for piece in pieces)
        quarter = in_half.shape[:1] + (inner,)
        packs = gather_rows(
            pieces + [in_half], [((0,), (1, 2, 3)), 4, 4],
            [(0, per, 0), (0, 256, 0), (0, 256, inner)],
            [(length, per), quarter, quarter], None, 2,
        )
        packed = [packs[0].reshape(shards, -1, per), None]
        in_conv, in_gate = [packs[1], None], [packs[2], None]
        outs_weight = [None, None]
        hosts = [
            (
                [([pieces[0]], pieces[1:]), in_half, out_half],
                [(1, per, 0, per), (1, 256, 0, inner), (0, 128, 0, model)],
            ),
            ([in_half, out_half], [(1, 256, inner, inner), (1, 128, 0, model)]),
        ]
    else:
        packed = lax.all_gather(jnp.concatenate(pieces, axis=0), AXES, axis=0).reshape(2, shards, -1, per)
        in_all = lax.all_gather(in_half, AXES, axis=0, tiled=True).reshape(2, model, -1)
        in_conv, in_gate = in_all[:, :, :inner], in_all[:, :, inner:]
        outs_weight = lax.all_gather(out_half, AXES, axis=0, tiled=True).reshape(2, inner, model)
        hosts = [([], []), ([], [])]
    def other(layer):
        pack = packed[layer]
        gain = pack[:, wide + rank + nstate + taps + 3, : norm_gain.shape[1]].reshape(-1).astype(F32)
        if per < LANES:
            flat = pack.swapaxes(0, 1).reshape(-1, inner)
            pack = flat.reshape(-1, inner // LANES, LANES).swapaxes(0, 1)
        return pack, gain, wide, nstate

    mine = lambda value: lax.dynamic_index_in_dim(value, section, 0, keepdims=False)[0]
    same, cut = places(mine(doc_lengths), count, taps - 1)
    state = interleave(mine(inputs).astype(F32))
    outs, kept, weights = [], [], []
    for layer in range(2):
        saved, moments, got = layer_forward(
            state, in_conv[layer], other(layer), same, cut, hosts[layer], 5 + layer
        )
        if kernels:
            if layer == 0:
                packed[1] = got.pop(0).reshape(shards, -1, per)
            (in_gate if layer else in_conv)[1], outs_weight[layer] = got
        result, gate, gated = layer_output(
            state, saved[1], saved[9], in_gate[layer], outs_weight[layer]
        )
        weights.append((in_conv[layer], in_gate[layer], outs_weight[layer]) + other(layer))
        kept.append(((state,) + saved + (gate, gated), moments))
        state = result
        outs.append(state)
    grad = interleave(mine(out_grad).astype(F32))
    def split(value):
        return value.reshape(shards, -1, value.shape[1])

    grads = [None] * 2
    parts, sums = [None] * 2, [{}, {}]
    for layer in (1, 0):
        if not kernels:
            host = lambda gout, gin_gate: ([], [])
        elif layer == 1:
            host = lambda gout, gin_gate: ([split(gout), split(gin_gate)], [(1, 256), (1, 512)])
        else:
            host = lambda gout, gin_gate: (
                [split(gout), parts[1][1], parts[1][0]], [(0, 256), (1, 512), (1, per)]
            )
        grad, gin_conv, gin_gate, gout, pack, found = layer_backward(
            grad, weights[layer], same, cut, *kept[layer], host, 7 + layer
        )
        grads[layer] = grad
        parts[layer] = [pack, split(gin_conv), split(gin_gate), split(gout)]
        if kernels and layer == 1:
            sums[1][3], sums[1][2] = found
        elif kernels:
            sums[0][3], sums[1][1], sums[1][0] = found

    if kernels:
        mine_first = [in_order(value) for value in outs + grads]
        results, (sums[0][2], sums[0][1], sums[0][0]) = reduce_rows(
            [parts[0][2], parts[0][1], parts[0][0]], [(0, 256), (0, 256), (0, per)], mine_first, 3
        )
        rows, gin_conv, gin_gate, gout = (
            jnp.where(section == 0, sums[0][i], sums[1][i]) for i in range(4)
        )
    else:
        found = []
        for side in parts:
            side[0] = jnp.concatenate(pieces_of(side[0]), axis=1)
        for pair in zip(*parts):
            both = jnp.stack(pair).reshape((-1,) + pair[0].shape[1:])
            found.append(lax.psum_scatter(both, AXES, scatter_dimension=0).astype(F32))
        rows, gin_conv, gin_gate, gout = found
    gin = jnp.concatenate([gin_conv, gin_gate], axis=1)

    def place(values):
        first, second = (in_order(value) for value in values)
        own = jnp.where(section == 0, first, second)
        other = jnp.where(section == 0, second, first)
        other = lax.ppermute(other, "section", [(0, 1), (1, 0)])
        both = jnp.stack([jnp.where(section == 0, own, other), jnp.where(section == 0, other, own)])
        return both

    both = (1, micro, 1, count, model)
    at = wide + rank + nstate
    tokens = micro * inputs.shape[1] * lax.axis_size("dp") * count * lax.axis_size("seq")
    if not kernels:
        results = place(outs), place(grads)
    return (
        results[0].reshape(both),
        results[1].reshape(both),
        rows[at + 8, : norm_gain.shape[1]][None],
        gin[None],
        rows[at : at + taps][None],
        rows[at + taps][None],
        rows[:wide].T[None],
        rows[wide : wide + rank][None],
        rows[at + taps + 1][None],
        rows[wide + rank : at][None],
        rows[at + taps + 2][None],
        gout[None],
        (rows[at + 9 : at + 11] / tokens)[None],
    )


def solution(mesh):
    vector = P("section", ("dp", "seq"))
    matrix = P("section", ("dp", "seq"), None)
    turned = P("section", None, ("dp", "seq"))
    tokens = P(None, "dp", "seq", None)
    in_specs = (
        tokens, P(None, "dp", None), tokens, vector, matrix, turned, vector, matrix, turned,
        vector, turned, vector, matrix,
    )
    result = P("section", None, "dp", "seq", None)
    out_specs = (
        result, result, vector, matrix, turned, vector, matrix, turned, vector, turned, vector,
        matrix, turned,
    )
    return jax.shard_map(body, mesh=mesh, in_specs=in_specs, out_specs=out_specs, check_vma=False)
```

```python
import functools
import itertools
import math

import jax
import jax.numpy as jnp
from jax import lax
from jax.experimental import pallas as pl
from jax.experimental.pallas import tpu as pltpu
from jax.sharding import PartitionSpec as P

EPS = 1e-05
LOG2E = math.log2(math.e)
LN2 = math.log(2.0)
CUT = 1e30
LANES = 128
CHUNKS = 8
VMEM_LIMIT = 66_000_000
F32 = jnp.float32
BF16 = jnp.bfloat16


def silu_slope(values):
    sigma = jax.nn.sigmoid(values)
    return sigma * (1.0 + values * (1.0 - sigma))


def interleave(rows):
    count = rows.shape[0]
    return rows.reshape(CHUNKS, count // CHUNKS, -1).swapaxes(0, 1).reshape(count, -1)


def in_order(rows):
    count = rows.shape[0]
    return rows.reshape(count // CHUNKS, CHUNKS, -1).swapaxes(0, 1).reshape(count, -1)


def column_params(**kw):
    return pltpu.CompilerParams(
        dimension_semantics=("arbitrary",), vmem_limit_bytes=VMEM_LIMIT, **kw
    )


def cols(rows, width=LANES):
    return pl.BlockSpec((rows, width), lambda j: (0, j))


def whole(*shape):
    return pl.BlockSpec(shape, lambda j: (0,) * len(shape))


def conv_taps(conv_ref, halo_ref, steps, reach):
    width = conv_ref.shape[1]
    own = conv_ref[...].astype(F32).reshape(steps, CHUNKS, width)
    tail = own[steps - reach :]
    moved = pltpu.roll(tail.reshape(reach * CHUNKS, width), 1, 0).reshape(reach, CHUNKS, width)
    first = lax.broadcasted_iota(jnp.int32, moved.shape, 1) == 0
    halo = halo_ref[...].astype(F32)[:, None, :]
    head = jnp.where(first, jnp.broadcast_to(halo, moved.shape), moved)
    return jnp.concatenate([head, own], axis=0)


def mask_of(same_ref, k, width):
    mask = jnp.concatenate([same_ref[k]] * (width // LANES), axis=1)
    return mask.reshape(-1, CHUNKS, width)


def convolve(ext, small_ref, same_ref, steps, reach):
    width = ext.shape[2]
    pre = jnp.broadcast_to(small_ref[reach + 1 : reach + 2, :], (steps * CHUNKS, width))
    pre = pre.reshape(steps, CHUNKS, width)
    for k in range(reach + 1):
        term = small_ref[k : k + 1, :][None] * ext[k : k + steps]
        pre = pre + (term if k == reach else term * mask_of(same_ref, k, ext.shape[2]))
    return pre.reshape(steps * CHUNKS, width)


def lanes_of(pack_ref, start, stop):
    return jnp.concatenate([pack_ref[i, start:stop, :] for i in range(pack_ref.shape[0])], axis=1)


def select_kernel(conv_ref, halo_ref, same_ref, pack_ref, act_ref, out_ref, acc):
    j = pl.program_id(0)
    count, width = conv_ref.shape
    reach = halo_ref.shape[0]
    steps = count // CHUNKS
    small_ref = lanes_of(pack_ref, pack_ref.shape[1] - 16, pack_ref.shape[1]).astype(F32)
    ext = conv_taps(conv_ref, halo_ref, steps, reach)
    pre = convolve(ext, small_ref, same_ref, steps, reach)
    act = (pre * jax.nn.sigmoid(pre)).astype(BF16)
    act_ref[...] = act

    @pl.when(j == 0)
    def _():
        acc[...] = jnp.zeros_like(acc)

    acc[...] += lax.dot_general(
        act, lanes_of(pack_ref, 0, acc.shape[1]), (((1,), (1,)), ((), ())),
        preferred_element_type=F32,
    )
    out_ref[...] = acc[...]


def pack_blocks(pack, width):
    return pl.BlockSpec((width // LANES,) + pack.shape[1:], lambda j: (j, 0, 0))


def select_call(conv_in, halo, same, pack, wide):
    count, inner = conv_in.shape
    width = min(512, inner)
    return pl.pallas_call(
        select_kernel,
        grid=(inner // width,),
        in_specs=[
            cols(count, width),
            cols(halo.shape[0], width),
            whole(*same.shape),
            pack_blocks(pack, width),
        ],
        out_specs=[cols(count, width), whole(count, wide)],
        out_shape=[
            jax.ShapeDtypeStruct((count, inner), BF16),
            jax.ShapeDtypeStruct((count, wide), F32),
        ],
        scratch_shapes=[pltpu.VMEM((count, wide), F32)],
        compiler_params=column_params(),
        name="conv_select",
    )(conv_in, halo, same, pack)


def spread(dst, src_ref, nstate, at):
    for n in range(nstate):
        dst[n] = jnp.broadcast_to(src_ref[:, at + n : at + n + 1], dst.shape[1:])


def chunk_links(ends, sums, rates, backward):
    row = lax.broadcasted_iota(jnp.int32, (CHUNKS, LANES), 0)
    gains = [jnp.exp2(sums * rate) for rate in rates]
    ends = list(ends)
    total = sums
    k = 1
    while k < CHUNKS:
        turn = CHUNKS - k if backward else k
        mask = row < CHUNKS - k if backward else row >= k
        ends = [
            jnp.where(mask, g * pltpu.roll(e, turn, 0) + e, e) for g, e in zip(gains, ends)
        ]
        gains = [jnp.where(mask, g * pltpu.roll(g, turn, 0), g) for g in gains]
        total = jnp.where(mask, pltpu.roll(total, turn, 0) + total, total)
        k *= 2
    turn = CHUNKS - 1 if backward else 1
    mask = row < CHUNKS - 1 if backward else row >= 1
    entering = [jnp.where(mask, pltpu.roll(e, turn, 0), 0.0) for e in ends]
    before = jnp.where(mask, pltpu.roll(total, turn, 0), 0.0)
    last = 0 if backward else CHUNKS - 1
    return entering, [e[last : last + 1] for e in ends], before, total[last : last + 1]


def rates_of(pack_ref, nstate):
    end = pack_ref.shape[1] - 16
    return -jnp.exp(pack_ref[0, end - nstate : end, :].astype(F32)) * LOG2E


def vector_of(pack_ref, row):
    at = pack_ref.shape[1] - 16
    return pack_ref[0, at : at + 16, :].astype(F32)[row : row + 1]


def rate_rows(rate, nstate):
    return [jnp.broadcast_to(rate[n : n + 1, :], (CHUNKS, LANES)) for n in range(nstate)]


def arriving_state(me, totals_ref, sums_ref, lanes, rate, backward):
    devices = totals_ref.shape[0]
    state = jnp.zeros(rate.shape, F32)
    order = range(devices - 1, 0, -1) if backward else range(devices - 1)
    for k in order:
        passed = jnp.exp2(rate * sums_ref[k, :, lanes]) * state
        passed = passed + totals_ref[k, :, lanes].astype(F32)
        state = jnp.where((k > me) if backward else (k < me), passed, state)
    return state


def conv_grad_kernel(
    conv_ref, halo_ref, same_ref, pack_ref, act_ref, dact_ref, dsel_ref,
    gbias_ref, gskip_ref, dconv_ref, tail_ref, spill_ref, gsel_ref, gsmall_ref,
):
    count, width = conv_ref.shape
    reach = halo_ref.shape[0]
    steps = count // CHUNKS
    ext = conv_taps(conv_ref, halo_ref, steps, reach)
    small_ref = lanes_of(pack_ref, pack_ref.shape[1] - 16, pack_ref.shape[1]).astype(F32)
    sel = lanes_of(pack_ref, 0, dsel_ref.shape[1])
    dsel = dsel_ref[...]
    gsel = lax.dot_general(
        dsel, act_ref[...], (((0,), (0,)), ((), ())), preferred_element_type=F32
    )
    dact = dact_ref[...] + jnp.dot(dsel, sel, preferred_element_type=F32)
    dpre = dact * silu_slope(convolve(ext, small_ref, same_ref, steps, reach))
    vectors = [jnp.sum(dpre, axis=0, keepdims=True), gbias_ref[...], gskip_ref[...]]
    dpre = dpre.reshape(steps, CHUNKS, width)
    parts, taps = [], []
    for k in range(reach + 1):
        masked = dpre if k == reach else dpre * mask_of(same_ref, k, width)
        taps.append(
            jnp.sum((masked * ext[k : k + steps]).reshape(count, width), axis=0, keepdims=True)
        )
        parts.append(masked * small_ref[k : k + 1, :][None])
    vectors = jnp.concatenate(taps + vectors + [jnp.zeros((4 - reach, width), F32)], axis=0)
    for i in range(width // LANES):
        gsel_ref[i] = gsel[:, i * LANES : (i + 1) * LANES].astype(gsel_ref.dtype)
        gsmall_ref[i] = vectors[:, i * LANES : (i + 1) * LANES]
    own = parts[reach]
    for k in range(reach):
        back = reach - k
        own = own + jnp.concatenate(
            [parts[k][back:], jnp.zeros((back, CHUNKS, width), F32)], axis=0
        )
    heads = []
    for e in range(reach):
        total = parts[0][e]
        for k in range(1, e + 1):
            total = total + parts[k][e - k]
        heads.append(total)
    head = jnp.stack(heads)
    spill_ref[...] = head[:, 0, :]
    row = lax.broadcasted_iota(jnp.int32, head.shape, 1)
    moved = pltpu.roll(head.reshape(reach * CHUNKS, width), reach * CHUNKS - 1, 0)
    moved = jnp.where(row == CHUNKS - 1, 0.0, moved.reshape(head.shape))
    tail = own[steps - reach :] + moved
    tail_ref[...] = tail[:, CHUNKS - 1, :]
    dconv = jnp.concatenate([own[: steps - reach], tail], axis=0)
    dconv_ref[...] = dconv.reshape(count, width).astype(BF16)


def conv_grad(conv_in, halo, same, pack, act, dact, dsel, gbias, gskip):
    count, inner = act.shape
    width = min(512, inner)
    reach = halo.shape[0]
    wide = dsel.shape[1]
    return pl.pallas_call(
        conv_grad_kernel,
        grid=(inner // width,),
        in_specs=[
            cols(count, width),
            cols(reach, width),
            whole(*same.shape),
            pack_blocks(pack, width),
            cols(count, width),
            cols(count, width),
            whole(count, wide),
            cols(1, width),
            cols(1, width),
        ],
        out_specs=[
            cols(count, width),
            cols(reach, width),
            cols(reach, width),
            pl.BlockSpec((width // LANES, wide, LANES), lambda j: (j, 0, 0)),
            pl.BlockSpec((width // LANES, 8, LANES), lambda j: (j, 0, 0)),
        ],
        out_shape=[
            jax.ShapeDtypeStruct((count, inner), BF16),
            jax.ShapeDtypeStruct((reach, inner), F32),
            jax.ShapeDtypeStruct((reach, inner), F32),
            jax.ShapeDtypeStruct((inner // LANES, wide, LANES), BF16),
            jax.ShapeDtypeStruct((inner // LANES, 8, LANES), F32),
        ],
        compiler_params=column_params(),
        name="conv_grad",
    )(conv_in, halo, same, pack, act, dact, dsel, gbias, gskip)


def shifted(value, axis, steps):
    count = lax.axis_size(axis)
    first, last = (max(0, -steps), min(count, count - steps))
    return lax.ppermute(value, axis, [(source, source + steps) for source in range(first, last)])


MESH = pl.DeviceIdType.MESH


def where_am_i():
    c, d, z = lax.axis_index("section"), lax.axis_index("dp"), lax.axis_index("seq")
    y, x = d // 2, d % 2
    flip_x, flip_y = y * 2 + (1 - x), (1 - y) * 2 + x
    return c, y, x, z, flip_x, flip_y


def peers_of(depth):
    c, y, x, z, flip_x, flip_y = where_am_i()
    peers = [{"section": 1 - c}, {"dp": flip_x}, {"dp": flip_y}]
    return peers + [{"seq": lax.rem(z + o, depth)} for o in range(1, depth)]


def hail(depth):
    barrier = pltpu.get_barrier_semaphore()
    for peer in peers_of(depth):
        pl.semaphore_signal(barrier, inc=1, device_id=peer, device_id_type=MESH)


def await_hails(depth):
    pl.semaphore_wait(pltpu.get_barrier_semaphore(), 2 + depth)


def greet(depth):
    hail(depth)
    await_hails(depth)


def pipeline(stages, count, lags, extras={}):
    for turn in range(count + lags[-1]):
        for lag, stage in zip(lags, stages):
            if 0 <= turn - lag < count:
                stage(turn - lag)
        if turn in extras:
            extras[turn]()


class Gather:
    def __init__(self, depth, layer, width, base, src, out, mine, send, recv, local):
        self.depth, self.layer, self.width, self.base = depth, layer, width, base
        self.src, self.out, self.mine = src, out, mine
        self.send, self.recv, self.local = send, recv, local
        self.count = mine.shape[0]
        c, y, x, z, flip_x, flip_y = where_am_i()
        self.c, self.y, self.x, self.z = c, y, x, z
        self.near = {"dp": (1 - c) * flip_y + c * flip_x}
        self.far = {"dp": (1 - c) * flip_x + c * flip_y}
        self.partner = {"section": 1 - c}

    def cols(self, k, base=0):
        if isinstance(k, int):
            return pl.ds(base + k * self.width, self.width)
        return pl.ds(pl.multiple_of(base + k * self.width, LANES), self.width)

    def remote(self, k, slot, src, dst, peer):
        return pltpu.make_async_remote_copy(
            src_ref=src, dst_ref=dst, send_sem=self.send.at[k, slot], recv_sem=self.recv.at[k, slot],
            device_id=peer, device_id_type=MESH,
        )

    def piece(self, k, at):
        return self.out.at[at[0], at[1], :, self.c, :, self.cols(k)]

    def pieces(self, k, half):
        rows = self.mine.shape[1]
        if not isinstance(self.src, tuple):
            return [(0, self.src.at[pl.ds(half * rows, rows), self.cols(k, self.base)])]
        found, at = [], 0
        for ref in self.src[half]:
            found.append((at, ref))
            at += ref.shape[0]
        return found

    def hand_wait(self, k):
        return self.remote(k, 0, self.mine.at[k], self.mine.at[k], self.partner)

    def keep_wait(self, k):
        return pltpu.make_async_copy(self.mine.at[k], self.mine.at[k], self.local.at[k, 0])

    def line(self, k):
        target = self.out.at[self.y, self.x, self.z, self.c, :, self.cols(k)]
        return [
            self.remote(k, o, self.mine.at[k], target, {"seq": lax.rem(self.z + o, self.depth)})
            for o in range(1, self.depth)
        ]

    def place(self, k):
        target = self.out.at[self.y, self.x, self.z, self.c, :, self.cols(k)]
        return pltpu.make_async_copy(self.mine.at[k], target, self.local.at[k, 1])

    def move(self, k, slot, at, peer):
        return self.remote(k, self.depth + slot, self.piece(k, at), self.piece(k, at), peer)

    def near_copy(self, k):
        return self.move(k, 0, (self.y, self.x), self.near)

    def far_copy(self, k, core):
        at = (slice(None), self.x) if core == 0 else (self.y, slice(None))
        return self.move(k, 1, at, self.far)

    def cross(self, k):
        return self.move(k, 2, (slice(None), slice(None)), self.partner)

    def first(self, k):
        @pl.when(self.c == self.layer)
        def _():
            for at, ref in self.pieces(k, 1 - self.layer):
                there = self.mine.at[k, pl.ds(at, ref.shape[0])]
                self.remote(k, 0, ref, there, self.partner).start()
            for at, ref in self.pieces(k, self.layer):
                here = self.mine.at[k, pl.ds(at, ref.shape[0])]
                pltpu.make_async_copy(ref, here, self.local.at[k, 0]).start()

    def along_z(self, k):
        @pl.when(self.c == self.layer)
        def _():
            self.hand_wait(k).wait_send()
            self.keep_wait(k).wait()

        @pl.when(self.c != self.layer)
        def _():
            self.hand_wait(k).wait_recv()

        for copy in self.line(k):
            copy.start()
        self.place(k).start()

    def along_near(self, k):
        for copy in self.line(k):
            copy.wait_recv()
        self.place(k).wait()
        self.near_copy(k).start()

    def along_far(self, k):
        self.near_copy(k).wait_recv()
        for core in (0, 1):

            @pl.when(self.c == core)
            def _(core=core):
                self.far_copy(k, core).start()

    def across(self, k):
        self.far_copy(k, 0).wait_recv()
        self.cross(k).start()

    def finish(self, k):
        self.cross(k).wait()
        for copy in self.line(k) + [self.near_copy(k), self.far_copy(k, 0)]:
            copy.wait_send()

    def stages(self):
        return [self.along_z, self.along_near, self.along_far, self.across, self.finish]


def gather_scratch(specs, depth):
    scratch = []
    for rows, columns, width, dtype in specs:
        chunks = columns // width
        scratch += [
            pltpu.VMEM((chunks, rows // 2, width), dtype),
            pltpu.SemaphoreType.DMA((chunks, depth + 3)),
            pltpu.SemaphoreType.DMA((chunks, depth + 3)),
            pltpu.SemaphoreType.DMA((chunks, 2)),
        ]
    return scratch


def gather_shape(rows, columns, depth, dtype):
    return jax.ShapeDtypeStruct((2, 2, depth, 2, rows // 2, columns), dtype)


def gather_kernel(tasks, depth, refs_of, relayed, *refs):
    count = len(tasks)
    inputs = 1 + max(i for of in refs_of for i in (sum(of, ()) if isinstance(of, tuple) else (of,)))
    srcs, refs = refs[:inputs], refs[inputs:]
    relay, refs = refs[:relayed], refs[relayed:]
    outs, relays, rest = refs[:count], refs[count : count + relayed], refs[count + relayed :]
    greet(depth)
    work = []
    for i, ((layer, width, base), of) in enumerate(zip(tasks, refs_of)):
        src = tuple([srcs[n] for n in half] for half in of) if isinstance(of, tuple) else srcs[of]
        gather = Gather(depth, layer, width, base, src, outs[i], *rest[4 * i : 4 * i + 4])
        work += [(gather, k) for k in range(gather.count)]
    for gather, k in work:
        gather.first(k)
    if relayed:
        held, sem = rest[4 * count :]
        pltpu.make_async_copy(relay[0], held, sem).start()
    pipeline(
        [lambda i, s=s: work[i][0].stages()[s](work[i][1]) for s in range(5)],
        len(work), (0, 2, 4, 6, 8),
    )
    if relayed:
        pltpu.make_async_copy(relay[0], held, sem).wait()
        last = pltpu.make_async_copy(held, relays[0], sem)
        last.start()
        last.wait()


def gather_rows(sources, refs_of, tasks, shapes, relay, collective):
    depth = lax.axis_size("seq")
    anywhere = pl.BlockSpec(memory_space=pl.ANY)
    dtype = sources[0].dtype
    relay = [] if relay is None else [relay]
    outs = pl.pallas_call(
        functools.partial(gather_kernel, tasks, depth, refs_of, len(relay)),
        in_specs=[anywhere] * (len(sources) + len(relay)),
        out_specs=[anywhere] * (len(tasks) + len(relay)),
        out_shape=[gather_shape(r, w, depth, dtype) for r, w in shapes]
        + [jax.ShapeDtypeStruct(r.shape, r.dtype) for r in relay],
        scratch_shapes=gather_scratch(
            [(r, w, t[1], dtype) for (r, w), t in zip(shapes, tasks)], depth
        )
        + sum([[pltpu.VMEM(r.shape, r.dtype), pltpu.SemaphoreType.DMA] for r in relay], []),
        compiler_params=pltpu.CompilerParams(
            collective_id=collective, has_side_effects=True, vmem_limit_bytes=VMEM_LIMIT
        ),
        name="gather_rows",
    )(*sources, *relay)
    return [flat_rows(out) for out in outs[: len(tasks)]] + list(outs[len(tasks) :])


def flat_rows(out):
    return out.reshape(-1, out.shape[-1])


class Reduce:
    def __init__(self, depth, layer, width, base, src, out, own, core, side, edge, line, done, send, recv, local):
        self.depth, self.layer, self.width, self.src, self.out = depth, layer, width, src, out
        self.base = base
        self.own, self.core, self.side, self.edge, self.line = own, core, side, edge, line
        self.done, self.send, self.recv, self.local = done, send, recv, local
        self.count, self.held = core.shape[0], own.shape[0]
        self.half = own.shape[4]
        c, y, x, z, flip_x, flip_y = where_am_i()
        self.c, self.y, self.x, self.z = c, y, x, z
        self.near = {"dp": (1 - c) * flip_x + c * flip_y}
        self.far = {"dp": (1 - c) * flip_y + c * flip_x}
        self.kept = (1 - c) * y + c * x
        self.partner = {"section": 1 - c}

    def cols(self, k, base=0):
        if isinstance(k, int):
            return pl.ds(base + k * self.width, self.width)
        return pl.ds(pl.multiple_of(base + k * self.width, LANES), self.width)

    def remote(self, k, slot, src, dst, peer):
        return pltpu.make_async_remote_copy(
            src_ref=src, dst_ref=dst, send_sem=self.send.at[k, slot], recv_sem=self.recv.at[k, slot],
            device_id=peer, device_id_type=MESH,
        )

    def pieces(self, k, half):
        if not isinstance(self.src, tuple):
            rows = pl.ds(half * self.half, self.half)
            return [(0, self.half, self.src.at[:, :, :, rows, self.cols(k)])]
        found, at = [], 0
        for ref in self.src[half]:
            found.append((at, ref.shape[3], ref))
            at += ref.shape[3]
        return found

    def hand_wait(self, k):
        return self.remote(k, 0, self.core.at[k], self.core.at[k], self.partner)

    def slot(self, k):
        return k % self.held if isinstance(k, int) else k & (self.held - 1)

    def keep_wait(self, k):
        own = self.own.at[self.slot(k)]
        return pltpu.make_async_copy(own, own, self.local.at[k, 0])

    def side_copy(self, k, core):
        at = (slice(None), 1 - self.x) if core == 0 else (1 - self.y, slice(None))
        return self.remote(k, 1, self.core.at[k, at[0], at[1]], self.side.at[k], self.near)

    def edges(self, k):
        return self.remote(k, 2, self.side.at[k, 1 - self.kept], self.edge.at[k], self.far)

    def lines(self, k):
        copies = []
        for o in range(1, self.depth):
            peer = lax.rem(self.z + o, self.depth)
            copies.append(
                self.remote(k, 2 + o, self.edge.at[k, peer], self.line.at[k, o - 1], {"seq": peer})
            )
        return copies

    def target(self):
        return pl.ds(self.c * self.half, self.half)

    def give(self, k):
        target = self.out.at[self.target(), self.cols(k, self.base)]
        return self.remote(k, 2 + self.depth, self.done.at[k], target, self.partner)

    def take(self, k):
        target = self.out.at[self.target(), self.cols(k, self.base)]
        return pltpu.make_async_copy(self.done.at[k], target, self.local.at[k, 1])

    def to_core(self, k):
        def begin(theirs, ours):
            for at, rows, ref in self.pieces(k, theirs):
                there = self.core.at[k, :, :, :, pl.ds(at, rows)]
                self.remote(k, 0, ref, there, self.partner).start()
            for at, rows, ref in self.pieces(k, ours):
                here = self.own.at[self.slot(k), :, :, :, pl.ds(at, rows)]
                pltpu.make_async_copy(ref, here, self.local.at[k, 0]).start()

        if not isinstance(self.src, tuple):
            begin(1 - self.c, self.c)
            return
        for core in (0, 1):

            @pl.when(self.c == core)
            def _(core=core):
                begin(1 - core, core)

    def to_near(self, k):
        self.hand_wait(k).wait_recv()
        self.keep_wait(k).wait()
        slot = self.slot(k)
        for at in itertools.product(range(2), range(2), range(self.depth)):
            self.core[(k,) + at] = self.core[(k,) + at] + self.own[(slot,) + at]
        for core in (0, 1):

            @pl.when(self.c == core)
            def _(core=core):
                self.side_copy(k, core).start()

    def to_far(self, k):
        self.side_copy(k, 0).wait_recv()
        c = self.c
        for u in range(2):
            a, b = (1 - c) * u + c * self.y, (1 - c) * self.x + c * u
            for e in range(self.depth):
                self.side[k, u, e] = self.side[k, u, e] + self.core[k, a, b, e]
        self.edges(k).start()

    def to_line(self, k):
        self.edges(k).wait_recv()
        for e in range(self.depth):
            self.edge[k, e] = self.edge[k, e] + self.side[k, self.kept, e]
        for copy in self.lines(k):
            copy.start()

    def to_end(self, k):
        for copy in self.lines(k):
            copy.wait_recv()
        total = self.edge[k, self.z].astype(F32)
        for o in range(self.depth - 1):
            total = total + self.line[k, o].astype(F32)
        self.done[k] = total

        @pl.when(self.c == self.layer)
        def _():
            self.take(k).start()

        @pl.when(self.c != self.layer)
        def _():
            self.give(k).start()

    def finish(self, k):
        @pl.when(self.c == self.layer)
        def _():
            self.take(k).wait()
            self.give(k).wait_recv()

        @pl.when(self.c != self.layer)
        def _():
            self.give(k).wait_send()

        for copy in [self.hand_wait(k), self.side_copy(k, 0), self.edges(k)] + self.lines(k):
            copy.wait_send()

    def stages(self):
        return [self.to_core, self.to_near, self.to_far, self.to_line, self.to_end, self.finish]


def reduce_scratch(specs, depth):
    scratch = []
    for rows, columns, width, dtype in specs:
        chunks, block = columns // width, (rows // 2, width)
        scratch += [
            pltpu.VMEM((min(chunks, 2), 2, 2, depth) + block, dtype),
            pltpu.VMEM((chunks, 2, 2, depth) + block, dtype),
            pltpu.VMEM((chunks, 2, depth) + block, dtype),
            pltpu.VMEM((chunks, depth) + block, dtype),
            pltpu.VMEM((chunks, depth - 1) + block, dtype),
            pltpu.VMEM((chunks,) + block, F32),
            pltpu.SemaphoreType.DMA((chunks, depth + 3)),
            pltpu.SemaphoreType.DMA((chunks, depth + 3)),
            pltpu.SemaphoreType.DMA((chunks, 2)),
        ]
    return scratch


def by_chip(value, depth):
    return value.reshape((2, 2, depth) + value.shape[1:])


def pieces_of(source):
    return list(source[0]) + list(source[1]) if isinstance(source, tuple) else [source]


def shard_of(source):
    first = pieces_of(source)[0]
    rows = sum(piece.shape[1] for piece in pieces_of(source))
    return (rows, first.shape[2])


def split_refs(refs, sources):
    found = []
    for numbers in sources:
        if numbers:
            one, two = numbers
            found.append((refs[:one], refs[one : one + two]))
            refs = refs[one + two :]
        else:
            found.append(refs[0])
            refs = refs[1:]
    return found, refs


def counts_of(sources):
    return [tuple(len(half) for half in s) if isinstance(s, tuple) else 0 for s in sources]


def reduce_kernel(tasks, numbers, homes, olds, depth, pairs, *refs):
    values, refs = refs[: 2 * pairs], refs[2 * pairs :]
    srcs, refs = split_refs(refs, numbers)
    refs = refs[olds:]
    placed, refs = refs[:pairs], refs[pairs:]
    outs, (loaded, ordered, load, swap_send, swap_recv, settle), rest = (
        refs[:homes], refs[homes : homes + 6], refs[homes + 6 :],
    )
    c = lax.axis_index("section")
    greet(depth)
    loads = [pltpu.make_async_copy(v, loaded.at[i], load.at[i]) for i, v in enumerate(values)]

    def local(i, src, dst):
        return pltpu.make_async_copy(src, dst, settle.at[i])

    def remote(i, src, dst):
        return pltpu.make_async_remote_copy(
            src_ref=src, dst_ref=dst, send_sem=swap_send.at[i], recv_sem=swap_recv.at[i],
            device_id={"section": 1 - c}, device_id_type=MESH,
        )

    def begin_moves(i, layer):
        for b in range(ordered.shape[1]):
            target = placed[i].at[layer, :, pl.ds(b * LANES, LANES)]
            local(i, ordered.at[2 * i + layer, b], target).start()
            remote(i, ordered.at[2 * i + 1 - layer, b], target).start()

    def end_moves(i, layer):
        local(i, ordered.at[2 * i + layer], ordered.at[2 * i + layer]).wait()
        remote(i, ordered.at[2 * i + 1 - layer], ordered.at[2 * i + 1 - layer]).wait()

    def each_pair(act):
        for layer in (0, 1):

            @pl.when(c == layer)
            def _(layer=layer):
                for i in range(pairs):
                    act(i, layer)

    def put_in_order():
        steps = loaded.shape[1] // CHUNKS
        for copy in loads:
            copy.wait()

        def step(i, _):
            for n in range(2 * pairs):
                rows = loaded[n, pl.ds(pl.multiple_of(i * CHUNKS, CHUNKS), CHUNKS), :]
                for b in range(ordered.shape[1]):
                    columns = rows[:, b * LANES : (b + 1) * LANES]
                    ordered[n, b, pl.ds(i, CHUNKS, stride=steps), :] = columns
            return 0

        lax.fori_loop(0, steps, step, 0)
        each_pair(begin_moves)

    work = []
    for i, (layer, width, home, base) in enumerate(tasks):
        item = Reduce(depth, layer, width, base, srcs[i], outs[home], *rest[9 * i : 9 * i + 9])
        work += [(item, k) for k in range(item.count)]
    for copy in loads:
        copy.start()
    pipeline(
        [lambda i, s=s: work[i][0].stages()[s](work[i][1]) for s in range(5)],
        len(work), (0, 1, 3, 5, 7), {6: put_in_order},
    )
    for item, k in work:
        item.finish(k)
    each_pair(end_moves)


def reduce_rows(values, tasks, homes, results, collective):
    depth = lax.axis_size("seq")
    pairs = len(results) // 2
    anywhere = pl.BlockSpec(memory_space=pl.ANY)
    arrays = [by_chip(piece, depth) for value in values for piece in pieces_of(value)]
    first = len(results) + len(arrays)
    olds = {i: home for i, home in enumerate(homes) if not isinstance(home, tuple)}
    count, model = results[0].shape
    blocks = (model // LANES, count, LANES)
    outs = pl.pallas_call(
        functools.partial(
            reduce_kernel, tasks, counts_of(values), len(homes), len(olds), depth, pairs
        ),
        in_specs=[anywhere] * (first + len(olds)),
        out_specs=[anywhere] * (pairs + len(homes)),
        out_shape=[jax.ShapeDtypeStruct((2, count, model), F32)] * pairs
        + [jax.ShapeDtypeStruct(home if isinstance(home, tuple) else home.shape, F32) for home in homes],
        scratch_shapes=[
            pltpu.VMEM((2 * pairs,) + results[0].shape, F32),
            pltpu.VMEM((2 * pairs,) + blocks, F32),
        ]
        + [pltpu.SemaphoreType.DMA((2 * pairs,))]
        + [pltpu.SemaphoreType.DMA((pairs,))] * 3
        + reduce_scratch([shard_of(v) + (t[1], BF16) for v, t in zip(values, tasks)], depth),
        input_output_aliases={first + n: pairs + i for n, i in enumerate(olds)},
        compiler_params=pltpu.CompilerParams(
            collective_id=collective, has_side_effects=True, vmem_limit_bytes=VMEM_LIMIT
        ),
        name="reduce_rows",
    )(*results, *arrays, *olds.values())
    return outs[:pairs], outs[pairs:]


def scan_map(phases, shift=0):
    def index(p, j, last):
        if phases == 2:
            return shift + j
        if phases == 0:
            return shift + j * (1 - p) + last * p
        return shift + j * p

    return index


def spec(rows, last, phases, width=LANES):
    index = scan_map(phases)
    return pl.BlockSpec((rows, width), lambda p, j: (0, index(p, j, last)))


def fixed(*shape):
    return pl.BlockSpec(shape, lambda p, j: (0,) * len(shape))


def timetable(now, before, rate, slots, works):
    for stage, start in enumerate(slots):
        chunk, earlier = ((now - start) * rate) >> 4, ((before - start) * rate) >> 4
        base = 0
        for count, stages in works:
            local = chunk - base

            @pl.when((chunk != earlier) & (local >= 0) & (local < count))
            def _(stages=stages, local=local, stage=stage):
                stages[stage](local)

            base += count


def wind_up(now, rate, slots, works):
    steps = [(stages, k) for count, stages in works for k in range(count)]
    while any(((now - start) * rate) >> 4 < len(steps) - 1 for start in slots):
        now += 1
        for stage, start in enumerate(slots):
            k = ((now - start) * rate) >> 4
            if k != ((now - 1 - start) * rate) >> 4 and 0 <= k < len(steps):
                steps[k][0][stage](steps[k][1])
    for count, stages in works:
        lax.fori_loop(0, count, lambda k, _, s=stages[-1]: (s(k), 0)[1], 0)


def exchange(total_ref, sum_ref, totals_ref, sums_ref, send, recv):
    count = totals_ref.shape[0]
    me = lax.axis_index("seq")
    copies = []
    for o in range(1, count):
        peer = {"seq": lax.rem(me + o, count)}
        for i, (src, dst) in enumerate(((total_ref, totals_ref), (sum_ref, sums_ref))):
            copies.append(
                pltpu.make_async_remote_copy(
                    src_ref=src, dst_ref=dst.at[me], send_sem=send.at[i, o - 1],
                    recv_sem=recv.at[i, o - 1], device_id=peer, device_id_type=MESH,
                )
            )
    for copy in copies:
        copy.start()
    for copy in copies:
        copy.wait()


def forward_scan_kernel(
    tasks, numbers, depth, lead, nstate, pack_ref, act_ref, sel_ref, cut_ref, *refs
):
    hosted = len(tasks)
    srcs, refs = split_refs(refs, numbers)
    (step_ref, sig_ref, moment_ref, full_ref, keep_ref), refs = refs[:5], refs[5:]
    gouts, refs = refs[:hosted], refs[hosted:]
    (low, inb, outb, decay, drives, enter, befores, total_ref, sum_ref, totals_ref, sums_ref, send, recv), rest = refs[:13], refs[13:]
    count = act_ref.shape[0]
    rank = low.shape[1]
    wide = sel_ref.shape[1]
    p, j = pl.program_id(0), pl.program_id(1)
    blocks = pl.num_programs(1)
    turn = p * blocks + j
    me = lax.axis_index("seq")
    lanes = pl.ds(pl.multiple_of(j * LANES, LANES), LANES)
    gathers = [
        Gather(depth, layer, width, base, srcs[i], gouts[i], *rest[4 * i : 4 * i + 4])
        for i, (layer, width, base, _) in enumerate(tasks)
    ]

    @pl.when(turn == 0)
    def _():
        hail(depth)
        low[...] = sel_ref[:, :rank].astype(BF16)
        spread(inb, sel_ref, nstate, rank)
        spread(outb, sel_ref, nstate, rank + nstate)

    @pl.when(turn == 1)
    def _():
        await_hails(depth)
        for gather in gathers:
            lax.fori_loop(0, gather.count, lambda k, _, g=gather: (g.first(k), 0)[1], 0)

    works = [(gather.count, gather.stages()) for gather in gathers]
    pace, slots = 15, (2, 5, 9, 13)
    timetable(turn, turn - 1, pace, slots, works)

    @pl.when(p == 0)
    def _():
        stepw = pack_ref[0, wide : wide + rank, :]
        pre = jnp.dot(low[...], stepw, preferred_element_type=F32) + vector_of(pack_ref, 5)
        near = jnp.exp(-jnp.abs(pre))
        step_all = jnp.maximum(pre, 0.0) + jnp.log1p(near)
        step_ref[...] = step_all
        sig_ref[...] = jnp.where(pre >= 0.0, 1.0, near) / (1.0 + near)
        moment_ref[0:1, :] = jnp.sum(step_all, axis=0, keepdims=True)
        moment_ref[1:2, :] = jnp.sum(step_all * step_all, axis=0, keepdims=True)
        rate = rates_of(pack_ref, nstate)
        rates = rate_rows(rate, nstate)

        def body(pair, carry):
            states, sums = carry
            act = act_ref[pl.ds(pl.multiple_of(pair * 16, 16), 16), :].astype(F32)
            for half in (0, 1):
                at = pl.ds(pl.multiple_of(pair * 16 + half * 8, 8), 8)
                step = step_ref[at, :]
                away = step + cut_ref[at, :]
                drive = step * act[half * 8 : half * 8 + 8]
                drives[j, at, :] = drive
                sums = sums + away
                new = []
                for n in range(nstate):
                    gain = jnp.exp2(away * rates[n])
                    decay[j, n, at, :] = gain
                    new.append(gain * states[n] + drive * inb[n, at, :])
                states = tuple(new)
            return states, sums

        zero = jnp.zeros((CHUNKS, LANES), F32)
        ends, sums = lax.fori_loop(0, count // 16, body, ((zero,) * nstate, zero), unroll=2)
        entering, totals, before, total = chunk_links(ends, sums, rates, False)
        for n in range(nstate):
            enter[j, n] = entering[n]
        total_ref[:, lanes] = jnp.concatenate(totals, axis=0).astype(total_ref.dtype)
        befores[j] = before
        sum_ref[:, lanes] = total

    @pl.when(turn == blocks)
    def _():
        exchange(total_ref, sum_ref, totals_ref, sums_ref, send, recv)

    @pl.when(p == 1)
    def _():
        rate = rates_of(pack_ref, nstate)
        rates = rate_rows(rate, nstate)
        arrived = arriving_state(me, totals_ref, sums_ref, lanes, rate, False)
        before = befores[j]
        states = tuple(
            enter[j, n] + jnp.exp2(before * rates[n]) * arrived[n : n + 1, :] for n in range(nstate)
        )
        skip = jnp.broadcast_to(vector_of(pack_ref, 6), (CHUNKS, LANES))

        def body(pair, states):
            rows = pl.ds(pl.multiple_of(pair * 16, 16), 16)
            act = act_ref[rows, :].astype(F32)
            held = []
            for half in (0, 1):
                at = pl.ds(pl.multiple_of(pair * 16 + half * 8, 8), 8)
                held.append(states)
                drive = drives[j, at, :]
                out = skip * act[half * 8 : half * 8 + 8]
                new = []
                for n in range(nstate):
                    state = decay[j, n, at, :] * states[n] + drive * inb[n, at, :]
                    out = out + state * outb[n, at, :]
                    new.append(state)
                states = tuple(new)
                full_ref[at, :] = out
            for n in range(nstate):
                both = jnp.concatenate([held[0][n], held[1][n]], axis=0)
                keep_ref[0, n, rows, :] = both.astype(keep_ref.dtype)
            return states

        ends = lax.fori_loop(0, count // 16, body, states, unroll=2)
        for n in range(nstate):
            both = jnp.concatenate([ends[n], ends[n]], axis=0)
            keep_ref[0, n, count : count + 16, :] = both.astype(keep_ref.dtype)

    @pl.when(turn == 2 * lead - 1)
    def _():
        wind_up(2 * lead - 1, pace, slots, works)


def forward_scan(pack, nstate, act, selected, cut, sources, tasks, collective):
    count, inner = act.shape
    rank = selected.shape[1] - 2 * nstate
    depth = lax.axis_size("seq")
    blocks = inner // LANES
    last = blocks - 1
    arrays = [piece for source in sources for piece in pieces_of(source)]
    lengths = [sum(piece.shape[0] for piece in pieces_of(source)) for source in sources]
    anywhere = pl.BlockSpec(memory_space=pl.ANY)
    outs = pl.pallas_call(
        functools.partial(forward_scan_kernel, tasks, counts_of(sources), depth, blocks, nstate),
        grid=(2, blocks),
        in_specs=[
            pl.BlockSpec((1,) + pack.shape[1:], lambda p, j: (j, 0, 0)),
            spec(count, last, 2),
            fixed(*selected.shape),
            fixed(count, LANES),
        ]
        + [anywhere] * len(arrays),
        out_specs=[
            spec(count, last, 0),
            spec(count, last, 0),
            spec(2, last, 0),
            spec(count, last, 1),
            pl.BlockSpec((1, nstate, count + 16, LANES), lambda p, j: (j * p, 0, 0, 0)),
        ]
        + [anywhere] * len(tasks),
        out_shape=[
            jax.ShapeDtypeStruct((count, inner), F32),
            jax.ShapeDtypeStruct((count, inner), F32),
            jax.ShapeDtypeStruct((2, inner), F32),
            jax.ShapeDtypeStruct((count, inner), F32),
            jax.ShapeDtypeStruct((blocks, nstate, count + 16, LANES), BF16),
        ]
        + [gather_shape(r, t[3], depth, BF16) for r, t in zip(lengths, tasks)],
        scratch_shapes=[
            pltpu.VMEM((count, rank), BF16),
            pltpu.VMEM((nstate, count, LANES), F32),
            pltpu.VMEM((nstate, count, LANES), F32),
            pltpu.VMEM((blocks, nstate, count, LANES), F32),
            pltpu.VMEM((blocks, count, LANES), F32),
            pltpu.VMEM((blocks, nstate, CHUNKS, LANES), F32),
            pltpu.VMEM((blocks, CHUNKS, LANES), F32),
            pltpu.VMEM((nstate, inner), BF16),
            pltpu.VMEM((1, inner), F32),
            pltpu.VMEM((depth, nstate, inner), BF16),
            pltpu.VMEM((depth, 1, inner), F32),
            pltpu.SemaphoreType.DMA((2, depth - 1)),
            pltpu.SemaphoreType.DMA((2, depth - 1)),
        ]
        + gather_scratch([(r, t[3], t[1], BF16) for r, t in zip(lengths, tasks)], depth),
        compiler_params=pltpu.CompilerParams(
            dimension_semantics=("arbitrary", "arbitrary"), collective_id=collective,
            has_side_effects=True, vmem_limit_bytes=VMEM_LIMIT,
        ),
        name="forward_scan",
    )(pack, act, selected, cut, *arrays)
    return outs[:5], [flat_rows(out) for out in outs[5:]]


def backward_scan_kernel(
    tasks, numbers, homes, olds, depth, lead, nstate, dfull_ref, step_ref, cut_ref, pack_ref, sel_ref, act_ref, sig_ref,
    keep_ref, *refs
):
    srcs, refs = split_refs(refs, numbers)
    refs = refs[olds:]
    (dact_ref, gbias_ref, gskip_ref, gdecay_ref, gstepw_ref, dsel_ref), refs = refs[:6], refs[6:]
    gouts, refs = refs[:homes], refs[homes:]
    (
        low, inb, outb, decay, enter, befores, total_ref, sum_ref, totals_ref, sums_ref,
        din_acc, dout_acc, decay_acc, dlow_acc, dstep_buf, send, recv,
    ), rest = refs[:17], refs[17:]
    count = act_ref.shape[0]
    rank = low.shape[1]
    wide = sel_ref.shape[1]
    pairs = count // 16
    p, j = pl.program_id(0), pl.program_id(1)
    blocks = pl.num_programs(1)
    turn = p * blocks + j
    me = lax.axis_index("seq")
    lanes = pl.ds(pl.multiple_of(j * LANES, LANES), LANES)
    items = [
        Reduce(depth, layer, width, base, srcs[i], gouts[home], *rest[9 * i : 9 * i + 9])
        for i, (layer, width, home, base) in enumerate(tasks)
    ]

    @pl.when(turn == 0)
    def _():
        hail(depth)
        low[...] = sel_ref[:, :rank].astype(BF16)
        spread(inb, sel_ref, nstate, rank)
        spread(outb, sel_ref, nstate, rank + nstate)
        din_acc[...] = jnp.zeros_like(din_acc)
        dout_acc[...] = jnp.zeros_like(dout_acc)
        dlow_acc[...] = jnp.zeros_like(dlow_acc)

    @pl.when(turn == 1)
    def _():
        await_hails(depth)

    works = [(item.count, item.stages()) for item in items]
    pace, slots = 6 if len(works) > 2 else 4, (2, 4, 9, 14, 18)
    timetable(turn + p * j, turn - 1 + p * jnp.maximum(j - 1, 0), pace, slots, works)

    @pl.when(p == 0)
    def _():
        rate = rates_of(pack_ref, nstate)
        rates = rate_rows(rate, nstate)

        def body(step_back, carry):
            states, sums = carry
            pair = pairs - 1 - step_back
            for half in (1, 0):
                at = pl.ds(pl.multiple_of(pair * 16 + half * 8, 8), 8)
                away = step_ref[at, :] + cut_ref[at, :]
                grad = dfull_ref[at, :]
                sums = sums + away
                new = []
                for n in range(nstate):
                    gain = jnp.exp2(away * rates[n])
                    decay[j, n, at, :] = gain
                    new.append(gain * (states[n] + outb[n, at, :] * grad))
                states = tuple(new)
            return states, sums

        zero = jnp.zeros((CHUNKS, LANES), F32)
        ends, sums = lax.fori_loop(0, pairs, body, ((zero,) * nstate, zero), unroll=2)
        entering, totals, before, total = chunk_links(ends, sums, rates, True)
        for n in range(nstate):
            enter[j, n] = entering[n]
        total_ref[:, lanes] = jnp.concatenate(totals, axis=0).astype(total_ref.dtype)
        befores[j] = before
        sum_ref[:, lanes] = total

    @pl.when(turn == blocks)
    def _():
        exchange(total_ref, sum_ref, totals_ref, sums_ref, send, recv)

    @pl.when(p == 1)
    def _():
        rate = rates_of(pack_ref, nstate)
        rates = rate_rows(rate, nstate)
        arrived = arriving_state(me, totals_ref, sums_ref, lanes, rate, True)
        before = befores[j]
        states = tuple(
            enter[j, n] + jnp.exp2(before * rates[n]) * arrived[n : n + 1, :] for n in range(nstate)
        )
        skip = jnp.broadcast_to(vector_of(pack_ref, 6), (CHUNKS, LANES))
        for n in range(nstate):
            decay_acc[n] = jnp.zeros((CHUNKS, LANES), F32)
            last = keep_ref[0, n, count : count + 16, :].astype(F32)[0:CHUNKS]
            dout_acc[n, pl.ds(count, CHUNKS), :] += last * dfull_ref[pl.ds(count - CHUNKS, CHUNKS), :]

        def body(step_back, carry):
            states, gskip = carry
            pair = pairs - 1 - step_back
            rows = pl.ds(pl.multiple_of(pair * 16, 16), 16)
            act = act_ref[rows, :].astype(F32)
            held = [keep_ref[0, n, rows, :].astype(F32) for n in range(nstate)]
            sums = [None] * nstate
            for half in (1, 0):
                at = pl.ds(pl.multiple_of(pair * 16 + half * 8, 8), 8)
                step = step_ref[at, :]
                act_now = act[half * 8 : half * 8 + 8]
                drive = step * act_now
                grad = dfull_ref[at, :]
                gskip = gskip + grad * act_now
                if half:
                    earlier = dfull_ref[pl.ds(pl.multiple_of(pair * 16, 8), 8), :]
                else:
                    earlier = dfull_ref[pl.ds(pl.multiple_of(jnp.maximum(pair * 16 - 8, 0), 8), 8), :]
                by_rate = jnp.zeros((CHUNKS, LANES), F32)
                mapped = jnp.zeros((CHUNKS, LANES), F32)
                new = []
                for n in range(nstate):
                    prior = held[n][half * 8 : half * 8 + 8]
                    adjoint = states[n] + outb[n, at, :] * grad
                    passed = adjoint * decay[j, n, at, :]
                    rho = passed * prior
                    by_rate = by_rate + rho * rates[n]
                    mapped = mapped + adjoint * inb[n, at, :]
                    sums[n] = rho * step if half else sums[n] + rho * step
                    din_acc[n, at, :] += adjoint * drive
                    dout_acc[n, at, :] += prior * earlier
                    new.append(passed)
                states = tuple(new)
                dstep_buf[at, :] = by_rate * LN2 + act_now * mapped
                dact_ref[at, :] = step * mapped + skip * grad
            for n in range(nstate):
                decay_acc[n] += sums[n]
            return states, gskip

        _, gskip = lax.fori_loop(0, pairs, body, (states, jnp.zeros((CHUNKS, LANES), F32)), unroll=2)
        gskip_ref[...] = jnp.sum(gskip, axis=0, keepdims=True)
        decays = [jnp.sum(decay_acc[n], axis=0, keepdims=True) for n in range(nstate)]
        gdecay = (rate * LN2) * jnp.concatenate(decays, axis=0)
        gdecay_ref[0] = gdecay.astype(gdecay_ref.dtype)
        dpre = dstep_buf[...] * sig_ref[...]
        gbias_ref[...] = jnp.sum(dpre, axis=0, keepdims=True)
        low_dpre = dpre.astype(BF16)
        gstepw_ref[0] = lax.dot_general(
            low[...], low_dpre, (((0,), (0,)), ((), ())), preferred_element_type=F32
        ).astype(gstepw_ref.dtype)
        dlow_acc[...] += lax.dot_general(
            low_dpre, pack_ref[0, wide : wide + rank, :], (((1,), (1,)), ((), ())),
            preferred_element_type=F32,
        )

    @pl.when(turn == 2 * lead - 1)
    def _():
        column = lax.broadcasted_iota(jnp.int32, (LANES, nstate), 1)
        din = jnp.zeros((count, nstate), F32)
        dout = jnp.zeros((count, nstate), F32)
        for n in range(nstate):
            pick = (column == n).astype(BF16)
            din = din + jnp.dot(din_acc[n].astype(BF16), pick, preferred_element_type=F32)
            part = dout_acc[n, CHUNKS : count + CHUNKS, :].astype(BF16)
            dout = dout + jnp.dot(part, pick, preferred_element_type=F32)
        dsel_ref[...] = jnp.concatenate([dlow_acc[...], din, dout], axis=1).astype(BF16)

    @pl.when(turn == 2 * lead - 1)
    def _():
        wind_up(3 * lead - 2, pace, slots, works)


def backward_scan(
    dfull, step, cut, pack, nstate, selected, act, sig, keep, sources, tasks, homes, collective
):
    count, inner = act.shape
    rank = selected.shape[1] - 2 * nstate
    depth = lax.axis_size("seq")
    blocks = inner // LANES
    last = blocks - 1
    arrays = [by_chip(piece, depth) for source in sources for piece in pieces_of(source)]
    olds = {i: home for i, home in enumerate(homes) if not isinstance(home, tuple)}
    shapes = [home if isinstance(home, tuple) else home.shape for home in homes]
    anywhere = pl.BlockSpec(memory_space=pl.ANY)
    outs = pl.pallas_call(
        functools.partial(
            backward_scan_kernel, tasks, counts_of(sources), len(homes), len(olds), depth, blocks, nstate
        ),
        grid=(2, blocks),
        in_specs=[
            spec(count, last, 2),
            spec(count, last, 2),
            fixed(count, LANES),
            pl.BlockSpec((1,) + pack.shape[1:], lambda p, j: (j, 0, 0)),
            fixed(*selected.shape),
            spec(count, last, 1),
            spec(count, last, 1),
            pl.BlockSpec((1, nstate, count + 16, LANES), lambda p, j: (j * p, 0, 0, 0)),
        ]
        + [anywhere] * (len(arrays) + len(olds)),
        out_specs=[
            spec(count, last, 1),
            spec(1, last, 1),
            spec(1, last, 1),
            pl.BlockSpec((1, nstate, LANES), lambda p, j: (j * p, 0, 0)),
            pl.BlockSpec((1, rank, LANES), lambda p, j: (j * p, 0, 0)),
            fixed(*selected.shape),
        ]
        + [anywhere] * len(homes),
        out_shape=[
            jax.ShapeDtypeStruct((count, inner), F32),
            jax.ShapeDtypeStruct((1, inner), F32),
            jax.ShapeDtypeStruct((1, inner), F32),
            jax.ShapeDtypeStruct((blocks, nstate, LANES), BF16),
            jax.ShapeDtypeStruct((blocks, rank, LANES), BF16),
            jax.ShapeDtypeStruct(selected.shape, BF16),
        ]
        + [jax.ShapeDtypeStruct(shape, F32) for shape in shapes],
        scratch_shapes=[
            pltpu.VMEM((count, rank), BF16),
            pltpu.VMEM((nstate, count, LANES), F32),
            pltpu.VMEM((nstate, count, LANES), F32),
            pltpu.VMEM((blocks, nstate, count, LANES), F32),
            pltpu.VMEM((blocks, nstate, CHUNKS, LANES), F32),
            pltpu.VMEM((blocks, CHUNKS, LANES), F32),
            pltpu.VMEM((nstate, inner), BF16),
            pltpu.VMEM((1, inner), F32),
            pltpu.VMEM((depth, nstate, inner), BF16),
            pltpu.VMEM((depth, 1, inner), F32),
            pltpu.VMEM((nstate, count, LANES), F32),
            pltpu.VMEM((nstate, count + CHUNKS, LANES), F32),
            pltpu.VMEM((nstate, CHUNKS, LANES), F32),
            pltpu.VMEM((count, rank), F32),
            pltpu.VMEM((count, LANES), F32),
            pltpu.SemaphoreType.DMA((2, depth - 1)),
            pltpu.SemaphoreType.DMA((2, depth - 1)),
        ]
        + reduce_scratch([shard_of(s) + (t[1], BF16) for s, t in zip(sources, tasks)], depth),
        input_output_aliases={8 + len(arrays) + n: 6 + i for n, i in enumerate(olds)},
        compiler_params=pltpu.CompilerParams(
            dimension_semantics=("arbitrary", "arbitrary"), collective_id=collective,
            has_side_effects=True, vmem_limit_bytes=VMEM_LIMIT,
        ),
        name="backward_scan",
    )(dfull, step, cut, pack, selected, act, sig, keep, *arrays, *olds.values())
    return outs[:6], outs[6:]


def places(lengths, count, reach):
    steps = count // CHUNKS
    base = lax.axis_index("seq") * count
    starts = jnp.cumsum(lengths) - lengths
    here = (
        base + jnp.arange(steps, dtype=jnp.int32)[:, None]
        + steps * jnp.arange(CHUNKS, dtype=jnp.int32)[None, :]
    )

    def segment(at):
        return jnp.sum((starts[:, None, None] <= at[None]).astype(jnp.int32), axis=0) - 1

    own = segment(here)
    same = jnp.stack(
        [(segment(here - reach + k) == own).astype(F32).reshape(count) for k in range(reach)]
    )
    same = jnp.broadcast_to(same[:, :, None], same.shape + (LANES,))
    opens = jnp.any(starts[:, None, None] == here[None], axis=0)
    cut = jnp.where(opens, CUT, 0.0).astype(F32).reshape(count, 1)
    return same, jnp.broadcast_to(cut, (count, LANES))


def layer_forward(xin, in_conv, other, same, cut, host, collective):
    pack, gain, wide, nstate = other
    count = xin.shape[0]
    inner = in_conv.shape[1]
    reach = same.shape[0]
    scale = lax.rsqrt(jnp.mean(xin * xin, axis=-1, keepdims=True) + EPS)
    normed = (xin * scale * gain).astype(BF16)
    conv_in = jnp.dot(normed, in_conv, preferred_element_type=F32).astype(BF16)
    last = conv_in[(count - reach * CHUNKS) :].reshape(reach, CHUNKS, inner)[:, CHUNKS - 1]
    halo = shifted(last, "seq", 1)
    act, selected = select_call(conv_in, halo, same, pack, wide)
    (step, sig, moments, full, keep), got = forward_scan(
        pack, nstate, act, selected, cut, host[0], host[1], collective
    )
    return (scale, normed, conv_in, halo, act, selected, step, sig, full, keep), moments, got


def layer_output(xin, normed, full, in_gate, out_weight):
    gate = jnp.dot(normed, in_gate, preferred_element_type=F32).astype(BF16)
    wide = gate.astype(F32)
    gated = (full * (wide * jax.nn.sigmoid(wide))).astype(BF16)
    return xin + jnp.dot(gated, out_weight, preferred_element_type=F32), gate, gated


def outer_sum(left, right):
    return lax.dot_general(left, right, (((0,), (0,)), ((), ())), preferred_element_type=F32)


def times_transposed(left, right):
    return lax.dot_general(left, right, (((1,), (1,)), ((), ())), preferred_element_type=F32)


def layer_backward(grad_out, weights, same, cut, saved, moments, host, collective):
    in_conv, in_gate, out_weight, pack, gain, _, nstate = weights
    (xin, scale, normed, conv_in, halo, act, selected, step, sig, full, keep, gate, gated) = saved
    count, inner = act.shape
    reach = same.shape[0]
    grad_low = grad_out.astype(BF16)
    dgated = times_transposed(grad_low, out_weight)
    gout = outer_sum(gated, grad_low).astype(BF16)
    wide = gate.astype(F32)
    dfull = dgated * (wide * jax.nn.sigmoid(wide))
    dgate = (dgated * full * silu_slope(wide)).astype(BF16)
    gin_gate = outer_sum(normed, dgate).astype(BF16)
    sources, tasks, homes = host(gout, gin_gate)
    (dact, gbias, gskip, gdecay, gstepw, dsel), found = backward_scan(
        dfull, step, cut, pack, nstate, selected, act, sig, keep, sources, tasks, homes, collective
    )
    dconv, tail, spill, gsel, gsmall = conv_grad(
        conv_in, halo, same, pack, act, dact, dsel, gbias, gskip
    )
    late = (tail + shifted(spill, "seq", -1)).astype(BF16)
    grid = dconv.reshape(count // CHUNKS, CHUNKS, inner)
    dconv = grid.at[count // CHUNKS - reach :, CHUNKS - 1].set(late).reshape(count, inner)
    gin_conv = outer_sum(normed, dconv).astype(BF16)
    dnormed = times_transposed(dconv, in_conv) + times_transposed(dgate, in_gate)
    unit = xin * scale
    ggain = jnp.sum(dnormed * unit, axis=0)
    dunit = dnormed * gain
    grad_in = scale * (dunit - unit * jnp.mean(dunit * unit, axis=-1, keepdims=True)) + grad_out
    shards = lax.axis_size(("dp", "seq"))
    per = inner // shards
    if per < LANES:
        blocked = lambda rows: rows.swapaxes(0, 1).reshape(rows.shape[1], shards, per).swapaxes(0, 1)
        gsel, gstepw, gdecay, gsmall = (blocked(rows) for rows in (gsel, gstepw, gdecay, gsmall))
    ggain = jnp.pad(ggain.reshape(shards, 1, -1), ((0, 0), (0, 0), (0, per - ggain.shape[0] // shards)))
    moments = moments.reshape(2, shards, per).swapaxes(0, 1)
    rest = jnp.concatenate([ggain, moments, jnp.zeros((shards, 5, per), F32)], axis=1)
    rest = jnp.concatenate([gsmall, rest], axis=1).astype(BF16)
    rows = ([gsel], [gstepw, gdecay, rest])
    return grad_in, gin_conv, gin_gate, gout, rows, found


AXES = ("section", "dp", "seq")


def body(
    inputs, doc_lengths, out_grad, norm_gain, in_weight, conv_weight, conv_bias, select_weight,
    step_weight, step_bias, log_decay, skip_gain, out_weight,
):
    section = lax.axis_index("section")
    micro, _, count, model = inputs.shape
    taps, per = conv_weight.shape[1:]
    shards = lax.axis_size(("dp", "seq"))
    inner = per * shards
    rank, nstate = step_weight.shape[1], log_decay.shape[1]
    wide = rank + 2 * nstate

    kernels = lax.axis_size("dp") == 4 and per % LANES == 0 and in_weight.shape[1] % 32 == 0
    pad = per - norm_gain.shape[1]
    vectors = [conv_weight[0], conv_bias, step_bias, skip_gain, jnp.pad(norm_gain, ((0, 0), (0, pad)))]
    vectors = [v.astype(F32) for v in vectors] + [jnp.zeros((16 - taps - 4, per), F32)]
    vectors = jnp.concatenate(vectors, axis=0).astype(BF16)
    pieces = [select_weight[0].T, step_weight[0], log_decay[0], vectors]
    in_half, out_half = in_weight[0], out_weight[0]
    if kernels:
        length = sum(piece.shape[0] for piece in pieces)
        quarter = in_half.shape[:1] + (inner,)
        packs = gather_rows(
            pieces + [in_half], [((0,), (1, 2, 3)), 4, 4],
            [(0, per, 0), (0, 256, 0), (0, 256, inner)],
            [(length, per), quarter, quarter], None, 2,
        )
        packed = [packs[0].reshape(shards, -1, per), None]
        in_conv, in_gate = [packs[1], None], [packs[2], None]
        outs_weight = [None, None]
        hosts = [
            (
                [([pieces[0]], pieces[1:]), in_half, out_half],
                [(1, per, 0, per), (1, 256, 0, inner), (0, 128, 0, model)],
            ),
            ([in_half, out_half], [(1, 256, inner, inner), (1, 128, 0, model)]),
        ]
    else:
        packed = lax.all_gather(jnp.concatenate(pieces, axis=0), AXES, axis=0).reshape(2, shards, -1, per)
        in_all = lax.all_gather(in_half, AXES, axis=0, tiled=True).reshape(2, model, -1)
        in_conv, in_gate = in_all[:, :, :inner], in_all[:, :, inner:]
        outs_weight = lax.all_gather(out_half, AXES, axis=0, tiled=True).reshape(2, inner, model)
        hosts = [([], []), ([], [])]
    def other(layer):
        pack = packed[layer]
        gain = pack[:, wide + rank + nstate + taps + 3, : norm_gain.shape[1]].reshape(-1).astype(F32)
        if per < LANES:
            flat = pack.swapaxes(0, 1).reshape(-1, inner)
            pack = flat.reshape(-1, inner // LANES, LANES).swapaxes(0, 1)
        return pack, gain, wide, nstate

    mine = lambda value: lax.dynamic_index_in_dim(value, section, 0, keepdims=False)[0]
    same, cut = places(mine(doc_lengths), count, taps - 1)
    state = interleave(mine(inputs).astype(F32))
    outs, kept, weights = [], [], []
    for layer in range(2):
        saved, moments, got = layer_forward(
            state, in_conv[layer], other(layer), same, cut, hosts[layer], 5 + layer
        )
        if kernels:
            if layer == 0:
                packed[1] = got.pop(0).reshape(shards, -1, per)
            (in_gate if layer else in_conv)[1], outs_weight[layer] = got
        result, gate, gated = layer_output(
            state, saved[1], saved[8], in_gate[layer], outs_weight[layer]
        )
        weights.append((in_conv[layer], in_gate[layer], outs_weight[layer]) + other(layer))
        kept.append(((state,) + saved + (gate, gated), moments))
        state = result
        outs.append(state)
    grad = interleave(mine(out_grad).astype(F32))
    def split(value):
        return value.reshape(shards, -1, value.shape[1])

    grads = [None] * 2
    parts = [None] * 2
    found = []
    for layer in (1, 0):
        if not kernels:
            host = lambda gout, gin_gate: ([], [], [])
        elif layer == 1:
            host = lambda gout, gin_gate: (
                [split(gout), split(gin_gate)], [(1, 256, 0, 0), (1, 512, 1, inner)],
                [(per, model), (in_half.shape[0], 2 * inner)],
            )
        else:
            host = lambda gout, gin_gate: (
                [split(gout), parts[1][1], parts[1][0], split(gin_gate)],
                [(0, 256, 0, 0), (1, 512, 1, 0), (1, per, 2, 0), (0, 512, 1, inner)],
                list(found) + [(length, per)],
            )
        grad, gin_conv, gin_gate, gout, pack, found = layer_backward(
            grad, weights[layer], same, cut, *kept[layer], host, 7 + layer
        )
        grads[layer] = grad
        parts[layer] = [pack, split(gin_conv), split(gin_gate), split(gout)]

    if kernels:
        results, (gin, rows) = reduce_rows(
            [parts[0][1], parts[0][0]], [(0, 256, 0, 0), (0, per, 1, 0)], [found[1], (length, per)],
            outs + grads, 3,
        )
        rows = jnp.where(section == 0, rows, found[2])
        gout = found[0]
    else:
        found = []
        for side in parts:
            side[0] = jnp.concatenate(pieces_of(side[0]), axis=1)
        for pair in zip(*parts):
            both = jnp.stack(pair).reshape((-1,) + pair[0].shape[1:])
            found.append(lax.psum_scatter(both, AXES, scatter_dimension=0).astype(F32))
        rows, gin_conv, gin_gate, gout = found
        gin = jnp.concatenate([gin_conv, gin_gate], axis=1)

    def place(values):
        first, second = (in_order(value) for value in values)
        own = jnp.where(section == 0, first, second)
        other = jnp.where(section == 0, second, first)
        other = lax.ppermute(other, "section", [(0, 1), (1, 0)])
        both = jnp.stack([jnp.where(section == 0, own, other), jnp.where(section == 0, other, own)])
        return both

    both = (1, micro, 1, count, model)
    at = wide + rank + nstate
    tokens = micro * inputs.shape[1] * lax.axis_size("dp") * count * lax.axis_size("seq")
    if not kernels:
        results = place(outs), place(grads)
    return (
        results[0].reshape(both),
        results[1].reshape(both),
        rows[at + 8, : norm_gain.shape[1]][None],
        gin[None],
        rows[at : at + taps][None],
        rows[at + taps][None],
        rows[:wide].T[None],
        rows[wide : wide + rank][None],
        rows[at + taps + 1][None],
        rows[wide + rank : at][None],
        rows[at + taps + 2][None],
        gout[None],
        (rows[at + 9 : at + 11] / tokens)[None],
    )


def solution(mesh):
    vector = P("section", ("dp", "seq"))
    matrix = P("section", ("dp", "seq"), None)
    turned = P("section", None, ("dp", "seq"))
    tokens = P(None, "dp", "seq", None)
    in_specs = (
        tokens, P(None, "dp", None), tokens, vector, matrix, turned, vector, matrix, turned,
        vector, turned, vector, matrix,
    )
    result = P("section", None, "dp", "seq", None)
    out_specs = (
        result, result, vector, matrix, turned, vector, matrix, turned, vector, turned, vector,
        matrix, turned,
    )
    return jax.shard_map(body, mesh=mesh, in_specs=in_specs, out_specs=out_specs, check_vma=False)
```

```python
import functools
import itertools
import math

import jax
import jax.numpy as jnp
from jax import lax
from jax.experimental import pallas as pl
from jax.experimental.pallas import tpu as pltpu
from jax.sharding import PartitionSpec as P

EPS = 1e-05
LOG2E = math.log2(math.e)
LN2 = math.log(2.0)
CUT = 1e30
LANES = 128
CHUNKS = 8
VMEM_LIMIT = 66_000_000
F32 = jnp.float32
BF16 = jnp.bfloat16


def silu_slope(values):
    sigma = jax.nn.sigmoid(values)
    return sigma * (1.0 + values * (1.0 - sigma))


def interleave(rows):
    count = rows.shape[0]
    return rows.reshape(CHUNKS, count // CHUNKS, -1).swapaxes(0, 1).reshape(count, -1)


def in_order(rows):
    count = rows.shape[0]
    return rows.reshape(count // CHUNKS, CHUNKS, -1).swapaxes(0, 1).reshape(count, -1)


def column_params(**kw):
    return pltpu.CompilerParams(
        dimension_semantics=("arbitrary",), vmem_limit_bytes=VMEM_LIMIT, **kw
    )


def cols(rows, width=LANES):
    return pl.BlockSpec((rows, width), lambda j: (0, j))


def whole(*shape):
    return pl.BlockSpec(shape, lambda j: (0,) * len(shape))


def conv_taps(conv_ref, halo_ref, steps, reach):
    width = conv_ref.shape[1]
    own = conv_ref[...].astype(F32).reshape(steps, CHUNKS, width)
    tail = own[steps - reach :]
    moved = pltpu.roll(tail.reshape(reach * CHUNKS, width), 1, 0).reshape(reach, CHUNKS, width)
    first = lax.broadcasted_iota(jnp.int32, moved.shape, 1) == 0
    halo = halo_ref[...].astype(F32)[:, None, :]
    head = jnp.where(first, jnp.broadcast_to(halo, moved.shape), moved)
    return jnp.concatenate([head, own], axis=0)


def mask_of(same_ref, k, width):
    mask = jnp.concatenate([same_ref[k]] * (width // LANES), axis=1)
    return mask.reshape(-1, CHUNKS, width)


def convolve(ext, small_ref, same_ref, steps, reach):
    width = ext.shape[2]
    pre = jnp.broadcast_to(small_ref[reach + 1 : reach + 2, :], (steps * CHUNKS, width))
    pre = pre.reshape(steps, CHUNKS, width)
    for k in range(reach + 1):
        term = small_ref[k : k + 1, :][None] * ext[k : k + steps]
        pre = pre + (term if k == reach else term * mask_of(same_ref, k, ext.shape[2]))
    return pre.reshape(steps * CHUNKS, width)


def lanes_of(pack_ref, start, stop):
    return jnp.concatenate([pack_ref[i, start:stop, :] for i in range(pack_ref.shape[0])], axis=1)


def select_kernel(conv_ref, halo_ref, same_ref, pack_ref, act_ref, out_ref, acc):
    j = pl.program_id(0)
    count, width = conv_ref.shape
    reach = halo_ref.shape[0]
    steps = count // CHUNKS
    small_ref = lanes_of(pack_ref, pack_ref.shape[1] - 16, pack_ref.shape[1]).astype(F32)
    ext = conv_taps(conv_ref, halo_ref, steps, reach)
    pre = convolve(ext, small_ref, same_ref, steps, reach)
    act = (pre * jax.nn.sigmoid(pre)).astype(BF16)
    act_ref[...] = act

    @pl.when(j == 0)
    def _():
        acc[...] = jnp.zeros_like(acc)

    acc[...] += lax.dot_general(
        act, lanes_of(pack_ref, 0, acc.shape[1]), (((1,), (1,)), ((), ())),
        preferred_element_type=F32,
    )
    out_ref[...] = acc[...]


def pack_blocks(pack, width):
    return pl.BlockSpec((width // LANES,) + pack.shape[1:], lambda j: (j, 0, 0))


def select_call(conv_in, halo, same, pack, wide):
    count, inner = conv_in.shape
    width = min(512, inner)
    return pl.pallas_call(
        select_kernel,
        grid=(inner // width,),
        in_specs=[
            cols(count, width),
            cols(halo.shape[0], width),
            whole(*same.shape),
            pack_blocks(pack, width),
        ],
        out_specs=[cols(count, width), whole(count, wide)],
        out_shape=[
            jax.ShapeDtypeStruct((count, inner), BF16),
            jax.ShapeDtypeStruct((count, wide), F32),
        ],
        scratch_shapes=[pltpu.VMEM((count, wide), F32)],
        compiler_params=column_params(),
        name="conv_select",
    )(conv_in, halo, same, pack)


def spread(dst, src_ref, nstate, at):
    for n in range(nstate):
        dst[n] = jnp.broadcast_to(src_ref[:, at + n : at + n + 1], dst.shape[1:])


def chunk_links(ends, sums, rates, backward):
    row = lax.broadcasted_iota(jnp.int32, (CHUNKS, LANES), 0)
    gains = [jnp.exp2(sums * rate) for rate in rates]
    ends = list(ends)
    total = sums
    k = 1
    while k < CHUNKS:
        turn = CHUNKS - k if backward else k
        mask = row < CHUNKS - k if backward else row >= k
        ends = [
            jnp.where(mask, g, 0.0) * pltpu.roll(e, turn, 0) + e for g, e in zip(gains, ends)
        ]
        if 2 * k < CHUNKS:
            gains = [g * pltpu.roll(g, turn, 0) for g in gains]
        total = jnp.where(mask, pltpu.roll(total, turn, 0) + total, total)
        k *= 2
    turn = CHUNKS - 1 if backward else 1
    mask = row < CHUNKS - 1 if backward else row >= 1
    entering = [jnp.where(mask, pltpu.roll(e, turn, 0), 0.0) for e in ends]
    before = jnp.where(mask, pltpu.roll(total, turn, 0), 0.0)
    last = 0 if backward else CHUNKS - 1
    return entering, [e[last : last + 1] for e in ends], before, total[last : last + 1]


def rates_of(pack_ref, nstate):
    end = pack_ref.shape[1] - 16
    return -jnp.exp(pack_ref[0, end - nstate : end, :].astype(F32)) * LOG2E


def vector_of(pack_ref, row):
    at = pack_ref.shape[1] - 16
    return pack_ref[0, at : at + 16, :].astype(F32)[row : row + 1]


def rate_rows(rate, nstate):
    return [jnp.broadcast_to(rate[n : n + 1, :], (CHUNKS, LANES)) for n in range(nstate)]


def arriving_state(me, totals_ref, sums_ref, lanes, rate, backward):
    devices = totals_ref.shape[0]
    state = jnp.zeros(rate.shape, F32)
    order = range(devices - 1, 0, -1) if backward else range(devices - 1)
    for k in order:
        passed = jnp.exp2(rate * sums_ref[k, :, lanes]) * state
        passed = passed + totals_ref[k, :, lanes].astype(F32)
        state = jnp.where((k > me) if backward else (k < me), passed, state)
    return state


def conv_grad_kernel(
    conv_ref, halo_ref, same_ref, pack_ref, act_ref, dact_ref, dsel_ref,
    gbias_ref, gskip_ref, dconv_ref, tail_ref, spill_ref, gsel_ref, gsmall_ref,
):
    count, width = conv_ref.shape
    reach = halo_ref.shape[0]
    steps = count // CHUNKS
    ext = conv_taps(conv_ref, halo_ref, steps, reach)
    small_ref = lanes_of(pack_ref, pack_ref.shape[1] - 16, pack_ref.shape[1]).astype(F32)
    sel = lanes_of(pack_ref, 0, dsel_ref.shape[1])
    dsel = dsel_ref[...]
    gsel = lax.dot_general(
        dsel, act_ref[...], (((0,), (0,)), ((), ())), preferred_element_type=F32
    )
    dact = dact_ref[...] + jnp.dot(dsel, sel, preferred_element_type=F32)
    dpre = dact * silu_slope(convolve(ext, small_ref, same_ref, steps, reach))
    vectors = [jnp.sum(dpre, axis=0, keepdims=True), gbias_ref[...], gskip_ref[...]]
    dpre = dpre.reshape(steps, CHUNKS, width)
    parts, taps = [], []
    for k in range(reach + 1):
        masked = dpre if k == reach else dpre * mask_of(same_ref, k, width)
        taps.append(
            jnp.sum((masked * ext[k : k + steps]).reshape(count, width), axis=0, keepdims=True)
        )
        parts.append(masked * small_ref[k : k + 1, :][None])
    vectors = jnp.concatenate(taps + vectors + [jnp.zeros((4 - reach, width), F32)], axis=0)
    for i in range(width // LANES):
        gsel_ref[i] = gsel[:, i * LANES : (i + 1) * LANES].astype(gsel_ref.dtype)
        gsmall_ref[i] = vectors[:, i * LANES : (i + 1) * LANES]
    own = parts[reach]
    for k in range(reach):
        back = reach - k
        own = own + jnp.concatenate(
            [parts[k][back:], jnp.zeros((back, CHUNKS, width), F32)], axis=0
        )
    heads = []
    for e in range(reach):
        total = parts[0][e]
        for k in range(1, e + 1):
            total = total + parts[k][e - k]
        heads.append(total)
    head = jnp.stack(heads)
    spill_ref[...] = head[:, 0, :]
    row = lax.broadcasted_iota(jnp.int32, head.shape, 1)
    moved = pltpu.roll(head.reshape(reach * CHUNKS, width), reach * CHUNKS - 1, 0)
    moved = jnp.where(row == CHUNKS - 1, 0.0, moved.reshape(head.shape))
    tail = own[steps - reach :] + moved
    tail_ref[...] = tail[:, CHUNKS - 1, :]
    dconv = jnp.concatenate([own[: steps - reach], tail], axis=0)
    dconv_ref[...] = dconv.reshape(count, width).astype(BF16)


def conv_grad(conv_in, halo, same, pack, act, dact, dsel, gbias, gskip):
    count, inner = act.shape
    width = min(512, inner)
    reach = halo.shape[0]
    wide = dsel.shape[1]
    return pl.pallas_call(
        conv_grad_kernel,
        grid=(inner // width,),
        in_specs=[
            cols(count, width),
            cols(reach, width),
            whole(*same.shape),
            pack_blocks(pack, width),
            cols(count, width),
            cols(count, width),
            whole(count, wide),
            cols(1, width),
            cols(1, width),
        ],
        out_specs=[
            cols(count, width),
            cols(reach, width),
            cols(reach, width),
            pl.BlockSpec((width // LANES, wide, LANES), lambda j: (j, 0, 0)),
            pl.BlockSpec((width // LANES, 8, LANES), lambda j: (j, 0, 0)),
        ],
        out_shape=[
            jax.ShapeDtypeStruct((count, inner), BF16),
            jax.ShapeDtypeStruct((reach, inner), F32),
            jax.ShapeDtypeStruct((reach, inner), F32),
            jax.ShapeDtypeStruct((inner // LANES, wide, LANES), BF16),
            jax.ShapeDtypeStruct((inner // LANES, 8, LANES), F32),
        ],
        compiler_params=column_params(),
        name="conv_grad",
    )(conv_in, halo, same, pack, act, dact, dsel, gbias, gskip)


def shifted(value, axis, steps):
    count = lax.axis_size(axis)
    first, last = (max(0, -steps), min(count, count - steps))
    return lax.ppermute(value, axis, [(source, source + steps) for source in range(first, last)])


MESH = pl.DeviceIdType.MESH


def where_am_i():
    c, d, z = lax.axis_index("section"), lax.axis_index("dp"), lax.axis_index("seq")
    y, x = d // 2, d % 2
    flip_x, flip_y = y * 2 + (1 - x), (1 - y) * 2 + x
    return c, y, x, z, flip_x, flip_y


def peers_of(depth):
    c, y, x, z, flip_x, flip_y = where_am_i()
    peers = [{"section": 1 - c}, {"dp": flip_x}, {"dp": flip_y}]
    return peers + [{"seq": lax.rem(z + o, depth)} for o in range(1, depth)]


def hail(depth):
    barrier = pltpu.get_barrier_semaphore()
    for peer in peers_of(depth):
        pl.semaphore_signal(barrier, inc=1, device_id=peer, device_id_type=MESH)


def await_hails(depth):
    pl.semaphore_wait(pltpu.get_barrier_semaphore(), 2 + depth)


def greet(depth):
    hail(depth)
    await_hails(depth)


def pipeline(stages, count, lags, extras={}):
    for turn in range(count + lags[-1]):
        for lag, stage in zip(lags, stages):
            if 0 <= turn - lag < count:
                stage(turn - lag)
        if turn in extras:
            extras[turn]()


class Gather:
    def __init__(self, depth, layer, width, base, src, out, mine, send, recv, local):
        self.depth, self.layer, self.width, self.base = depth, layer, width, base
        self.src, self.out, self.mine = src, out, mine
        self.send, self.recv, self.local = send, recv, local
        self.count = mine.shape[0]
        c, y, x, z, flip_x, flip_y = where_am_i()
        self.c, self.y, self.x, self.z = c, y, x, z
        self.near = {"dp": (1 - c) * flip_y + c * flip_x}
        self.far = {"dp": (1 - c) * flip_x + c * flip_y}
        self.partner = {"section": 1 - c}

    def cols(self, k, base=0):
        if isinstance(k, int):
            return pl.ds(base + k * self.width, self.width)
        return pl.ds(pl.multiple_of(base + k * self.width, LANES), self.width)

    def remote(self, k, slot, src, dst, peer):
        return pltpu.make_async_remote_copy(
            src_ref=src, dst_ref=dst, send_sem=self.send.at[k, slot], recv_sem=self.recv.at[k, slot],
            device_id=peer, device_id_type=MESH,
        )

    def piece(self, k, at):
        return self.out.at[at[0], at[1], :, self.c, :, self.cols(k)]

    def pieces(self, k, half):
        rows = self.mine.shape[1]
        if not isinstance(self.src, tuple):
            return [(0, self.src.at[pl.ds(half * rows, rows), self.cols(k, self.base)])]
        found, at = [], 0
        for ref in self.src[half]:
            found.append((at, ref))
            at += ref.shape[0]
        return found

    def hand_wait(self, k):
        return self.remote(k, 0, self.mine.at[k], self.mine.at[k], self.partner)

    def keep_wait(self, k):
        return pltpu.make_async_copy(self.mine.at[k], self.mine.at[k], self.local.at[k, 0])

    def line(self, k):
        target = self.out.at[self.y, self.x, self.z, self.c, :, self.cols(k)]
        return [
            self.remote(k, o, self.mine.at[k], target, {"seq": lax.rem(self.z + o, self.depth)})
            for o in range(1, self.depth)
        ]

    def place(self, k):
        target = self.out.at[self.y, self.x, self.z, self.c, :, self.cols(k)]
        return pltpu.make_async_copy(self.mine.at[k], target, self.local.at[k, 1])

    def move(self, k, slot, at, peer):
        return self.remote(k, self.depth + slot, self.piece(k, at), self.piece(k, at), peer)

    def near_copy(self, k):
        return self.move(k, 0, (self.y, self.x), self.near)

    def far_copy(self, k, core):
        at = (slice(None), self.x) if core == 0 else (self.y, slice(None))
        return self.move(k, 1, at, self.far)

    def cross(self, k):
        return self.move(k, 2, (slice(None), slice(None)), self.partner)

    def first(self, k):
        @pl.when(self.c == self.layer)
        def _():
            for at, ref in self.pieces(k, 1 - self.layer):
                there = self.mine.at[k, pl.ds(at, ref.shape[0])]
                self.remote(k, 0, ref, there, self.partner).start()
            for at, ref in self.pieces(k, self.layer):
                here = self.mine.at[k, pl.ds(at, ref.shape[0])]
                pltpu.make_async_copy(ref, here, self.local.at[k, 0]).start()

    def along_z(self, k):
        @pl.when(self.c == self.layer)
        def _():
            self.hand_wait(k).wait_send()
            self.keep_wait(k).wait()

        @pl.when(self.c != self.layer)
        def _():
            self.hand_wait(k).wait_recv()

        for copy in self.line(k):
            copy.start()
        self.place(k).start()

    def along_near(self, k):
        for copy in self.line(k):
            copy.wait_recv()
        self.place(k).wait()
        self.near_copy(k).start()

    def along_far(self, k):
        self.near_copy(k).wait_recv()
        for core in (0, 1):

            @pl.when(self.c == core)
            def _(core=core):
                self.far_copy(k, core).start()

    def across(self, k):
        self.far_copy(k, 0).wait_recv()
        self.cross(k).start()

    def finish(self, k):
        self.cross(k).wait()
        for copy in self.line(k) + [self.near_copy(k), self.far_copy(k, 0)]:
            copy.wait_send()

    def stages(self):
        return [self.along_z, self.along_near, self.along_far, self.across, self.finish]


def gather_scratch(specs, depth):
    scratch = []
    for rows, columns, width, dtype in specs:
        chunks = columns // width
        scratch += [
            pltpu.VMEM((chunks, rows // 2, width), dtype),
            pltpu.SemaphoreType.DMA((chunks, depth + 3)),
            pltpu.SemaphoreType.DMA((chunks, depth + 3)),
            pltpu.SemaphoreType.DMA((chunks, 2)),
        ]
    return scratch


def gather_shape(rows, columns, depth, dtype):
    return jax.ShapeDtypeStruct((2, 2, depth, 2, rows // 2, columns), dtype)


def gather_kernel(tasks, depth, refs_of, relayed, *refs):
    count = len(tasks)
    inputs = 1 + max(i for of in refs_of for i in (sum(of, ()) if isinstance(of, tuple) else (of,)))
    srcs, refs = refs[:inputs], refs[inputs:]
    relay, refs = refs[:relayed], refs[relayed:]
    outs, relays, rest = refs[:count], refs[count : count + relayed], refs[count + relayed :]
    greet(depth)
    work = []
    for i, ((layer, width, base), of) in enumerate(zip(tasks, refs_of)):
        src = tuple([srcs[n] for n in half] for half in of) if isinstance(of, tuple) else srcs[of]
        gather = Gather(depth, layer, width, base, src, outs[i], *rest[4 * i : 4 * i + 4])
        work += [(gather, k) for k in range(gather.count)]
    for gather, k in work:
        gather.first(k)
    if relayed:
        held, sem = rest[4 * count :]
        pltpu.make_async_copy(relay[0], held, sem).start()
    pipeline(
        [lambda i, s=s: work[i][0].stages()[s](work[i][1]) for s in range(5)],
        len(work), (0, 2, 4, 6, 8),
    )
    if relayed:
        pltpu.make_async_copy(relay[0], held, sem).wait()
        last = pltpu.make_async_copy(held, relays[0], sem)
        last.start()
        last.wait()


def gather_rows(sources, refs_of, tasks, shapes, relay, collective):
    depth = lax.axis_size("seq")
    anywhere = pl.BlockSpec(memory_space=pl.ANY)
    dtype = sources[0].dtype
    relay = [] if relay is None else [relay]
    outs = pl.pallas_call(
        functools.partial(gather_kernel, tasks, depth, refs_of, len(relay)),
        in_specs=[anywhere] * (len(sources) + len(relay)),
        out_specs=[anywhere] * (len(tasks) + len(relay)),
        out_shape=[gather_shape(r, w, depth, dtype) for r, w in shapes]
        + [jax.ShapeDtypeStruct(r.shape, r.dtype) for r in relay],
        scratch_shapes=gather_scratch(
            [(r, w, t[1], dtype) for (r, w), t in zip(shapes, tasks)], depth
        )
        + sum([[pltpu.VMEM(r.shape, r.dtype), pltpu.SemaphoreType.DMA] for r in relay], []),
        compiler_params=pltpu.CompilerParams(
            collective_id=collective, has_side_effects=True, vmem_limit_bytes=VMEM_LIMIT
        ),
        name="gather_rows",
    )(*sources, *relay)
    return [flat_rows(out) for out in outs[: len(tasks)]] + list(outs[len(tasks) :])


def flat_rows(out):
    return out.reshape(-1, out.shape[-1])


class Reduce:
    def __init__(self, depth, layer, width, base, src, out, own, core, side, edge, line, done, send, recv, local):
        self.depth, self.layer, self.width, self.src, self.out = depth, layer, width, src, out
        self.base = base
        self.own, self.core, self.side, self.edge, self.line = own, core, side, edge, line
        self.done, self.send, self.recv, self.local = done, send, recv, local
        self.count, self.held = core.shape[0], own.shape[0]
        self.half = own.shape[4]
        c, y, x, z, flip_x, flip_y = where_am_i()
        self.c, self.y, self.x, self.z = c, y, x, z
        self.near = {"dp": (1 - c) * flip_x + c * flip_y}
        self.far = {"dp": (1 - c) * flip_y + c * flip_x}
        self.kept = (1 - c) * y + c * x
        self.partner = {"section": 1 - c}

    def cols(self, k, base=0):
        if isinstance(k, int):
            return pl.ds(base + k * self.width, self.width)
        return pl.ds(pl.multiple_of(base + k * self.width, LANES), self.width)

    def remote(self, k, slot, src, dst, peer):
        return pltpu.make_async_remote_copy(
            src_ref=src, dst_ref=dst, send_sem=self.send.at[k, slot], recv_sem=self.recv.at[k, slot],
            device_id=peer, device_id_type=MESH,
        )

    def pieces(self, k, half):
        if not isinstance(self.src, tuple):
            rows = pl.ds(half * self.half, self.half)
            return [(0, self.half, self.src.at[:, :, :, rows, self.cols(k)])]
        found, at = [], 0
        for ref in self.src[half]:
            found.append((at, ref.shape[3], ref))
            at += ref.shape[3]
        return found

    def hand_wait(self, k):
        return self.remote(k, 0, self.core.at[k], self.core.at[k], self.partner)

    def slot(self, k):
        return k % self.held if isinstance(k, int) else k & (self.held - 1)

    def keep_wait(self, k):
        own = self.own.at[self.slot(k)]
        return pltpu.make_async_copy(own, own, self.local.at[k, 0])

    def side_copy(self, k, core):
        at = (slice(None), 1 - self.x) if core == 0 else (1 - self.y, slice(None))
        return self.remote(k, 1, self.core.at[k, at[0], at[1]], self.side.at[k], self.near)

    def edges(self, k):
        return self.remote(k, 2, self.side.at[k, 1 - self.kept], self.edge.at[k], self.far)

    def lines(self, k):
        copies = []
        for o in range(1, self.depth):
            peer = lax.rem(self.z + o, self.depth)
            copies.append(
                self.remote(k, 2 + o, self.edge.at[k, peer], self.line.at[k, o - 1], {"seq": peer})
            )
        return copies

    def target(self):
        return pl.ds(self.c * self.half, self.half)

    def give(self, k):
        target = self.out.at[self.target(), self.cols(k, self.base)]
        return self.remote(k, 2 + self.depth, self.done.at[k], target, self.partner)

    def take(self, k):
        target = self.out.at[self.target(), self.cols(k, self.base)]
        return pltpu.make_async_copy(self.done.at[k], target, self.local.at[k, 1])

    def to_core(self, k):
        def begin(theirs, ours):
            for at, rows, ref in self.pieces(k, theirs):
                there = self.core.at[k, :, :, :, pl.ds(at, rows)]
                self.remote(k, 0, ref, there, self.partner).start()
            for at, rows, ref in self.pieces(k, ours):
                here = self.own.at[self.slot(k), :, :, :, pl.ds(at, rows)]
                pltpu.make_async_copy(ref, here, self.local.at[k, 0]).start()

        if not isinstance(self.src, tuple):
            begin(1 - self.c, self.c)
            return
        for core in (0, 1):

            @pl.when(self.c == core)
            def _(core=core):
                begin(1 - core, core)

    def to_near(self, k):
        self.hand_wait(k).wait_recv()
        self.keep_wait(k).wait()
        slot = self.slot(k)
        for at in itertools.product(range(2), range(2), range(self.depth)):
            self.core[(k,) + at] = self.core[(k,) + at] + self.own[(slot,) + at]
        for core in (0, 1):

            @pl.when(self.c == core)
            def _(core=core):
                self.side_copy(k, core).start()

    def to_far(self, k):
        self.side_copy(k, 0).wait_recv()
        c = self.c
        for u in range(2):
            a, b = (1 - c) * u + c * self.y, (1 - c) * self.x + c * u
            for e in range(self.depth):
                self.side[k, u, e] = self.side[k, u, e] + self.core[k, a, b, e]
        self.edges(k).start()

    def to_line(self, k):
        self.edges(k).wait_recv()
        for e in range(self.depth):
            self.edge[k, e] = self.edge[k, e] + self.side[k, self.kept, e]
        for copy in self.lines(k):
            copy.start()

    def to_end(self, k):
        for copy in self.lines(k):
            copy.wait_recv()
        total = self.edge[k, self.z].astype(F32)
        for o in range(self.depth - 1):
            total = total + self.line[k, o].astype(F32)
        self.done[k] = total

        @pl.when(self.c == self.layer)
        def _():
            self.take(k).start()

        @pl.when(self.c != self.layer)
        def _():
            self.give(k).start()

    def finish(self, k):
        @pl.when(self.c == self.layer)
        def _():
            self.take(k).wait()
            self.give(k).wait_recv()

        @pl.when(self.c != self.layer)
        def _():
            self.give(k).wait_send()

        for copy in [self.hand_wait(k), self.side_copy(k, 0), self.edges(k)] + self.lines(k):
            copy.wait_send()

    def stages(self):
        return [self.to_core, self.to_near, self.to_far, self.to_line, self.to_end, self.finish]


def reduce_scratch(specs, depth):
    scratch = []
    for rows, columns, width, dtype in specs:
        chunks, block = columns // width, (rows // 2, width)
        scratch += [
            pltpu.VMEM((min(chunks, 2), 2, 2, depth) + block, dtype),
            pltpu.VMEM((chunks, 2, 2, depth) + block, dtype),
            pltpu.VMEM((chunks, 2, depth) + block, dtype),
            pltpu.VMEM((chunks, depth) + block, dtype),
            pltpu.VMEM((chunks, depth - 1) + block, dtype),
            pltpu.VMEM((chunks,) + block, F32),
            pltpu.SemaphoreType.DMA((chunks, depth + 3)),
            pltpu.SemaphoreType.DMA((chunks, depth + 3)),
            pltpu.SemaphoreType.DMA((chunks, 2)),
        ]
    return scratch


def by_chip(value, depth):
    return value.reshape((2, 2, depth) + value.shape[1:])


def pieces_of(source):
    return list(source[0]) + list(source[1]) if isinstance(source, tuple) else [source]


def shard_of(source):
    first = pieces_of(source)[0]
    rows = sum(piece.shape[1] for piece in pieces_of(source))
    return (rows, first.shape[2])


def split_refs(refs, sources):
    found = []
    for numbers in sources:
        if numbers:
            one, two = numbers
            found.append((refs[:one], refs[one : one + two]))
            refs = refs[one + two :]
        else:
            found.append(refs[0])
            refs = refs[1:]
    return found, refs


def counts_of(sources):
    return [tuple(len(half) for half in s) if isinstance(s, tuple) else 0 for s in sources]


def reduce_kernel(tasks, numbers, homes, olds, depth, pairs, *refs):
    values, refs = refs[: 2 * pairs], refs[2 * pairs :]
    srcs, refs = split_refs(refs, numbers)
    refs = refs[olds:]
    placed, refs = refs[:pairs], refs[pairs:]
    outs, (loaded, ordered, load, swap_send, swap_recv, settle), rest = (
        refs[:homes], refs[homes : homes + 6], refs[homes + 6 :],
    )
    c = lax.axis_index("section")
    greet(depth)
    loads = [pltpu.make_async_copy(v, loaded.at[i], load.at[i]) for i, v in enumerate(values)]

    def local(i, src, dst):
        return pltpu.make_async_copy(src, dst, settle.at[i])

    def remote(i, src, dst):
        return pltpu.make_async_remote_copy(
            src_ref=src, dst_ref=dst, send_sem=swap_send.at[i], recv_sem=swap_recv.at[i],
            device_id={"section": 1 - c}, device_id_type=MESH,
        )

    def begin_moves(i, layer):
        for b in range(ordered.shape[1]):
            target = placed[i].at[layer, :, pl.ds(b * LANES, LANES)]
            local(i, ordered.at[2 * i + layer, b], target).start()
            remote(i, ordered.at[2 * i + 1 - layer, b], target).start()

    def end_moves(i, layer):
        local(i, ordered.at[2 * i + layer], ordered.at[2 * i + layer]).wait()
        remote(i, ordered.at[2 * i + 1 - layer], ordered.at[2 * i + 1 - layer]).wait()

    def each_pair(act):
        for layer in (0, 1):

            @pl.when(c == layer)
            def _(layer=layer):
                for i in range(pairs):
                    act(i, layer)

    def put_in_order():
        steps = loaded.shape[1] // CHUNKS
        for copy in loads:
            copy.wait()

        def step(i, _):
            for n in range(2 * pairs):
                rows = loaded[n, pl.ds(pl.multiple_of(i * CHUNKS, CHUNKS), CHUNKS), :]
                for b in range(ordered.shape[1]):
                    columns = rows[:, b * LANES : (b + 1) * LANES]
                    ordered[n, b, pl.ds(i, CHUNKS, stride=steps), :] = columns
            return 0

        lax.fori_loop(0, steps, step, 0)
        each_pair(begin_moves)

    work = []
    for i, (layer, width, home, base) in enumerate(tasks):
        item = Reduce(depth, layer, width, base, srcs[i], outs[home], *rest[9 * i : 9 * i + 9])
        work += [(item, k) for k in range(item.count)]
    for copy in loads:
        copy.start()
    pipeline(
        [lambda i, s=s: work[i][0].stages()[s](work[i][1]) for s in range(5)],
        len(work), (0, 1, 3, 5, 7), {6: put_in_order},
    )
    for item, k in work:
        item.finish(k)
    each_pair(end_moves)


def reduce_rows(values, tasks, homes, results, collective):
    depth = lax.axis_size("seq")
    pairs = len(results) // 2
    anywhere = pl.BlockSpec(memory_space=pl.ANY)
    arrays = [by_chip(piece, depth) for value in values for piece in pieces_of(value)]
    first = len(results) + len(arrays)
    olds = {i: home for i, home in enumerate(homes) if not isinstance(home, tuple)}
    count, model = results[0].shape
    blocks = (model // LANES, count, LANES)
    outs = pl.pallas_call(
        functools.partial(
            reduce_kernel, tasks, counts_of(values), len(homes), len(olds), depth, pairs
        ),
        in_specs=[anywhere] * (first + len(olds)),
        out_specs=[anywhere] * (pairs + len(homes)),
        out_shape=[jax.ShapeDtypeStruct((2, count, model), F32)] * pairs
        + [jax.ShapeDtypeStruct(home if isinstance(home, tuple) else home.shape, F32) for home in homes],
        scratch_shapes=[
            pltpu.VMEM((2 * pairs,) + results[0].shape, F32),
            pltpu.VMEM((2 * pairs,) + blocks, F32),
        ]
        + [pltpu.SemaphoreType.DMA((2 * pairs,))]
        + [pltpu.SemaphoreType.DMA((pairs,))] * 3
        + reduce_scratch([shard_of(v) + (t[1], BF16) for v, t in zip(values, tasks)], depth),
        input_output_aliases={first + n: pairs + i for n, i in enumerate(olds)},
        compiler_params=pltpu.CompilerParams(
            collective_id=collective, has_side_effects=True, vmem_limit_bytes=VMEM_LIMIT
        ),
        name="reduce_rows",
    )(*results, *arrays, *olds.values())
    return outs[:pairs], outs[pairs:]


def scan_map(phases, shift=0):
    def index(p, j, last):
        if phases == 2:
            return shift + j
        if phases == 0:
            return shift + j * (1 - p) + last * p
        return shift + j * p

    return index


def spec(rows, last, phases, width=LANES):
    index = scan_map(phases)
    return pl.BlockSpec((rows, width), lambda p, j: (0, index(p, j, last)))


def fixed(*shape):
    return pl.BlockSpec(shape, lambda p, j: (0,) * len(shape))


def timetable(now, before, rate, slots, works):
    for stage, start in enumerate(slots):
        chunk, earlier = ((now - start) * rate) >> 4, ((before - start) * rate) >> 4
        base = 0
        for count, stages in works:
            local = chunk - base

            @pl.when((chunk != earlier) & (local >= 0) & (local < count))
            def _(stages=stages, local=local, stage=stage):
                stages[stage](local)

            base += count


def wind_up(now, rate, slots, works):
    steps = [(stages, k) for count, stages in works for k in range(count)]
    while any(((now - start) * rate) >> 4 < len(steps) - 1 for start in slots):
        now += 1
        for stage, start in enumerate(slots):
            k = ((now - start) * rate) >> 4
            if k != ((now - 1 - start) * rate) >> 4 and 0 <= k < len(steps):
                steps[k][0][stage](steps[k][1])
    for count, stages in works:
        lax.fori_loop(0, count, lambda k, _, s=stages[-1]: (s(k), 0)[1], 0)


def exchange(total_ref, sum_ref, totals_ref, sums_ref, send, recv):
    count = totals_ref.shape[0]
    me = lax.axis_index("seq")
    copies = []
    for o in range(1, count):
        peer = {"seq": lax.rem(me + o, count)}
        for i, (src, dst) in enumerate(((total_ref, totals_ref), (sum_ref, sums_ref))):
            copies.append(
                pltpu.make_async_remote_copy(
                    src_ref=src, dst_ref=dst.at[me], send_sem=send.at[i, o - 1],
                    recv_sem=recv.at[i, o - 1], device_id=peer, device_id_type=MESH,
                )
            )
    for copy in copies:
        copy.start()
    for copy in copies:
        copy.wait()


def forward_scan_kernel(
    tasks, numbers, depth, lead, nstate, pack_ref, act_ref, sel_ref, cut_ref, *refs
):
    hosted = len(tasks)
    srcs, refs = split_refs(refs, numbers)
    (step_ref, sig_ref, moment_ref, full_ref, keep_ref), refs = refs[:5], refs[5:]
    gouts, refs = refs[:hosted], refs[hosted:]
    (low, inb, outb, decay, drives, enter, befores, total_ref, sum_ref, totals_ref, sums_ref, send, recv), rest = refs[:13], refs[13:]
    count = act_ref.shape[0]
    rank = low.shape[1]
    wide = sel_ref.shape[1]
    p, j = pl.program_id(0), pl.program_id(1)
    blocks = pl.num_programs(1)
    turn = p * blocks + j
    me = lax.axis_index("seq")
    lanes = pl.ds(pl.multiple_of(j * LANES, LANES), LANES)
    gathers = [
        Gather(depth, layer, width, base, srcs[i], gouts[i], *rest[4 * i : 4 * i + 4])
        for i, (layer, width, base, _) in enumerate(tasks)
    ]

    @pl.when(turn == 0)
    def _():
        hail(depth)
        low[...] = sel_ref[:, :rank].astype(BF16)
        spread(inb, sel_ref, nstate, rank)
        spread(outb, sel_ref, nstate, rank + nstate)

    @pl.when(turn == 1)
    def _():
        await_hails(depth)
        for gather in gathers:
            lax.fori_loop(0, gather.count, lambda k, _, g=gather: (g.first(k), 0)[1], 0)

    works = [(gather.count, gather.stages()) for gather in gathers]
    pace, slots = 15, (2, 5, 9, 13)
    timetable(turn, turn - 1, pace, slots, works)

    @pl.when(p == 0)
    def _():
        stepw = pack_ref[0, wide : wide + rank, :]
        pre = jnp.dot(low[...], stepw, preferred_element_type=F32) + vector_of(pack_ref, 5)
        near = jnp.exp(-jnp.abs(pre))
        step_all = jnp.maximum(pre, 0.0) + jnp.log1p(near)
        step_ref[...] = step_all
        sig_ref[...] = jnp.where(pre >= 0.0, 1.0, near) / (1.0 + near)
        moment_ref[0:1, :] = jnp.sum(step_all, axis=0, keepdims=True)
        moment_ref[1:2, :] = jnp.sum(step_all * step_all, axis=0, keepdims=True)
        rate = rates_of(pack_ref, nstate)
        rates = rate_rows(rate, nstate)

        def body(pair, carry):
            states, sums = carry
            act = act_ref[pl.ds(pl.multiple_of(pair * 16, 16), 16), :].astype(F32)
            for half in (0, 1):
                at = pl.ds(pl.multiple_of(pair * 16 + half * 8, 8), 8)
                step = step_ref[at, :]
                away = step + cut_ref[at, :]
                drive = step * act[half * 8 : half * 8 + 8]
                drives[j, at, :] = drive
                sums = sums + away
                new = []
                for n in range(nstate):
                    gain = jnp.exp2(away * rates[n])
                    decay[j, n, at, :] = gain
                    new.append(gain * states[n] + drive * inb[n, at, :])
                states = tuple(new)
            return states, sums

        zero = jnp.zeros((CHUNKS, LANES), F32)
        ends, sums = lax.fori_loop(0, count // 16, body, ((zero,) * nstate, zero), unroll=2)
        entering, totals, before, total = chunk_links(ends, sums, rates, False)
        for n in range(nstate):
            enter[j, n] = entering[n]
        total_ref[:, lanes] = jnp.concatenate(totals, axis=0).astype(total_ref.dtype)
        befores[j] = before
        sum_ref[:, lanes] = total

    @pl.when(turn == blocks)
    def _():
        exchange(total_ref, sum_ref, totals_ref, sums_ref, send, recv)

    @pl.when(p == 1)
    def _():
        rate = rates_of(pack_ref, nstate)
        rates = rate_rows(rate, nstate)
        arrived = arriving_state(me, totals_ref, sums_ref, lanes, rate, False)
        before = befores[j]
        states = tuple(
            enter[j, n] + jnp.exp2(before * rates[n]) * arrived[n : n + 1, :] for n in range(nstate)
        )
        skip = jnp.broadcast_to(vector_of(pack_ref, 6), (CHUNKS, LANES))

        def body(pair, states):
            rows = pl.ds(pl.multiple_of(pair * 16, 16), 16)
            act = act_ref[rows, :].astype(F32)
            held = []
            for half in (0, 1):
                at = pl.ds(pl.multiple_of(pair * 16 + half * 8, 8), 8)
                held.append(states)
                drive = drives[j, at, :]
                out = skip * act[half * 8 : half * 8 + 8]
                new = []
                for n in range(nstate):
                    state = decay[j, n, at, :] * states[n] + drive * inb[n, at, :]
                    out = out + state * outb[n, at, :]
                    new.append(state)
                states = tuple(new)
                full_ref[at, :] = out
            for n in range(nstate):
                both = jnp.concatenate([held[0][n], held[1][n]], axis=0)
                keep_ref[0, n, rows, :] = both.astype(keep_ref.dtype)
            return states

        ends = lax.fori_loop(0, count // 16, body, states, unroll=2)
        for n in range(nstate):
            both = jnp.concatenate([ends[n], ends[n]], axis=0)
            keep_ref[0, n, count : count + 16, :] = both.astype(keep_ref.dtype)

    @pl.when(turn == 2 * lead - 1)
    def _():
        wind_up(2 * lead - 1, pace, slots, works)


def forward_scan(pack, nstate, act, selected, cut, sources, tasks, collective):
    count, inner = act.shape
    rank = selected.shape[1] - 2 * nstate
    depth = lax.axis_size("seq")
    blocks = inner // LANES
    last = blocks - 1
    arrays = [piece for source in sources for piece in pieces_of(source)]
    lengths = [sum(piece.shape[0] for piece in pieces_of(source)) for source in sources]
    anywhere = pl.BlockSpec(memory_space=pl.ANY)
    outs = pl.pallas_call(
        functools.partial(forward_scan_kernel, tasks, counts_of(sources), depth, blocks, nstate),
        grid=(2, blocks),
        in_specs=[
            pl.BlockSpec((1,) + pack.shape[1:], lambda p, j: (j, 0, 0)),
            spec(count, last, 2),
            fixed(*selected.shape),
            fixed(count, LANES),
        ]
        + [anywhere] * len(arrays),
        out_specs=[
            spec(count, last, 0),
            spec(count, last, 0),
            spec(2, last, 0),
            spec(count, last, 1),
            pl.BlockSpec((1, nstate, count + 16, LANES), lambda p, j: (j * p, 0, 0, 0)),
        ]
        + [anywhere] * len(tasks),
        out_shape=[
            jax.ShapeDtypeStruct((count, inner), F32),
            jax.ShapeDtypeStruct((count, inner), F32),
            jax.ShapeDtypeStruct((2, inner), F32),
            jax.ShapeDtypeStruct((count, inner), F32),
            jax.ShapeDtypeStruct((blocks, nstate, count + 16, LANES), BF16),
        ]
        + [gather_shape(r, t[3], depth, BF16) for r, t in zip(lengths, tasks)],
        scratch_shapes=[
            pltpu.VMEM((count, rank), BF16),
            pltpu.VMEM((nstate, count, LANES), F32),
            pltpu.VMEM((nstate, count, LANES), F32),
            pltpu.VMEM((blocks, nstate, count, LANES), F32),
            pltpu.VMEM((blocks, count, LANES), F32),
            pltpu.VMEM((blocks, nstate, CHUNKS, LANES), F32),
            pltpu.VMEM((blocks, CHUNKS, LANES), F32),
            pltpu.VMEM((nstate, inner), BF16),
            pltpu.VMEM((1, inner), F32),
            pltpu.VMEM((depth, nstate, inner), BF16),
            pltpu.VMEM((depth, 1, inner), F32),
            pltpu.SemaphoreType.DMA((2, depth - 1)),
            pltpu.SemaphoreType.DMA((2, depth - 1)),
        ]
        + gather_scratch([(r, t[3], t[1], BF16) for r, t in zip(lengths, tasks)], depth),
        compiler_params=pltpu.CompilerParams(
            dimension_semantics=("arbitrary", "arbitrary"), collective_id=collective,
            has_side_effects=True, vmem_limit_bytes=VMEM_LIMIT,
        ),
        name="forward_scan",
    )(pack, act, selected, cut, *arrays)
    return outs[:5], [flat_rows(out) for out in outs[5:]]


def backward_scan_kernel(
    tasks, numbers, homes, olds, depth, lead, nstate, dfull_ref, step_ref, cut_ref, pack_ref, sel_ref, act_ref, sig_ref,
    keep_ref, *refs
):
    srcs, refs = split_refs(refs, numbers)
    refs = refs[olds:]
    (dact_ref, gbias_ref, gskip_ref, gdecay_ref, gstepw_ref, dsel_ref), refs = refs[:6], refs[6:]
    gouts, refs = refs[:homes], refs[homes:]
    (
        low, inb, outb, decay, enter, befores, total_ref, sum_ref, totals_ref, sums_ref,
        din_acc, dout_acc, decay_acc, dlow_acc, dstep_buf, send, recv,
    ), rest = refs[:17], refs[17:]
    count = act_ref.shape[0]
    rank = low.shape[1]
    wide = sel_ref.shape[1]
    pairs = count // 16
    p, j = pl.program_id(0), pl.program_id(1)
    blocks = pl.num_programs(1)
    turn = p * blocks + j
    me = lax.axis_index("seq")
    lanes = pl.ds(pl.multiple_of(j * LANES, LANES), LANES)
    items = [
        Reduce(depth, layer, width, base, srcs[i], gouts[home], *rest[9 * i : 9 * i + 9])
        for i, (layer, width, home, base) in enumerate(tasks)
    ]

    @pl.when(turn == 0)
    def _():
        hail(depth)
        low[...] = sel_ref[:, :rank].astype(BF16)
        spread(inb, sel_ref, nstate, rank)
        spread(outb, sel_ref, nstate, rank + nstate)
        din_acc[...] = jnp.zeros_like(din_acc)
        dout_acc[...] = jnp.zeros_like(dout_acc)
        dlow_acc[...] = jnp.zeros_like(dlow_acc)

    @pl.when(turn == 1)
    def _():
        await_hails(depth)

    works = [(item.count, item.stages()) for item in items]
    pace, slots = 6 if len(works) > 2 else 4, (2, 4, 9, 14, 18)
    timetable(turn + p * j, turn - 1 + p * jnp.maximum(j - 1, 0), pace, slots, works)

    @pl.when(p == 0)
    def _():
        rate = rates_of(pack_ref, nstate)
        rates = rate_rows(rate, nstate)

        def body(step_back, carry):
            states, sums = carry
            pair = pairs - 1 - step_back
            for half in (1, 0):
                at = pl.ds(pl.multiple_of(pair * 16 + half * 8, 8), 8)
                away = step_ref[at, :] + cut_ref[at, :]
                grad = dfull_ref[at, :]
                sums = sums + away
                new = []
                for n in range(nstate):
                    gain = jnp.exp2(away * rates[n])
                    decay[j, n, at, :] = gain
                    new.append(gain * (states[n] + outb[n, at, :] * grad))
                states = tuple(new)
            return states, sums

        zero = jnp.zeros((CHUNKS, LANES), F32)
        ends, sums = lax.fori_loop(0, pairs, body, ((zero,) * nstate, zero), unroll=2)
        entering, totals, before, total = chunk_links(ends, sums, rates, True)
        for n in range(nstate):
            enter[j, n] = entering[n]
        total_ref[:, lanes] = jnp.concatenate(totals, axis=0).astype(total_ref.dtype)
        befores[j] = before
        sum_ref[:, lanes] = total

    @pl.when(turn == blocks)
    def _():
        exchange(total_ref, sum_ref, totals_ref, sums_ref, send, recv)

    @pl.when(p == 1)
    def _():
        rate = rates_of(pack_ref, nstate)
        rates = rate_rows(rate, nstate)
        arrived = arriving_state(me, totals_ref, sums_ref, lanes, rate, True)
        before = befores[j]
        states = tuple(
            enter[j, n] + jnp.exp2(before * rates[n]) * arrived[n : n + 1, :] for n in range(nstate)
        )
        skip = jnp.broadcast_to(vector_of(pack_ref, 6), (CHUNKS, LANES))
        for n in range(nstate):
            decay_acc[n] = jnp.zeros((CHUNKS, LANES), F32)
            last = keep_ref[0, n, count : count + 16, :].astype(F32)[0:CHUNKS]
            dout_acc[n, pl.ds(count, CHUNKS), :] += last * dfull_ref[pl.ds(count - CHUNKS, CHUNKS), :]

        def body(step_back, carry):
            states, gskip = carry
            pair = pairs - 1 - step_back
            rows = pl.ds(pl.multiple_of(pair * 16, 16), 16)
            act = act_ref[rows, :].astype(F32)
            held = [keep_ref[0, n, rows, :].astype(F32) for n in range(nstate)]
            sums = [None] * nstate
            for half in (1, 0):
                at = pl.ds(pl.multiple_of(pair * 16 + half * 8, 8), 8)
                step = step_ref[at, :]
                act_now = act[half * 8 : half * 8 + 8]
                drive = step * act_now
                grad = dfull_ref[at, :]
                gskip = gskip + grad * act_now
                if half:
                    earlier = dfull_ref[pl.ds(pl.multiple_of(pair * 16, 8), 8), :]
                else:
                    earlier = dfull_ref[pl.ds(pl.multiple_of(jnp.maximum(pair * 16 - 8, 0), 8), 8), :]
                by_rate = jnp.zeros((CHUNKS, LANES), F32)
                mapped = jnp.zeros((CHUNKS, LANES), F32)
                new = []
                for n in range(nstate):
                    prior = held[n][half * 8 : half * 8 + 8]
                    adjoint = states[n] + outb[n, at, :] * grad
                    passed = adjoint * decay[j, n, at, :]
                    rho = passed * prior
                    by_rate = by_rate + rho * rates[n]
                    mapped = mapped + adjoint * inb[n, at, :]
                    sums[n] = rho * step if half else sums[n] + rho * step
                    din_acc[n, at, :] += adjoint * drive
                    dout_acc[n, at, :] += prior * earlier
                    new.append(passed)
                states = tuple(new)
                dstep_buf[at, :] = by_rate * LN2 + act_now * mapped
                dact_ref[at, :] = step * mapped + skip * grad
            for n in range(nstate):
                decay_acc[n] += sums[n]
            return states, gskip

        _, gskip = lax.fori_loop(0, pairs, body, (states, jnp.zeros((CHUNKS, LANES), F32)), unroll=2)
        gskip_ref[...] = jnp.sum(gskip, axis=0, keepdims=True)
        decays = [jnp.sum(decay_acc[n], axis=0, keepdims=True) for n in range(nstate)]
        gdecay = (rate * LN2) * jnp.concatenate(decays, axis=0)
        gdecay_ref[0] = gdecay.astype(gdecay_ref.dtype)
        dpre = dstep_buf[...] * sig_ref[...]
        gbias_ref[...] = jnp.sum(dpre, axis=0, keepdims=True)
        low_dpre = dpre.astype(BF16)
        gstepw_ref[0] = lax.dot_general(
            low[...], low_dpre, (((0,), (0,)), ((), ())), preferred_element_type=F32
        ).astype(gstepw_ref.dtype)
        dlow_acc[...] += lax.dot_general(
            low_dpre, pack_ref[0, wide : wide + rank, :], (((1,), (1,)), ((), ())),
            preferred_element_type=F32,
        )

    @pl.when(turn == 2 * lead - 1)
    def _():
        column = lax.broadcasted_iota(jnp.int32, (LANES, nstate), 1)
        din = jnp.zeros((count, nstate), F32)
        dout = jnp.zeros((count, nstate), F32)
        for n in range(nstate):
            pick = (column == n).astype(BF16)
            din = din + jnp.dot(din_acc[n].astype(BF16), pick, preferred_element_type=F32)
            part = dout_acc[n, CHUNKS : count + CHUNKS, :].astype(BF16)
            dout = dout + jnp.dot(part, pick, preferred_element_type=F32)
        dsel_ref[...] = jnp.concatenate([dlow_acc[...], din, dout], axis=1).astype(BF16)

    @pl.when(turn == 2 * lead - 1)
    def _():
        wind_up(3 * lead - 2, pace, slots, works)


def backward_scan(
    dfull, step, cut, pack, nstate, selected, act, sig, keep, sources, tasks, homes, collective
):
    count, inner = act.shape
    rank = selected.shape[1] - 2 * nstate
    depth = lax.axis_size("seq")
    blocks = inner // LANES
    last = blocks - 1
    arrays = [by_chip(piece, depth) for source in sources for piece in pieces_of(source)]
    olds = {i: home for i, home in enumerate(homes) if not isinstance(home, tuple)}
    shapes = [home if isinstance(home, tuple) else home.shape for home in homes]
    anywhere = pl.BlockSpec(memory_space=pl.ANY)
    outs = pl.pallas_call(
        functools.partial(
            backward_scan_kernel, tasks, counts_of(sources), len(homes), len(olds), depth, blocks, nstate
        ),
        grid=(2, blocks),
        in_specs=[
            spec(count, last, 2),
            spec(count, last, 2),
            fixed(count, LANES),
            pl.BlockSpec((1,) + pack.shape[1:], lambda p, j: (j, 0, 0)),
            fixed(*selected.shape),
            spec(count, last, 1),
            spec(count, last, 1),
            pl.BlockSpec((1, nstate, count + 16, LANES), lambda p, j: (j * p, 0, 0, 0)),
        ]
        + [anywhere] * (len(arrays) + len(olds)),
        out_specs=[
            spec(count, last, 1),
            spec(1, last, 1),
            spec(1, last, 1),
            pl.BlockSpec((1, nstate, LANES), lambda p, j: (j * p, 0, 0)),
            pl.BlockSpec((1, rank, LANES), lambda p, j: (j * p, 0, 0)),
            fixed(*selected.shape),
        ]
        + [anywhere] * len(homes),
        out_shape=[
            jax.ShapeDtypeStruct((count, inner), F32),
            jax.ShapeDtypeStruct((1, inner), F32),
            jax.ShapeDtypeStruct((1, inner), F32),
            jax.ShapeDtypeStruct((blocks, nstate, LANES), BF16),
            jax.ShapeDtypeStruct((blocks, rank, LANES), BF16),
            jax.ShapeDtypeStruct(selected.shape, BF16),
        ]
        + [jax.ShapeDtypeStruct(shape, F32) for shape in shapes],
        scratch_shapes=[
            pltpu.VMEM((count, rank), BF16),
            pltpu.VMEM((nstate, count, LANES), F32),
            pltpu.VMEM((nstate, count, LANES), F32),
            pltpu.VMEM((blocks, nstate, count, LANES), F32),
            pltpu.VMEM((blocks, nstate, CHUNKS, LANES), F32),
            pltpu.VMEM((blocks, CHUNKS, LANES), F32),
            pltpu.VMEM((nstate, inner), BF16),
            pltpu.VMEM((1, inner), F32),
            pltpu.VMEM((depth, nstate, inner), BF16),
            pltpu.VMEM((depth, 1, inner), F32),
            pltpu.VMEM((nstate, count, LANES), F32),
            pltpu.VMEM((nstate, count + CHUNKS, LANES), F32),
            pltpu.VMEM((nstate, CHUNKS, LANES), F32),
            pltpu.VMEM((count, rank), F32),
            pltpu.VMEM((count, LANES), F32),
            pltpu.SemaphoreType.DMA((2, depth - 1)),
            pltpu.SemaphoreType.DMA((2, depth - 1)),
        ]
        + reduce_scratch([shard_of(s) + (t[1], BF16) for s, t in zip(sources, tasks)], depth),
        input_output_aliases={8 + len(arrays) + n: 6 + i for n, i in enumerate(olds)},
        compiler_params=pltpu.CompilerParams(
            dimension_semantics=("arbitrary", "arbitrary"), collective_id=collective,
            has_side_effects=True, vmem_limit_bytes=VMEM_LIMIT,
        ),
        name="backward_scan",
    )(dfull, step, cut, pack, selected, act, sig, keep, *arrays, *olds.values())
    return outs[:6], outs[6:]


def places(lengths, count, reach):
    steps = count // CHUNKS
    base = lax.axis_index("seq") * count
    starts = jnp.cumsum(lengths) - lengths
    here = (
        base + jnp.arange(steps, dtype=jnp.int32)[:, None]
        + steps * jnp.arange(CHUNKS, dtype=jnp.int32)[None, :]
    )

    def segment(at):
        return jnp.sum((starts[:, None, None] <= at[None]).astype(jnp.int32), axis=0) - 1

    own = segment(here)
    same = jnp.stack(
        [(segment(here - reach + k) == own).astype(F32).reshape(count) for k in range(reach)]
    )
    same = jnp.broadcast_to(same[:, :, None], same.shape + (LANES,))
    opens = jnp.any(starts[:, None, None] == here[None], axis=0)
    cut = jnp.where(opens, CUT, 0.0).astype(F32).reshape(count, 1)
    return same, jnp.broadcast_to(cut, (count, LANES))


def layer_forward(xin, in_conv, other, same, cut, host, collective):
    pack, gain, wide, nstate = other
    count = xin.shape[0]
    inner = in_conv.shape[1]
    reach = same.shape[0]
    scale = lax.rsqrt(jnp.mean(xin * xin, axis=-1, keepdims=True) + EPS)
    normed = (xin * scale * gain).astype(BF16)
    conv_in = jnp.dot(normed, in_conv, preferred_element_type=F32).astype(BF16)
    last = conv_in[(count - reach * CHUNKS) :].reshape(reach, CHUNKS, inner)[:, CHUNKS - 1]
    halo = shifted(last, "seq", 1)
    act, selected = select_call(conv_in, halo, same, pack, wide)
    (step, sig, moments, full, keep), got = forward_scan(
        pack, nstate, act, selected, cut, host[0], host[1], collective
    )
    return (scale, normed, conv_in, halo, act, selected, step, sig, full, keep), moments, got


def layer_output(xin, normed, full, in_gate, out_weight):
    gate = jnp.dot(normed, in_gate, preferred_element_type=F32).astype(BF16)
    wide = gate.astype(F32)
    gated = (full * (wide * jax.nn.sigmoid(wide))).astype(BF16)
    return xin + jnp.dot(gated, out_weight, preferred_element_type=F32), gate, gated


def outer_sum(left, right):
    return lax.dot_general(left, right, (((0,), (0,)), ((), ())), preferred_element_type=F32)


def times_transposed(left, right):
    return lax.dot_general(left, right, (((1,), (1,)), ((), ())), preferred_element_type=F32)


def layer_backward(grad_out, weights, same, cut, saved, moments, host, collective):
    in_conv, in_gate, out_weight, pack, gain, _, nstate = weights
    (xin, scale, normed, conv_in, halo, act, selected, step, sig, full, keep, gate, gated) = saved
    count, inner = act.shape
    reach = same.shape[0]
    grad_low = grad_out.astype(BF16)
    dgated = times_transposed(grad_low, out_weight)
    gout = outer_sum(gated, grad_low).astype(BF16)
    wide = gate.astype(F32)
    dfull = dgated * (wide * jax.nn.sigmoid(wide))
    dgate = (dgated * full * silu_slope(wide)).astype(BF16)
    gin_gate = outer_sum(normed, dgate).astype(BF16)
    sources, tasks, homes = host(gout, gin_gate)
    (dact, gbias, gskip, gdecay, gstepw, dsel), found = backward_scan(
        dfull, step, cut, pack, nstate, selected, act, sig, keep, sources, tasks, homes, collective
    )
    dconv, tail, spill, gsel, gsmall = conv_grad(
        conv_in, halo, same, pack, act, dact, dsel, gbias, gskip
    )
    late = (tail + shifted(spill, "seq", -1)).astype(BF16)
    grid = dconv.reshape(count // CHUNKS, CHUNKS, inner)
    dconv = grid.at[count // CHUNKS - reach :, CHUNKS - 1].set(late).reshape(count, inner)
    gin_conv = outer_sum(normed, dconv).astype(BF16)
    dnormed = times_transposed(dconv, in_conv) + times_transposed(dgate, in_gate)
    unit = xin * scale
    ggain = jnp.sum(dnormed * unit, axis=0)
    dunit = dnormed * gain
    grad_in = scale * (dunit - unit * jnp.mean(dunit * unit, axis=-1, keepdims=True)) + grad_out
    shards = lax.axis_size(("dp", "seq"))
    per = inner // shards
    if per < LANES:
        blocked = lambda rows: rows.swapaxes(0, 1).reshape(rows.shape[1], shards, per).swapaxes(0, 1)
        gsel, gstepw, gdecay, gsmall = (blocked(rows) for rows in (gsel, gstepw, gdecay, gsmall))
    ggain = jnp.pad(ggain.reshape(shards, 1, -1), ((0, 0), (0, 0), (0, per - ggain.shape[0] // shards)))
    moments = moments.reshape(2, shards, per).swapaxes(0, 1)
    rest = jnp.concatenate([ggain, moments, jnp.zeros((shards, 5, per), F32)], axis=1)
    rest = jnp.concatenate([gsmall, rest], axis=1).astype(BF16)
    rows = ([gsel], [gstepw, gdecay, rest])
    return grad_in, gin_conv, gin_gate, gout, rows, found


AXES = ("section", "dp", "seq")


def body(
    inputs, doc_lengths, out_grad, norm_gain, in_weight, conv_weight, conv_bias, select_weight,
    step_weight, step_bias, log_decay, skip_gain, out_weight,
):
    section = lax.axis_index("section")
    micro, _, count, model = inputs.shape
    taps, per = conv_weight.shape[1:]
    shards = lax.axis_size(("dp", "seq"))
    inner = per * shards
    rank, nstate = step_weight.shape[1], log_decay.shape[1]
    wide = rank + 2 * nstate

    kernels = lax.axis_size("dp") == 4 and per % LANES == 0 and in_weight.shape[1] % 32 == 0
    pad = per - norm_gain.shape[1]
    vectors = [conv_weight[0], conv_bias, step_bias, skip_gain, jnp.pad(norm_gain, ((0, 0), (0, pad)))]
    vectors = [v.astype(F32) for v in vectors] + [jnp.zeros((16 - taps - 4, per), F32)]
    vectors = jnp.concatenate(vectors, axis=0).astype(BF16)
    pieces = [select_weight[0].T, step_weight[0], log_decay[0], vectors]
    in_half, out_half = in_weight[0], out_weight[0]
    if kernels:
        length = sum(piece.shape[0] for piece in pieces)
        quarter = in_half.shape[:1] + (inner,)
        packs = gather_rows(
            pieces + [in_half], [((0,), (1, 2, 3)), 4, 4],
            [(0, per, 0), (0, 256, 0), (0, 256, inner)],
            [(length, per), quarter, quarter], None, 2,
        )
        packed = [packs[0].reshape(shards, -1, per), None]
        in_conv, in_gate = [packs[1], None], [packs[2], None]
        outs_weight = [None, None]
        hosts = [
            (
                [([pieces[0]], pieces[1:]), in_half, out_half],
                [(1, per, 0, per), (1, 256, 0, inner), (0, 128, 0, model)],
            ),
            ([in_half, out_half], [(1, 256, inner, inner), (1, 128, 0, model)]),
        ]
    else:
        packed = lax.all_gather(jnp.concatenate(pieces, axis=0), AXES, axis=0).reshape(2, shards, -1, per)
        in_all = lax.all_gather(in_half, AXES, axis=0, tiled=True).reshape(2, model, -1)
        in_conv, in_gate = in_all[:, :, :inner], in_all[:, :, inner:]
        outs_weight = lax.all_gather(out_half, AXES, axis=0, tiled=True).reshape(2, inner, model)
        hosts = [([], []), ([], [])]
    def other(layer):
        pack = packed[layer]
        gain = pack[:, wide + rank + nstate + taps + 3, : norm_gain.shape[1]].reshape(-1).astype(F32)
        if per < LANES:
            flat = pack.swapaxes(0, 1).reshape(-1, inner)
            pack = flat.reshape(-1, inner // LANES, LANES).swapaxes(0, 1)
        return pack, gain, wide, nstate

    mine = lambda value: lax.dynamic_index_in_dim(value, section, 0, keepdims=False)[0]
    same, cut = places(mine(doc_lengths), count, taps - 1)
    state = interleave(mine(inputs).astype(F32))
    outs, kept, weights = [], [], []
    for layer in range(2):
        saved, moments, got = layer_forward(
            state, in_conv[layer], other(layer), same, cut, hosts[layer], 5 + layer
        )
        if kernels:
            if layer == 0:
                packed[1] = got.pop(0).reshape(shards, -1, per)
            (in_gate if layer else in_conv)[1], outs_weight[layer] = got
        result, gate, gated = layer_output(
            state, saved[1], saved[8], in_gate[layer], outs_weight[layer]
        )
        weights.append((in_conv[layer], in_gate[layer], outs_weight[layer]) + other(layer))
        kept.append(((state,) + saved + (gate, gated), moments))
        state = result
        outs.append(state)
    grad = interleave(mine(out_grad).astype(F32))
    def split(value):
        return value.reshape(shards, -1, value.shape[1])

    grads = [None] * 2
    parts = [None] * 2
    found = []
    for layer in (1, 0):
        if not kernels:
            host = lambda gout, gin_gate: ([], [], [])
        elif layer == 1:
            host = lambda gout, gin_gate: (
                [split(gout), split(gin_gate)], [(1, 256, 0, 0), (1, 512, 1, inner)],
                [(per, model), (in_half.shape[0], 2 * inner)],
            )
        else:
            host = lambda gout, gin_gate: (
                [split(gout), parts[1][1], parts[1][0], split(gin_gate)],
                [(0, 256, 0, 0), (1, 512, 1, 0), (1, per, 2, 0), (0, 512, 1, inner)],
                list(found) + [(length, per)],
            )
        grad, gin_conv, gin_gate, gout, pack, found = layer_backward(
            grad, weights[layer], same, cut, *kept[layer], host, 7 + layer
        )
        grads[layer] = grad
        parts[layer] = [pack, split(gin_conv), split(gin_gate), split(gout)]

    if kernels:
        results, (gin, rows) = reduce_rows(
            [parts[0][1], parts[0][0]], [(0, 256, 0, 0), (0, per, 1, 0)], [found[1], (length, per)],
            outs + grads, 3,
        )
        rows = jnp.where(section == 0, rows, found[2])
        gout = found[0]
    else:
        found = []
        for side in parts:
            side[0] = jnp.concatenate(pieces_of(side[0]), axis=1)
        for pair in zip(*parts):
            both = jnp.stack(pair).reshape((-1,) + pair[0].shape[1:])
            found.append(lax.psum_scatter(both, AXES, scatter_dimension=0).astype(F32))
        rows, gin_conv, gin_gate, gout = found
        gin = jnp.concatenate([gin_conv, gin_gate], axis=1)

    def place(values):
        first, second = (in_order(value) for value in values)
        own = jnp.where(section == 0, first, second)
        other = jnp.where(section == 0, second, first)
        other = lax.ppermute(other, "section", [(0, 1), (1, 0)])
        both = jnp.stack([jnp.where(section == 0, own, other), jnp.where(section == 0, other, own)])
        return both

    both = (1, micro, 1, count, model)
    at = wide + rank + nstate
    tokens = micro * inputs.shape[1] * lax.axis_size("dp") * count * lax.axis_size("seq")
    if not kernels:
        results = place(outs), place(grads)
    return (
        results[0].reshape(both),
        results[1].reshape(both),
        rows[at + 8, : norm_gain.shape[1]][None],
        gin[None],
        rows[at : at + taps][None],
        rows[at + taps][None],
        rows[:wide].T[None],
        rows[wide : wide + rank][None],
        rows[at + taps + 1][None],
        rows[wide + rank : at][None],
        rows[at + taps + 2][None],
        gout[None],
        (rows[at + 9 : at + 11] / tokens)[None],
    )


def solution(mesh):
    vector = P("section", ("dp", "seq"))
    matrix = P("section", ("dp", "seq"), None)
    turned = P("section", None, ("dp", "seq"))
    tokens = P(None, "dp", "seq", None)
    in_specs = (
        tokens, P(None, "dp", None), tokens, vector, matrix, turned, vector, matrix, turned,
        vector, turned, vector, matrix,
    )
    result = P("section", None, "dp", "seq", None)
    out_specs = (
        result, result, vector, matrix, turned, vector, matrix, turned, vector, turned, vector,
        matrix, turned,
    )
    return jax.shard_map(body, mesh=mesh, in_specs=in_specs, out_specs=out_specs, check_vma=False)
```
